256 devices in a mesh: grp: 4 (over z_hi), vocab: 8 (over z_lo, x), rows: 8 (over y, core).
Axes of the slice: x: 4, y: 4, z: 8 (z_hi: 4, z_lo: 2; z = z_hi * 2 + z_lo), core: 2. Of those that a mesh axis runs over, the one named last changes fastest.
Arguments:
- mentor_final_hiddens: bfloat16 [5632, 4096], P(('rows', 'grp')), may hold values from -600 to 600
- mentor_readout_matrix: bfloat16 [4096, 32128], P('rows', ('grp', 'vocab')), may hold values from -0.09375 to 0.09375
- learner_final_hiddens: bfloat16 [5632, 2048], P('rows'), may hold values from -600 to 600
- learner_readout_matrix: bfloat16 [2048, 32128], P('rows', ('grp', 'vocab')), may hold values from -0.125 to 0.125
- label_tokens_ids: int32 [5632], P('rows'), may hold values from 0 to 32127
- corruption_kinds: int32 [5632], P('rows'), may hold values from 0 to 2
- heat_per_kind: float32 [3], replicated, may hold values from 1 to 4
Outputs:
- divergence: float32 [5632], P('rows')
- hidden_grad: float32 [5632, 2048], P('rows', ('grp', 'vocab'))
- weight_grad: float32 [2048, 32128], P('rows', ('grp', 'vocab'))
The draws below stay inside these ranges and needn't reach their ends.
All inputs are finite; a program needn't handle non-finite values.
Results may differ from the reference program's by a relative error of at most 0.0026.
Values may be sent and summed in bfloat16 or wider, within the bound.
A program may use at most 128 MiB of HBM per device.

```python
import math
import jax
import jax.numpy as jnp
import numpy as np
from jax import lax

DT = 4096
DS = 2048
V = 32128
ROW_DEV = 704
ROWS = 5632
CORRUPTION_AIMS = 3
N_ROWS = 8


def scaled_states(key, width):
    base = 3.0 * jax.random.normal(key, (ROWS, width), jnp.float32)
    return jnp.clip(base, -18.0, 18.0)


def draw_mentor_final_hiddens(key, part):
    return scaled_states(jax.random.fold_in(key, 11), DT).astype(jnp.bfloat16)


def draw_learner_final_hiddens(key, part):
    return scaled_states(jax.random.fold_in(key, 23), DS).astype(jnp.bfloat16)


def set_ends(entries, rng, least, largest):
    longest = entries.shape.index(max(entries.shape))
    spots = []
    for shift in (0, 1):
        where = [jax.random.randint(jax.random.fold_in(rng, axis), (), 0, length) for axis, length in enumerate(entries.shape)]
        where[longest] = (where[longest] + shift) % entries.shape[longest]
        spots.append(tuple(where))
    return entries.at[spots[0]].set(least).at[spots[1]].set(largest)


def block_levels(key, dims, shards, low, top_value):
    level = 1.0
    for axis_at, parts in shards:
        steps = jax.random.uniform(jax.random.fold_in(jax.random.fold_in(key, 6), axis_at), (parts,), jnp.float32, low / len(shards), top_value / len(shards))
        level = level * jnp.repeat(jnp.exp(steps), dims[axis_at] // parts).reshape((-1,) + (1,) * (len(dims) - 1 - axis_at))
    return level


def rank_table(count, skew):
    loads = [(1 << 20) // math.isqrt(rank ** skew) + 1 for rank in range(1, count + 1)]
    scale = 1 + sum(loads) // (1 << 30)
    return np.cumsum(np.array([max(1, weight // scale) for weight in loads]))


def skewed_ids(key, dims, count, skew):
    grid = rank_table(count, skew)
    lot = jax.random.randint(jax.random.fold_in(key, 1), dims, 0, int(grid[count - 1]))
    standing = jnp.searchsorted(jnp.asarray(grid, jnp.int32), lot, side="right")
    return jax.random.permutation(jax.random.fold_in(key, 2), count)[standing].astype(jnp.int32)


def noise(stream_key, shape, scale, limit, cuts=(), kind=jnp.bfloat16):
    array = jax.random.normal(stream_key, shape, jnp.float32) * scale
    if len(cuts) > 0:
        array = block_levels(stream_key, shape, cuts, -0.22, 0.18) * array
    return jnp.clip(array, min=-limit, max=limit).astype(kind)


def setup_inputs(seed: int = 0) -> dict:
    streams_of = jax.random.split(jax.random.key(seed), 8)
    mentor_final_hiddens = draw_mentor_final_hiddens(jax.random.fold_in(streams_of[7], 71), 0)
    mentor_readout_matrix = noise(streams_of[1], (DT, V), DT ** -0.5, 0.09375, ((0, 8), (1, 32)))
    learner_final_hiddens = draw_learner_final_hiddens(jax.random.fold_in(streams_of[7], 71), 0)
    learner_readout_matrix = noise(streams_of[3], (DS, V), DS ** -0.5, 0.125, ((0, 8), (1, 32)))
    label_tokens_ids = set_ends(skewed_ids(streams_of[4], (ROWS,), V, 2), jax.random.fold_in(streams_of[4], 3), 0, V - 1).astype(jnp.int32)
    corruption_kinds = set_ends(jax.random.randint(streams_of[5], (ROWS,), 0, CORRUPTION_AIMS), jax.random.fold_in(streams_of[5], 1), 0, CORRUPTION_AIMS - 1).astype(jnp.int32)
    heat_per_kind = jnp.clip(jnp.exp(jax.random.uniform(streams_of[6], (CORRUPTION_AIMS,), jnp.float32, math.log(1.0), math.log(4.0))), 1.0, 4.0)
    return dict(mentor_final_hiddens=mentor_final_hiddens, mentor_readout_matrix=mentor_readout_matrix, learner_final_hiddens=learner_final_hiddens, learner_readout_matrix=learner_readout_matrix, label_tokens_ids=label_tokens_ids, corruption_kinds=corruption_kinds, heat_per_kind=heat_per_kind)


def heat_scalar(corruption_kinds, heat_per_kind):
    picked_positions = (corruption_kinds[:, None] == jnp.arange(CORRUPTION_AIMS, dtype=jnp.int32)[None, :]).astype(jnp.float32)
    return jnp.sum(picked_positions * heat_per_kind[None, :], axis=1)


def reference(mentor_final_hiddens, mentor_readout_matrix, learner_final_hiddens, learner_readout_matrix, label_tokens_ids, corruption_kinds, heat_per_kind):
    teach_blocks = mentor_final_hiddens.reshape(N_ROWS, ROW_DEV, DT)
    stud_blocks = learner_final_hiddens.reshape(N_ROWS, ROW_DEV, DS)
    target_blocks = label_tokens_ids.reshape(N_ROWS, ROW_DEV)
    objective_blocks = corruption_kinds.reshape(N_ROWS, ROW_DEV)
    vocab_ids = jnp.arange(V, dtype=jnp.int32)

    def block(carry, pieces):
        teach, stud, target, corruption_aim = pieces
        mentor_scores = jnp.dot(teach, mentor_readout_matrix, preferred_element_type=jnp.float32)
        learner_scores = jnp.dot(stud, learner_readout_matrix, preferred_element_type=jnp.float32)
        smoothing_heat = heat_scalar(corruption_aim, heat_per_kind)[:, None]
        mentor_divided_scores = mentor_scores / smoothing_heat
        learner_divided_scores = learner_scores / smoothing_heat
        lse_t = jax.nn.logsumexp(mentor_divided_scores, axis=1)
        lse_s = jax.nn.logsumexp(learner_divided_scores, axis=1)
        lse_c = jax.nn.logsumexp(learner_scores, axis=1)
        mentor_distribution = jnp.exp(mentor_divided_scores - lse_t[:, None])
        learner_distribution = jnp.exp(learner_divided_scores - lse_s[:, None])
        mixed_distribution = jnp.exp(learner_scores - lse_c[:, None])
        divergence = jnp.sum(mentor_distribution * (mentor_divided_scores - learner_divided_scores), axis=1) - lse_t + lse_s
        indicator_vector = (target[:, None] == vocab_ids[None, :]).astype(jnp.float32)
        score_derivative = (smoothing_heat * (learner_distribution - mentor_distribution) + mixed_distribution - indicator_vector).astype(jnp.bfloat16)
        hidden_grad = lax.dot_general(score_derivative, learner_readout_matrix, (((1,), (1,)), ((), ())), preferred_element_type=jnp.float32)
        weight_grad = carry + lax.dot_general(stud, score_derivative, (((0,), (0,)), ((), ())), preferred_element_type=jnp.float32)
        return weight_grad, (divergence, hidden_grad)

    start = jnp.zeros((DS, V), jnp.float32)
    weight_grad, (divergence, hidden_grad) = lax.scan(block, start, (teach_blocks, stud_blocks, target_blocks, objective_blocks))
    return divergence.reshape(ROWS), hidden_grad.reshape(ROWS, DS), weight_grad
```

```python
import functools

import jax
import jax.numpy as jnp
from jax import lax
from jax.experimental import pallas as pl
from jax.experimental.pallas import tpu as pltpu
from jax.sharding import Mesh
from jax.sharding import PartitionSpec as P

AXES = ("zh", "zl", "x", "y", "c")
GRP_VOCAB = ("zh", "zl", "x")
ROWS = ("y", "c")
CHUNKS = 16
MESH = pl.DeviceIdType.MESH


def here():
    return {name: lax.axis_index(name) for name in AXES}


def at_z(z):
    z = lax.rem(z + 16, 8)
    return {"zh": z // 2, "zl": lax.rem(z, 2)}


def at_x(x):
    return {"x": lax.rem(x + 8, 4)}


def at_y(y):
    return {"y": lax.rem(y + 8, 4)}


def to(src, dst, sems, k, device):
    send, recv = sems
    return pltpu.make_async_remote_copy(
        src_ref=src,
        dst_ref=dst,
        send_sem=send.at[k],
        recv_sem=recv.at[k],
        device_id=device,
        device_id_type=MESH,
    )


def greet(devices):
    barrier = pltpu.get_barrier_semaphore()
    for device in devices:
        pl.semaphore_signal(barrier, inc=1, device_id=device, device_id_type=MESH)
    pl.semaphore_wait(barrier, len(devices))


def ds(start, size):
    return pl.ds(pl.multiple_of(start, size), size)


class Ring:
    def __init__(self, shard, whole, ring, pair):
        me = here()
        self.y, self.c = me["y"], me["c"]
        self.shard, self.whole, self.ring, self.pair = shard, whole, ring, pair
        self.width = shard.shape[1]
        self.nxt, self.prv = at_y(self.y + 1), at_y(self.y - 1)
        self.partner = {"c": 1 - self.c}

    def block(self, y, c, half=None):
        width = self.width
        first = (lax.rem(y + 8, 4) * 2 + c) * width
        if half is None:
            return self.whole.at[:, pl.ds(pl.multiple_of(first, width), width)]
        cut = width // 2
        return self.whole.at[:, pl.ds(pl.multiple_of(first + half * cut, cut), cut)]

    def own(self, half):
        cut = self.width // 2
        return self.shard.at[:, half * cut : (half + 1) * cut]

    MOVES = (("n", 0, 0), ("p", 0, 1), ("n", 0, 1), ("p", 0, 0), ("n", 1, 0), ("p", 1, 1))

    def send(self, k):
        way, hops, half = self.MOVES[k]
        owner = self.y - hops if way == "n" else self.y + hops
        src = self.own(half) if hops == 0 else self.block(owner, self.c, half)
        device = self.nxt if way == "n" else self.prv
        return to(src, self.block(owner, self.c, half), self.ring, k, device)

    def landed(self, k):
        way, hops, half = self.MOVES[k]
        owner = self.y - 1 - hops if way == "n" else self.y + 1 + hops
        return owner, half

    def wait(self, k):
        owner, half = self.landed(k)
        spot = self.block(owner, self.c, half)
        to(spot, spot, self.ring, k, self.nxt).wait_recv()

    def give(self, k):
        if k == 6:
            return to(self.shard, self.block(self.y, self.c), self.pair, 6, self.partner)
        spot = self.block(*((self.landed(k)[0], self.c, self.landed(k)[1])))
        return to(spot, spot, self.pair, k, self.partner)

    def taken(self, k):
        if k == 6:
            spot = self.block(self.y, 1 - self.c)
        else:
            owner, half = self.landed(k)
            spot = self.block(owner, 1 - self.c, half)
        to(spot, spot, self.pair, k, self.partner).wait_recv()


class Chain:
    def __init__(self, shard, whole, up, down):
        me = here()
        self.zh, self.zl = me["zh"], me["zl"]
        z = self.zh * 2 + self.zl
        self.above, self.below = at_z(z + 1), at_z(z - 1)
        self.shard, self.whole, self.up, self.down = shard, whole, up, down
        self.rows, self.wide = shard.shape[0], shard.shape[1] // CHUNKS

    def cut(self, k):
        return ds(k * self.wide, self.wide)

    def spot(self, quarter, k):
        q = lax.rem(quarter + 8, 4)
        return self.whole.at[ds(q * self.rows, self.rows), self.cut(k)]

    def mine(self, k):
        return self.shard.at[:, self.cut(k)]

    def up_move(self, n, k, src, quarter):
        return to(src, self.spot(quarter, k), self.up, n * CHUNKS + k, self.above)

    def down_move(self, n, k, src, quarter):
        return to(src, self.spot(quarter, k), self.down, n * CHUNKS + k, self.below)

    def wait_up(self, n, k):
        spot = self.spot(self.zh - 1 - n, k)
        to(spot, spot, self.up, n * CHUNKS + k, self.above).wait_recv()

    def wait_down(self, n, k):
        spot = self.spot(self.zh + 1 + n, k)
        to(spot, spot, self.down, n * CHUNKS + k, self.below).wait_recv()

    def start(self):
        @pl.loop(0, CHUNKS)
        def _(k):
            @pl.when(self.zl == 1)
            def _():
                self.up_move(0, k, self.mine(k), self.zh).start()

            @pl.when(self.zl == 0)
            def _():
                self.down_move(0, k, self.mine(k), self.zh).start()

    def first(self, k, parity):
        self.wait_up(0, k)

        @pl.when(self.zl == 0)
        def _():
            self.up_move(0, k, self.spot(self.zh - 1, k), self.zh - 1).start()

        if parity == 0:

            @pl.when(self.zl == 1)
            def _():
                self.up_move(1, k, self.spot(self.zh - 1, k), self.zh - 1).start()

        self.wait_down(0, k)

        @pl.when(self.zl == 1)
        def _():
            self.down_move(0, k, self.spot(self.zh + 1, k), self.zh + 1).start()

        if parity == 1:

            @pl.when(self.zl == 0)
            def _():
                self.down_move(1, k, self.spot(self.zh + 1, k), self.zh + 1).start()

    def second(self, k, parity):
        if parity == 0:
            self.wait_up(1, k)

            @pl.when(self.zl == 0)
            def _():
                self.up_move(1, k, self.spot(self.zh - 2, k), self.zh - 2).start()
        else:
            self.wait_down(1, k)

            @pl.when(self.zl == 1)
            def _():
                self.down_move(1, k, self.spot(self.zh + 2, k), self.zh + 2).start()

    def finish(self):
        @pl.loop(0, CHUNKS // 2)
        def _(j):
            for parity in (0, 1):
                k = 2 * j + parity
                spot = self.spot(self.zh, k)
                to(spot, spot, self.up, k, self.above).wait_send()
                to(spot, spot, self.down, k, self.below).wait_send()
                if parity == 0:
                    to(spot, spot, self.up, CHUNKS + k, self.above).wait_send()
                else:
                    to(spot, spot, self.down, CHUNKS + k, self.below).wait_send()


def gather_kernel(
    ht, wt, ws, ht_out, wt_out, ws_out, ht_all, wt_all, ws_all, own_sem, out_sem,
    up_s, up_r, down_s, down_r, ring_t_s, ring_t_r, ring_s_s, ring_s_r, pair_t_s, pair_t_r, pair_s_s, pair_s_r,
):
    me = here()
    z = me["zh"] * 2 + me["zl"]
    chain = Chain(ht, ht_all, (up_s, up_r), (down_s, down_r))
    teacher = Ring(wt, wt_all, (ring_t_s, ring_t_r), (pair_t_s, pair_t_r))
    student = Ring(ws, ws_all, (ring_s_s, ring_s_r), (pair_s_s, pair_s_r))
    own = [
        pltpu.make_async_copy(ws, student.block(me["y"], me["c"]), own_sem.at[0]),
        pltpu.make_async_copy(wt, teacher.block(me["y"], me["c"]), own_sem.at[1]),
        pltpu.make_async_copy(ht, ht_all.at[ds(me["zh"] * ht.shape[0], ht.shape[0]), :], own_sem.at[2]),
    ]
    for copy in own:
        copy.start()
    greet([teacher.nxt, teacher.prv, teacher.partner, at_z(z + 1), at_z(z - 1)])
    for ring in (student, teacher):
        for k in range(4):
            ring.send(k).start()
    chain.start()
    student.give(6).start()
    teacher.give(6).start()

    def firsts(start, stop):
        @pl.loop(start, stop)
        def _(j):
            chain.first(2 * j, 0)
            chain.first(2 * j + 1, 1)

    def arrivals(ring):
        for k, onward in ((0, 4), (1, 5), (2, None), (3, None)):
            ring.wait(k)
            if onward is not None:
                ring.send(onward).start()
            ring.give(k).start()

    firsts(0, 3)
    arrivals(student)
    firsts(3, CHUNKS // 2)
    arrivals(teacher)

    @pl.loop(0, CHUNKS // 2)
    def _(j):
        chain.second(2 * j, 0)
        chain.second(2 * j + 1, 1)

    for copy in own:
        copy.wait()
    outs = [pltpu.make_async_copy(ht_all, ht_out, out_sem.at[0])]
    outs[0].start()
    for ring in (student, teacher):
        for k in (4, 5):
            ring.wait(k)
            ring.give(k).start()
        for k in range(7):
            ring.taken(k)
        outs.append(pltpu.make_async_copy(ring.whole, (wt_out if ring is teacher else ws_out), out_sem.at[len(outs)]))
        outs[-1].start()
    for ring in (student, teacher):
        for k in range(6):
            ring.send(k).wait_send()
        for k in range(7):
            ring.give(k).wait_send()
    chain.finish()
    for copy in outs:
        copy.wait()


def gather_all(ht, wt, ws):
    dma = pltpu.SemaphoreType.DMA
    shapes = (
        (ht.shape[0] * 4, ht.shape[1]),
        (wt.shape[0], wt.shape[1] * 8),
        (ws.shape[0], ws.shape[1] * 8),
    )
    return pl.pallas_call(
        gather_kernel,
        out_shape=[jax.ShapeDtypeStruct(s, jnp.bfloat16) for s in shapes],
        in_specs=[pl.BlockSpec(memory_space=pl.ANY)] * 3,
        out_specs=[pl.BlockSpec(memory_space=pl.ANY)] * 3,
        scratch_shapes=[pltpu.VMEM(s, jnp.bfloat16) for s in shapes]
        + [dma((3,)), dma((3,))]
        + [dma((2 * CHUNKS,))] * 4
        + [dma((6,))] * 4
        + [dma((7,))] * 4,
        compiler_params=pltpu.CompilerParams(
            collective_id=0, has_side_effects=True, vmem_limit_bytes=32 << 20
        ),
        name="gather",
    )(ht, wt, ws)


STATS = 7


def merge(first, second):
    out = []
    for peak, sums in ((0, (1, 2)), (3, (4,)), (5, (6,))):
        top = jnp.maximum(first[peak], second[peak])
        a, b = jnp.exp(first[peak] - top), jnp.exp(second[peak] - top)
        out.append(top)
        for k in sums:
            out.append(first[k] * a + second[k] * b)
    return out


def lines(block):
    return [block[k : k + 1, :] for k in range(STATS)]


def folded(ref, count):
    parts = [lines(ref[k]) for k in range(count)]
    while len(parts) > 1:
        parts = [merge(parts[k], parts[k + 1]) for k in range(0, len(parts), 2)]
    return parts[0]


def stats_kernel(mine, out, near, far, xs, xr, zs, zr):
    me = here()
    x, z = me["x"], me["zh"] * 2 + me["zl"]
    xs_of = [at_x(x + k) for k in range(1, 4)]
    zs_of = [at_z(z + k) for k in range(1, 8)]
    greet(xs_of + zs_of)
    near[x] = mine[...]
    sends = []
    for k, device in enumerate(xs_of):
        sends.append(to(mine, near.at[x], (xs, xr), k, device))
        sends[-1].start()
    for k in range(3):
        to(mine, near.at[lax.rem(x + 3 - k, 4)], (xs, xr), k, xs_of[0]).wait_recv()
    for k, line in enumerate(folded(near, 4)):
        far[z, k : k + 1, :] = line
    for k, device in enumerate(zs_of):
        sends.append(to(far.at[z], far.at[z], (zs, zr), k, device))
        sends[-1].start()
    for k in range(7):
        to(mine, far.at[lax.rem(z + 7 - k, 8)], (zs, zr), k, zs_of[0]).wait_recv()
    for k, line in enumerate(folded(far, 8)):
        out[k : k + 1, :] = line
    out[STATS:, :] = mine[STATS:, :]
    for copy in sends:
        copy.wait_send()


def combine_stats(stats):
    dma = pltpu.SemaphoreType.DMA
    return pl.pallas_call(
        stats_kernel,
        out_shape=jax.ShapeDtypeStruct(stats.shape, jnp.float32),
        in_specs=[pl.BlockSpec(memory_space=pltpu.VMEM)],
        out_specs=pl.BlockSpec(memory_space=pltpu.VMEM),
        scratch_shapes=[
            pltpu.VMEM((4, *stats.shape), jnp.float32),
            pltpu.VMEM((8, *stats.shape), jnp.float32),
            dma((3,)), dma((3,)), dma((7,)), dma((7,)),
        ],
        compiler_params=pltpu.CompilerParams(collective_id=1, has_side_effects=True),
        name="stats",
    )(stats)


class Scatter4:
    def __init__(self, index, nxt, prv, own, bufs, temps, sems):
        self.i, self.nxt, self.prv, self.own = index, nxt, prv, own
        self.bufs, self.temps, self.sems = bufs, temps, sems

    def move(self, k, src, device):
        return to(src, self.bufs.at[k], self.sems, k, device)

    def send(self, k):
        i, nxt, prv = self.i, self.nxt, self.prv
        if k >= 4:
            return self.move(k, self.temps.at[k - 4], (nxt, prv)[k - 4])
        target, side, device = ((i + 2, 0, nxt), (i + 2, 1, prv), (i + 1, 1, nxt), (i - 1, 0, prv))[k]
        return self.move(k, self.own(target, side), device)

    def start(self):
        for k in range(4):
            self.send(k).start()

    def arrived(self, k):
        self.move(k, self.bufs.at[k], self.nxt).wait_recv()

    def middle(self):
        self.arrived(0)
        self.temps[0] = self.own(self.i + 1, 0)[...] + self.bufs[0]
        self.send(4).start()
        self.arrived(1)
        self.temps[1] = self.own(self.i - 1, 1)[...] + self.bufs[1]
        self.send(5).start()

    def last(self, put):
        for k in (2, 3, 4, 5):
            self.arrived(k)
        put(0, self.own(self.i, 0)[...] + self.bufs[3] + self.bufs[4])
        put(1, self.own(self.i, 1)[...] + self.bufs[2] + self.bufs[5])

    def finish(self):
        for k in range(6):
            self.send(k).wait_send()


class Scatter8:
    def __init__(self, index, nxt, prv, own, bufs, temps, up, down):
        self.i, self.nxt, self.prv, self.own = index, nxt, prv, own
        self.bufs, self.temps, self.up, self.down = bufs, temps, up, down
        self.n = bufs.shape[2]
        self.halves = (slice(0, self.n // 2), slice(self.n // 2, self.n))

    def up_move(self, s):
        if s == 0:
            src, dst = self.own(self.i + 4).at[self.halves[0]], self.bufs.at[0, 0, self.halves[0]]
        else:
            src, dst = self.temps.at[0, s - 1], self.bufs.at[0, s]
        return to(src, dst, self.up, s, self.nxt)

    def down_move(self, s):
        if s == 0:
            src, dst = self.own(self.i - 4).at[self.halves[1]], self.bufs.at[1, 0, self.halves[1]]
        else:
            src, dst = self.temps.at[1, s - 1], self.bufs.at[1, s]
        return to(src, dst, self.down, s, self.prv)

    def start(self):
        self.up_move(0).start()
        self.down_move(0).start()

    def step(self, s):
        a, b = self.halves
        self.up_move(s - 1).wait_recv()
        mine = self.own(self.i + 4 - s)
        if s == 1:
            self.temps[0, 0, a] = mine[a] + self.bufs[0, 0, a]
            self.temps[0, 0, b] = mine[b]
        else:
            self.temps[0, s - 1] = mine[...] + self.bufs[0, s - 1]
        self.up_move(s).start()
        self.down_move(s - 1).wait_recv()
        mine = self.own(self.i - 4 + s)
        if s == 1:
            self.temps[1, 0, a] = mine[a]
            self.temps[1, 0, b] = mine[b] + self.bufs[1, 0, b]
        else:
            self.temps[1, s - 1] = mine[...] + self.bufs[1, s - 1]
        self.down_move(s).start()

    def last(self):
        self.up_move(3).wait_recv()
        self.down_move(3).wait_recv()
        return self.own(self.i)[...] + self.bufs[0, 3] + self.bufs[1, 3]

    def finish(self):
        for s in range(4):
            self.up_move(s).wait_send()
            self.down_move(s).wait_send()


def scatter_kernel(
    wg, hg, wg_out, hg_out, pair_buf, y_buf, y_tmp, ux_buf, ux_tmp, uz_own, uz_buf, uz_tmp, vz_buf, vz_tmp, vx_own, vx_buf,
    vx_tmp, pair_s, pair_r, y_s, y_r, ux_s, ux_r, vx_s, vx_r, uzu_s, uzu_r, uzd_s, uzd_r, vzu_s, vzu_r, vzd_s, vzd_r,
):
    me = here()
    x, y, c, z = me["x"], me["y"], me["c"], me["zh"] * 2 + me["zl"]
    partner = {"c": 1 - c}
    x_nxt, x_prv, y_nxt, y_prv, z_nxt, z_prv = at_x(x + 1), at_x(x - 1), at_y(y + 1), at_y(y - 1), at_z(z + 1), at_z(z - 1)
    greet([partner, x_nxt, x_prv, y_nxt, y_prv, z_nxt, z_prv])
    wide = wg.shape[1] // 8
    half = wide // 2

    def given(k):
        src = wg.at[:, pl.ds(pl.multiple_of((k * 2 + 1 - c) * wide, wide), wide)]
        return to(src, pair_buf.at[k], (pair_s, pair_r), k, partner)

    order = [lax.rem(y + k, 4) for k in (2, 1, 3, 0)]
    for k in order:
        given(k).start()

    ux = Scatter4(x, x_nxt, x_prv, lambda t, side: hg.at[:, lax.rem(t + 8, 4), 0, side], ux_buf, ux_tmp, (ux_s, ux_r))
    vz = Scatter8(z, z_nxt, z_prv, lambda t: hg.at[lax.rem(t + 16, 8), :, 1], vz_buf, vz_tmp, (vzu_s, vzu_r), (vzd_s, vzd_r))
    uz = Scatter8(z, z_nxt, z_prv, lambda t: uz_own.at[lax.rem(t + 16, 8)], uz_buf, uz_tmp, (uzu_s, uzu_r), (uzd_s, uzd_r))
    vx = Scatter4(x, x_nxt, x_prv, lambda t, side: vx_own.at[lax.rem(t + 8, 4), side], vx_buf, vx_tmp, (vx_s, vx_r))
    wy = Scatter4(
        y, y_nxt, y_prv, lambda t, side: pair_buf.at[lax.rem(t + 8, 4), :, side * half : (side + 1) * half], y_buf, y_tmp, (y_s, y_r)
    )

    def put_ux(side, value):
        uz_own[:, side] = value

    def put_vx(side, value):
        hg_out[1, side] = value

    def put_wy(side, value):
        wg_out[:, side * half : (side + 1) * half] = value

    ux.start()
    vz.start()
    for n, k in enumerate(order):
        given(k).wait_recv()
        pair_buf[k] = pair_buf[k] + wg[:, pl.ds(pl.multiple_of((k * 2 + c) * wide, wide), wide)]
        for number in ((0, 1), (2,), (3,), ())[n]:
            wy.send(number).start()
    vz.step(1)
    ux.middle()
    vz.step(2)
    wy.middle()
    vz.step(3)
    ux.last(put_ux)
    uz.start()
    vx_own[...] = vz.last()
    vx.start()
    uz.step(1)
    vx.middle()
    uz.step(2)
    uz.step(3)
    wy.last(put_wy)
    vx.last(put_vx)
    hg_out[0] = uz.last()
    for k in order:
        given(k).wait_send()
    for ring in (ux, vz, uz, vx, wy):
        ring.finish()


def scatter_sums(wg, hg):
    dma, f32 = pltpu.SemaphoreType.DMA, jnp.float32
    vocab, wide = wg.shape[0], wg.shape[1] // 8
    rows, tokens = hg.shape[0] // 128, hg.shape[1]
    tile = (rows, tokens)
    vmem = lambda *shape: pltpu.VMEM(shape, f32)
    out = pl.pallas_call(
        scatter_kernel,
        out_shape=[jax.ShapeDtypeStruct((vocab, wide), f32), jax.ShapeDtypeStruct((2, 2, *tile), f32)],
        in_specs=[pl.BlockSpec(memory_space=pltpu.VMEM)] * 2,
        out_specs=[pl.BlockSpec(memory_space=pltpu.VMEM)] * 2,
        scratch_shapes=[
            vmem(4, vocab, wide), vmem(6, vocab, wide // 2), vmem(2, vocab, wide // 2),
            vmem(6, 8, *tile), vmem(2, 8, *tile),
            vmem(8, 2, *tile), vmem(2, 4, 2, *tile), vmem(2, 3, 2, *tile),
            vmem(2, 4, 4, 2, *tile), vmem(2, 3, 4, 2, *tile),
            vmem(4, 2, *tile), vmem(6, *tile), vmem(2, *tile),
        ]
        + [dma((4,))] * 2
        + [dma((6,))] * 6
        + [dma((4,))] * 8,
        compiler_params=pltpu.CompilerParams(collective_id=2, has_side_effects=True, vmem_limit_bytes=56 << 20),
        name="scatter",
    )(wg, hg.reshape(8, 4, 2, 2, rows, tokens))
    return out[0], out[1].reshape(rows * 4, tokens)


def heat_scalar(corruption_kinds, heat_per_kind):
    picked = (corruption_kinds[:, None] == jnp.arange(heat_per_kind.shape[0], dtype=jnp.int32)[None, :]).astype(jnp.float32)
    return jnp.sum(picked * heat_per_kind[None, :], axis=1)


def local(ht, wt, hs, ws, labels, kinds, heats):
    ht_all, wt_all, ws_all = gather_all(ht, wt.T, ws.T)
    f32 = jnp.float32
    both = (((1,), (1,)), ((), ()))
    logit_t = lax.dot_general(wt_all, ht_all, both, preferred_element_type=f32)
    logit_s = lax.dot_general(ws_all, hs, both, preferred_element_type=f32)
    tau = heat_scalar(kinds, heats)[None, :]
    scaled_t, scaled_s = logit_t / tau, logit_s / tau
    top_t, top_s, top_c = (jnp.max(v, axis=0, keepdims=True) for v in (scaled_t, scaled_s, logit_s))
    exp_t, exp_s, exp_c = jnp.exp(scaled_t - top_t), jnp.exp(scaled_s - top_s), jnp.exp(logit_s - top_c)
    total = lambda v: jnp.sum(v, axis=0, keepdims=True)
    stats = jnp.concatenate(
        [top_t, total(exp_t), total(exp_t * (scaled_t - scaled_s)), top_s, total(exp_s), top_c, total(exp_c), tau]
    )
    whole = combine_stats(stats)
    peak_t, sum_t, cross, peak_s, sum_s, peak_c, sum_c = (whole[k : k + 1] for k in range(STATS))
    divergence = (cross / sum_t - peak_t - jnp.log(sum_t) + peak_s + jnp.log(sum_s))[0]
    prob_t = exp_t * (jnp.exp(top_t - peak_t) / sum_t)
    prob_s = exp_s * (jnp.exp(top_s - peak_s) / sum_s)
    prob_c = exp_c * (jnp.exp(top_c - peak_c) / sum_c)
    vocab = wt.shape[1]
    entries = lax.axis_index(GRP_VOCAB) * vocab + jnp.arange(vocab, dtype=jnp.int32)
    hot = (labels[None, :] == entries[:, None]).astype(f32)
    grad = (tau * (prob_s - prob_t) + prob_c - hot).astype(jnp.bfloat16)
    hg = lax.dot_general(ws_all, grad, (((0,), (0,)), ((), ())), preferred_element_type=f32)
    wg = lax.dot_general(grad, hs, (((1,), (0,)), ((), ())), preferred_element_type=f32)
    wg, hg = scatter_sums(wg, hg)
    return divergence, hg.T, wg.T


def solution(mesh):
    finer = Mesh(mesh.devices.reshape(mesh.shape["grp"], 2, 4, 4, 2), AXES)
    return jax.shard_map(
        local,
        mesh=finer,
        in_specs=(
            P((*ROWS, "zh"), None),
            P(ROWS, GRP_VOCAB),
            P(ROWS, None),
            P(ROWS, GRP_VOCAB),
            P(ROWS),
            P(ROWS),
            P(),
        ),
        out_specs=(P(ROWS), P(ROWS, GRP_VOCAB), P(ROWS, GRP_VOCAB)),
        check_vma=False,
    )
```

```python
import functools

import jax
import jax.numpy as jnp
from jax import lax
from jax.experimental import pallas as pl
from jax.experimental.pallas import tpu as pltpu
from jax.sharding import Mesh
from jax.sharding import PartitionSpec as P

AXES = ("zh", "zl", "x", "y", "c")
GRP_VOCAB = ("zh", "zl", "x")
ROWS = ("y", "c")
CHUNKS = 16
MESH = pl.DeviceIdType.MESH


def here():
    return {name: lax.axis_index(name) for name in AXES}


def at_z(z):
    z = lax.rem(z + 16, 8)
    return {"zh": z // 2, "zl": lax.rem(z, 2)}


def at_x(x):
    return {"x": lax.rem(x + 8, 4)}


def at_y(y):
    return {"y": lax.rem(y + 8, 4)}


def to(src, dst, sems, k, device):
    send, recv = sems
    return pltpu.make_async_remote_copy(
        src_ref=src,
        dst_ref=dst,
        send_sem=send.at[k],
        recv_sem=recv.at[k],
        device_id=device,
        device_id_type=MESH,
    )


def greet(devices):
    barrier = pltpu.get_barrier_semaphore()
    for device in devices:
        pl.semaphore_signal(barrier, inc=1, device_id=device, device_id_type=MESH)
    pl.semaphore_wait(barrier, len(devices))


def ds(start, size):
    return pl.ds(pl.multiple_of(start, size), size)


class Ring:
    def __init__(self, shard, whole, ring, pair):
        me = here()
        self.y, self.c = me["y"], me["c"]
        self.shard, self.whole, self.ring, self.pair = shard, whole, ring, pair
        self.nxt, self.prv = at_y(self.y + 1), at_y(self.y - 1)
        self.partner = {"c": 1 - self.c}

    def block(self, y, c, half=None):
        r = lax.rem(y + 8, 4) * 2 + c
        return self.whole.at[r] if half is None else self.whole.at[r, half]

    MOVES = (("n", 0, 0), ("p", 0, 1), ("n", 0, 1), ("p", 0, 0), ("n", 1, 0), ("p", 1, 1))

    def send(self, k):
        way, hops, half = self.MOVES[k]
        owner = self.y - hops if way == "n" else self.y + hops
        device = self.nxt if way == "n" else self.prv
        spot = self.block(owner, self.c, half)
        return to(spot, spot, self.ring, k, device)

    def landed(self, k):
        way, hops, half = self.MOVES[k]
        owner = self.y - 1 - hops if way == "n" else self.y + 1 + hops
        return owner, half

    def wait(self, k):
        owner, half = self.landed(k)
        spot = self.block(owner, self.c, half)
        to(spot, spot, self.ring, k, self.nxt).wait_recv()

    def give(self, k):
        if k == 6:
            spot = self.block(self.y, self.c)
            return to(spot, spot, self.pair, 6, self.partner)
        owner, half = self.landed(k)
        spot = self.block(owner, self.c, half)
        return to(spot, spot, self.pair, k, self.partner)

    def taken(self, k):
        if k == 6:
            spot = self.block(self.y, 1 - self.c)
        else:
            owner, half = self.landed(k)
            spot = self.block(owner, 1 - self.c, half)
        to(spot, spot, self.pair, k, self.partner).wait_recv()


class Chain:
    def __init__(self, whole, rows, out1, mate1, out2, mate2):
        me = here()
        self.zh, self.zl = me["zh"], me["zl"]
        z = self.zh * 2 + self.zl
        self.away = 2 * self.zl - 1
        self.out, self.mate = at_z(z + self.away), at_z(z - self.away)
        self.whole, self.sems = whole, (out1, mate1, out2, mate2)
        self.rows = rows

    def move(self, kind, slot, k, quarter, device):
        q = lax.rem(quarter + 8, 4)
        spot = self.whole.at[k, ds(q * self.rows, self.rows)]
        return to(spot, spot, self.sems[kind], slot, device)

    def out1(self, k):
        return self.move(0, k, k, self.zh, self.out)

    def mate1(self, k):
        return self.move(1, k, k, self.zh + self.away, self.mate)

    def out2(self, j):
        return self.move(2, j, 2 * j + 1 - self.zl, self.zh - self.away, self.out)

    def mate2(self, j):
        return self.move(3, j, 2 * j + self.zl, self.zh + 2 * self.away, self.mate)

    def got_out1(self, k):
        self.move(0, k, k, self.zh + self.away, self.out).wait_recv()

    def got_mate1(self, k):
        self.move(1, k, k, self.zh - self.away, self.out).wait_recv()

    def got_out2(self, j):
        self.move(2, j, 2 * j + self.zl, self.zh + 2 * self.away, self.out).wait_recv()

    def got_mate2(self, j):
        self.move(3, j, 2 * j + 1 - self.zl, self.zh - 2 * self.away, self.out).wait_recv()

    def pair(self, j):
        for k in (2 * j, 2 * j + 1):
            self.got_out1(k)
            self.mate1(k).start()

        @pl.when(j > 0)
        def _():
            self.back(j - 1)

    def back(self, j):
        self.got_mate1(2 * j)
        self.got_mate1(2 * j + 1)
        self.out2(j).start()

    def second(self, j):
        self.got_out2(j)
        self.mate2(j).start()

    def finish(self):
        @pl.loop(0, CHUNKS // 2)
        def _(j):
            for k in (2 * j, 2 * j + 1):
                self.out1(k).wait_send()
                self.mate1(k).wait_send()
            self.out2(j).wait_send()
            self.mate2(j).wait_send()


STATS = 7


def merge(first, second):
    out = []
    for peak, sums in ((0, (1, 2)), (3, (4,)), (5, (6,))):
        top = jnp.maximum(first[peak], second[peak])
        a, b = jnp.exp(first[peak] - top), jnp.exp(second[peak] - top)
        out.append(top)
        for k in sums:
            out.append(first[k] * a + second[k] * b)
    return out


def lines(block):
    return [block[k : k + 1, :] for k in range(STATS)]


def folded(ref, count):
    parts = [lines(ref[k]) for k in range(count)]
    while len(parts) > 1:
        parts = [merge(parts[k], parts[k + 1]) for k in range(0, len(parts), 2)]
    return parts[0]


class Exchange:
    def __init__(self, near, far, xs, zs):
        me = here()
        self.x, self.z = me["x"], me["zh"] * 2 + me["zl"]
        self.xs_of = [at_x(self.x + k) for k in range(1, 4)]
        self.zs_of = [at_z(self.z + k) for k in range(1, 8)]
        self.near, self.far, self.xs, self.zs = near, far, xs, zs

    def run(self, mine, out):
        x, z, near, far = self.x, self.z, self.near, self.far
        near[x] = mine[...]
        sends = [to(near.at[x], near.at[x], self.xs, k, device) for k, device in enumerate(self.xs_of)]
        for copy in sends:
            copy.start()
        for k in range(3):
            spot = near.at[lax.rem(x + 3 - k, 4)]
            to(spot, spot, self.xs, k, self.xs_of[0]).wait_recv()
        for k, line in enumerate(folded(near, 4)):
            far[z, k : k + 1, :] = line
        more = [to(far.at[z], far.at[z], self.zs, k, device) for k, device in enumerate(self.zs_of)]
        for copy in more:
            copy.start()
        for k in range(7):
            spot = far.at[lax.rem(z + 7 - k, 8)]
            to(spot, spot, self.zs, k, self.zs_of[0]).wait_recv()
        for k, line in enumerate(folded(far, 8)):
            out[k : k + 1, :] = line
        out[STATS:, :] = mine[STATS:, :]
        for copy in sends + more:
            copy.wait_send()


BOTH_MINOR = (((1,), (1,)), ((), ()))


def forward_kernel(
    tau, ht, wt, hs, ws, lt_out, ls_out, ws_out, local_out, whole_out,
    ht_all, wt_all, hs_all, ws_all, lt, ls, near, far, own_sem, out_sem,
    o1s, o1r, m1s, m1r, o2s, o2r, m2s, m2r, ring_t_s, ring_t_r, ring_s_s, ring_s_r, pair_t_s, pair_t_r, pair_s_s, pair_s_r,
    xs, xr, zs, zr,
):
    me = here()
    y, c = me["y"], me["c"]
    chain = Chain(ht_all, ht.shape[0], (o1s, o1r), (m1s, m1r), (o2s, o2r), (m2s, m2r))
    teacher = Ring(wt, wt_all, (ring_t_s, ring_t_r), (pair_t_s, pair_t_r))
    student = Ring(ws, ws_all, (ring_s_s, ring_s_r), (pair_s_s, pair_s_r))
    exchange = Exchange(near, far, (xs, xr), (zs, zr))
    wide, tokens, padded = ht_all.shape[2], hs.shape[0], lt.shape[1]
    first = 4 * (y + 3)

    def mine(k):
        chunk = lax.rem(k + first, CHUNKS)
        spot = ht_all.at[k, ds(me["zh"] * ht.shape[0], ht.shape[0])]
        return pltpu.make_async_copy(ht.at[:, ds(chunk * wide, wide)], spot, own_sem.at[k])

    own = []
    for ring in (student, teacher):
        half = ring.shard.shape[1] // 2
        for side in (0, 1):
            src = ring.shard.at[:, side * half : (side + 1) * half]
            own.append(pltpu.make_async_copy(src, ring.block(y, c, side), own_sem.at[CHUNKS + len(own)]))
    states = pltpu.make_async_copy(hs, hs_all.at[pl.ds(0, tokens)], own_sem.at[CHUNKS + 4])

    @pl.loop(0, CHUNKS)
    def _(k):
        mine(k).start()

    for copy in own:
        copy.start()
    states.start()
    greet([teacher.nxt, teacher.prv, teacher.partner] + exchange.xs_of + exchange.zs_of)
    for copy in own:
        copy.wait()
    for k in range(4):
        student.send(k).start()
    for k in range(2):
        teacher.send(k).start()

    @pl.loop(0, CHUNKS)
    def _(k):
        mine(k).wait()
        chain.out1(k).start()

    student.give(6).start()
    teacher.give(6).start()
    states.wait()

    def arrivals(ring):
        for k, onward in ((0, 4), (1, 5), (2, None), (3, None)):
            ring.wait(k)
            if onward is not None:
                ring.send(onward).start()
            ring.give(k).start()

    def block_of(i):
        return lax.rem(i + 2 * (y + 3), 8)

    def student_block(i):
        r = block_of(i)

        @pl.loop(0, padded // 256)
        def _(n):
            tile = ds(n * 256, 256)
            part = lax.dot_general(
                jnp.concatenate([ws_all[r, 0], ws_all[r, 1]], axis=1),
                hs_all[tile, ds(r * ws.shape[1], ws.shape[1])],
                BOTH_MINOR,
                preferred_element_type=jnp.float32,
            )

            @pl.when(i == 0)
            def _():
                ls[:, tile] = part

            @pl.when(i > 0)
            def _():
                ls[:, tile] += part

    def teacher_block(i):
        r = block_of(i)

        @pl.loop(0, padded // 256)
        def _(n):
            tile = ds(n * 256, 256)
            part = lax.dot_general(
                jnp.concatenate([wt_all[r, 0], wt_all[r, 1]], axis=1),
                jnp.concatenate([ht_all[2 * i, tile], ht_all[2 * i + 1, tile]], axis=1),
                BOTH_MINOR,
                preferred_element_type=jnp.float32,
            )

            @pl.when(i == 0)
            def _():
                lt[:, tile] = part

            @pl.when(i > 0)
            def _():
                lt[:, tile] += part

    outs = []

    def put(src, dst):
        outs.append(pltpu.make_async_copy(src, dst, out_sem.at[len(outs)]))
        outs[-1].start()

    @pl.loop(0, 3)
    def _(j):
        chain.pair(j)

    arrivals(student)
    for k in range(2, 4):
        teacher.send(k).start()
    for k in (6, 0, 1, 2, 3):
        student.taken(k)

    @pl.loop(3, 6)
    def _(j):
        chain.pair(j)
        student_block(2 * (j - 3))
        student_block(2 * (j - 3) + 1)

    for k in (4, 5):
        student.wait(k)
        student.give(k).start()

    @pl.loop(6, CHUNKS // 2)
    def _(j):
        chain.pair(j)

    chain.back(CHUNKS // 2 - 1)
    for k in (4, 5):
        student.taken(k)
    student_block(6)
    student_block(7)
    half = ws.shape[1] // 2
    for n in range(16):
        put(ws_all.at[n // 2, n % 2], ws_out.at[:, n * half : (n + 1) * half])
    put(ls, ls_out)

    @pl.loop(0, padded // 128)
    def _(n):
        tile = ds(n * 128, 128)
        share = 1.0 / tau[:, tile]
        v = ls[:, tile]
        top = jnp.max(v, axis=0, keepdims=True)
        v = v - top
        local_out[3:4, tile] = top * share
        local_out[4:5, tile] = jnp.sum(jnp.exp(v * share), axis=0, keepdims=True)
        local_out[5:6, tile] = top
        local_out[6:7, tile] = jnp.sum(jnp.exp(v), axis=0, keepdims=True)
        local_out[7:8, tile] = tau[:, tile]

    arrivals(teacher)
    for k in (6, 0, 1, 2, 3):
        teacher.taken(k)

    @pl.loop(0, 6)
    def _(i):
        chain.second(i)

        @pl.when(i > 0)
        def _():
            chain.got_mate2(i - 1)
            teacher_block(i - 1)

    chain.second(6)
    chain.second(7)
    for k in (4, 5):
        teacher.wait(k)
        teacher.give(k).start()

    @pl.loop(5, 8)
    def _(i):
        chain.got_mate2(i)

        @pl.when(i == 6)
        def _():
            for k in (4, 5):
                teacher.taken(k)

        teacher_block(i)

    put(lt, lt_out)

    @pl.loop(0, padded // 128)
    def _(n):
        tile = ds(n * 128, 128)
        share = 1.0 / tau[:, tile]
        v = lt[:, tile] * share
        top = jnp.max(v, axis=0, keepdims=True)
        e = jnp.exp(v - top)
        local_out[0:1, tile] = top
        local_out[1:2, tile] = jnp.sum(e, axis=0, keepdims=True)
        local_out[2:3, tile] = jnp.sum(e * (v - ls[:, tile] * share), axis=0, keepdims=True)

    exchange.run(local_out, whole_out)
    for ring in (student, teacher):
        for k in range(6):
            ring.send(k).wait_send()
        for k in range(7):
            ring.give(k).wait_send()
    chain.finish()
    for copy in outs:
        copy.wait()


def forward(tau, ht, wt, hs, ws):
    dma, b16, f32 = pltpu.SemaphoreType.DMA, jnp.bfloat16, jnp.float32
    vocab, tokens, padded = wt.shape[0], hs.shape[0], tau.shape[1]
    space, vmem = pl.BlockSpec(memory_space=pl.ANY), pl.BlockSpec(memory_space=pltpu.VMEM)
    logits = jax.ShapeDtypeStruct((vocab, padded), f32)
    stats = jax.ShapeDtypeStruct((8, padded), f32)
    pairs = lambda *shape: [dma(shape), dma(shape)]
    return pl.pallas_call(
        forward_kernel,
        out_shape=[logits, logits, jax.ShapeDtypeStruct((vocab, ws.shape[1] * 8), b16), stats, stats],
        in_specs=[vmem] + [space] * 4,
        out_specs=[space] * 3 + [vmem] * 2,
        scratch_shapes=[
            pltpu.VMEM((CHUNKS, padded, ht.shape[1] // CHUNKS), b16),
            pltpu.VMEM((8, 2, vocab, wt.shape[1] // 2), b16),
            pltpu.VMEM((padded, hs.shape[1]), b16),
            pltpu.VMEM((8, 2, vocab, ws.shape[1] // 2), b16),
            pltpu.VMEM((vocab, padded), f32),
            pltpu.VMEM((vocab, padded), f32),
            pltpu.VMEM((4, 8, padded), f32),
            pltpu.VMEM((8, 8, padded), f32),
            dma((CHUNKS + 5,)),
            dma((18,)),
        ]
        + pairs(CHUNKS) * 2
        + pairs(CHUNKS // 2) * 2
        + pairs(6) * 2
        + pairs(7) * 2
        + pairs(3)
        + pairs(7),
        compiler_params=pltpu.CompilerParams(collective_id=0, has_side_effects=True, vmem_limit_bytes=56 << 20),
        name="forward",
    )(tau, ht, wt, hs, ws)


class Scatter4:
    def __init__(self, index, nxt, prv, own, bufs, temps, sems):
        self.i, self.nxt, self.prv, self.own = index, nxt, prv, own
        self.bufs, self.temps, self.sems = bufs, temps, sems

    def move(self, k, src, device):
        return to(src, self.bufs.at[k], self.sems, k, device)

    def send(self, k):
        i, nxt, prv = self.i, self.nxt, self.prv
        if k >= 4:
            return self.move(k, self.temps.at[k - 4], (nxt, prv)[k - 4])
        target, side, device = ((i + 2, 0, nxt), (i + 2, 1, prv), (i + 1, 1, nxt), (i - 1, 0, prv))[k]
        return self.move(k, self.own(target, side), device)

    def start(self):
        for k in range(4):
            self.send(k).start()

    def arrived(self, k):
        self.move(k, self.bufs.at[k], self.nxt).wait_recv()

    def middle(self):
        self.arrived(0)
        self.temps[0] = self.own(self.i + 1, 0)[...] + self.bufs[0]
        self.send(4).start()
        self.arrived(1)
        self.temps[1] = self.own(self.i - 1, 1)[...] + self.bufs[1]
        self.send(5).start()

    def last(self, put):
        for k in (2, 3, 4, 5):
            self.arrived(k)
        put(0, self.own(self.i, 0)[...] + self.bufs[3] + self.bufs[4])
        put(1, self.own(self.i, 1)[...] + self.bufs[2] + self.bufs[5])

    def finish(self):
        for k in range(6):
            self.send(k).wait_send()


class Scatter8:
    def __init__(self, index, nxt, prv, own, bufs, temps, up, down):
        self.i, self.nxt, self.prv, self.own = index, nxt, prv, own
        self.bufs, self.temps, self.up, self.down = bufs, temps, up, down
        self.n = bufs.shape[2]
        self.halves = (slice(0, self.n // 2), slice(self.n // 2, self.n))

    def up_move(self, s):
        if s == 0:
            src, dst = self.own(self.i + 4).at[self.halves[0]], self.bufs.at[0, 0, self.halves[0]]
        else:
            src, dst = self.temps.at[0, s - 1], self.bufs.at[0, s]
        return to(src, dst, self.up, s, self.nxt)

    def down_move(self, s):
        if s == 0:
            src, dst = self.own(self.i - 4).at[self.halves[1]], self.bufs.at[1, 0, self.halves[1]]
        else:
            src, dst = self.temps.at[1, s - 1], self.bufs.at[1, s]
        return to(src, dst, self.down, s, self.prv)

    def start(self):
        self.up_move(0).start()
        self.down_move(0).start()

    def step(self, s):
        a, b = self.halves
        self.up_move(s - 1).wait_recv()
        mine = self.own(self.i + 4 - s)
        if s == 1:
            self.temps[0, 0, a] = mine[a] + self.bufs[0, 0, a]
            self.temps[0, 0, b] = mine[b]
        else:
            self.temps[0, s - 1] = mine[...] + self.bufs[0, s - 1]
        self.up_move(s).start()
        self.down_move(s - 1).wait_recv()
        mine = self.own(self.i - 4 + s)
        if s == 1:
            self.temps[1, 0, a] = mine[a]
            self.temps[1, 0, b] = mine[b] + self.bufs[1, 0, b]
        else:
            self.temps[1, s - 1] = mine[...] + self.bufs[1, s - 1]
        self.down_move(s).start()

    def last(self):
        self.up_move(3).wait_recv()
        self.down_move(3).wait_recv()
        return self.own(self.i)[...] + self.bufs[0, 3] + self.bufs[1, 3]

    def finish(self):
        for s in range(4):
            self.up_move(s).wait_send()
            self.down_move(s).wait_send()


def scatter_kernel(
    wg, hg, wg_out, hg_out, pair_buf, y_buf, y_tmp, ux_buf, ux_tmp, uz_own, uz_buf, uz_tmp, vz_buf, vz_tmp, vx_own, vx_buf,
    vx_tmp, pair_s, pair_r, y_s, y_r, ux_s, ux_r, vx_s, vx_r, uzu_s, uzu_r, uzd_s, uzd_r, vzu_s, vzu_r, vzd_s, vzd_r,
):
    me = here()
    x, y, c, z = me["x"], me["y"], me["c"], me["zh"] * 2 + me["zl"]
    partner = {"c": 1 - c}
    x_nxt, x_prv, y_nxt, y_prv, z_nxt, z_prv = at_x(x + 1), at_x(x - 1), at_y(y + 1), at_y(y - 1), at_z(z + 1), at_z(z - 1)
    greet([partner, x_nxt, x_prv, y_nxt, y_prv, z_nxt, z_prv])
    wide = wg.shape[1] // 8
    half = wide // 2

    def given(k):
        src = wg.at[:, pl.ds(pl.multiple_of((k * 2 + 1 - c) * wide, wide), wide)]
        return to(src, pair_buf.at[k], (pair_s, pair_r), k, partner)

    order = [lax.rem(y + k, 4) for k in (2, 1, 3, 0)]
    for k in order:
        given(k).start()

    ux = Scatter4(x, x_nxt, x_prv, lambda t, side: hg.at[:, lax.rem(t + 8, 4), 0, side], ux_buf, ux_tmp, (ux_s, ux_r))
    vz = Scatter8(z, z_nxt, z_prv, lambda t: hg.at[lax.rem(t + 16, 8), :, 1], vz_buf, vz_tmp, (vzu_s, vzu_r), (vzd_s, vzd_r))
    uz = Scatter8(z, z_nxt, z_prv, lambda t: uz_own.at[lax.rem(t + 16, 8)], uz_buf, uz_tmp, (uzu_s, uzu_r), (uzd_s, uzd_r))
    vx = Scatter4(x, x_nxt, x_prv, lambda t, side: vx_own.at[lax.rem(t + 8, 4), side], vx_buf, vx_tmp, (vx_s, vx_r))
    wy = Scatter4(
        y, y_nxt, y_prv, lambda t, side: pair_buf.at[lax.rem(t + 8, 4), :, side * half : (side + 1) * half], y_buf, y_tmp, (y_s, y_r)
    )

    def put_ux(side, value):
        uz_own[:, side] = value

    def put_vx(side, value):
        hg_out[1, side] = value

    def put_wy(side, value):
        wg_out[:, side * half : (side + 1) * half] = value

    ux.start()
    vz.start()
    for n, k in enumerate(order):
        given(k).wait_recv()
        pair_buf[k] = pair_buf[k] + wg[:, pl.ds(pl.multiple_of((k * 2 + c) * wide, wide), wide)]
        for number in ((0, 1), (2,), (3,), ())[n]:
            wy.send(number).start()
    vz.step(1)
    ux.middle()
    vz.step(2)
    wy.middle()
    vz.step(3)
    ux.last(put_ux)
    uz.start()
    vx_own[...] = vz.last()
    vx.start()
    uz.step(1)
    vx.middle()
    uz.step(2)
    uz.step(3)
    wy.last(put_wy)
    vx.last(put_vx)
    hg_out[0] = uz.last()
    for k in order:
        given(k).wait_send()
    for ring in (ux, vz, uz, vx, wy):
        ring.finish()


def scatter_sums(wg, hg):
    dma, f32 = pltpu.SemaphoreType.DMA, jnp.float32
    vocab, wide = wg.shape[0], wg.shape[1] // 8
    rows, tokens = hg.shape[0] // 128, hg.shape[1]
    tile = (rows, tokens)
    vmem = lambda *shape: pltpu.VMEM(shape, f32)
    out = pl.pallas_call(
        scatter_kernel,
        out_shape=[jax.ShapeDtypeStruct((vocab, wide), f32), jax.ShapeDtypeStruct((2, 2, *tile), f32)],
        in_specs=[pl.BlockSpec(memory_space=pltpu.VMEM)] * 2,
        out_specs=[pl.BlockSpec(memory_space=pltpu.VMEM)] * 2,
        scratch_shapes=[
            vmem(4, vocab, wide), vmem(6, vocab, wide // 2), vmem(2, vocab, wide // 2),
            vmem(6, 8, *tile), vmem(2, 8, *tile),
            vmem(8, 2, *tile), vmem(2, 4, 2, *tile), vmem(2, 3, 2, *tile),
            vmem(2, 4, 4, 2, *tile), vmem(2, 3, 4, 2, *tile),
            vmem(4, 2, *tile), vmem(6, *tile), vmem(2, *tile),
        ]
        + [dma((4,))] * 2
        + [dma((6,))] * 6
        + [dma((4,))] * 8,
        compiler_params=pltpu.CompilerParams(collective_id=2, has_side_effects=True, vmem_limit_bytes=56 << 20),
        name="scatter",
    )(wg, hg.reshape(8, 4, 2, 2, rows, tokens))
    return out[0], out[1].reshape(rows * 4, tokens)


def heat_scalar(corruption_kinds, heat_per_kind):
    picked = (corruption_kinds[:, None] == jnp.arange(heat_per_kind.shape[0], dtype=jnp.int32)[None, :]).astype(jnp.float32)
    return jnp.sum(picked * heat_per_kind[None, :], axis=1)


def local(ht, wt, hs, ws, labels, kinds, heats):
    f32 = jnp.float32
    vocab, tokens = wt.shape[1], hs.shape[0]
    padded = -(-tokens // 256) * 256
    tau = jnp.pad(heat_scalar(kinds, heats), (0, padded - tokens), constant_values=1.0)[None, :]
    logit_t, logit_s, ws_all, stats, whole = forward(tau, ht, wt.T, hs, ws.T)
    logit_t, logit_s, tau, whole = (v[:, :tokens] for v in (logit_t, logit_s, tau, whole))
    peak_t, sum_t, cross, peak_s, sum_s, peak_c, sum_c = (whole[k : k + 1] for k in range(STATS))
    lse_t, lse_s, lse_c = peak_t + jnp.log(sum_t), peak_s + jnp.log(sum_s), peak_c + jnp.log(sum_c)
    divergence = (cross / sum_t - peak_t - jnp.log(sum_t) + peak_s + jnp.log(sum_s))[0]
    share = 1.0 / tau
    prob_t, prob_s = jnp.exp(logit_t * share - lse_t), jnp.exp(logit_s * share - lse_s)
    prob_c = jnp.exp(logit_s - lse_c)
    entries = lax.axis_index(GRP_VOCAB) * vocab + jnp.arange(vocab, dtype=jnp.int32)
    hot = (labels[None, :] == entries[:, None]).astype(f32)
    grad = (tau * (prob_s - prob_t) + prob_c - hot).astype(jnp.bfloat16)
    hg = lax.dot_general(ws_all, grad, (((0,), (0,)), ((), ())), preferred_element_type=f32)
    wg = lax.dot_general(grad, hs, (((1,), (0,)), ((), ())), preferred_element_type=f32)
    wg, hg = scatter_sums(wg, hg)
    return divergence, hg.T, wg.T


def solution(mesh):
    finer = Mesh(mesh.devices.reshape(mesh.shape["grp"], 2, 4, 4, 2), AXES)
    return jax.shard_map(
        local,
        mesh=finer,
        in_specs=(
            P((*ROWS, "zh"), None),
            P(ROWS, GRP_VOCAB),
            P(ROWS, None),
            P(ROWS, GRP_VOCAB),
            P(ROWS),
            P(ROWS),
            P(),
        ),
        out_specs=(P(ROWS), P(ROWS, GRP_VOCAB), P(ROWS, GRP_VOCAB)),
        check_vma=False,
    )
```

```python
import functools

import jax
import jax.numpy as jnp
from jax import lax
from jax.experimental import pallas as pl
from jax.experimental.pallas import tpu as pltpu
from jax.sharding import Mesh
from jax.sharding import PartitionSpec as P

AXES = ("zh", "zl", "x", "y", "c")
GRP_VOCAB = ("zh", "zl", "x")
ROWS = ("y", "c")
CHUNKS = 16
MESH = pl.DeviceIdType.MESH


def here():
    return {name: lax.axis_index(name) for name in AXES}


def at_z(z):
    z = lax.rem(z + 16, 8)
    return {"zh": z // 2, "zl": lax.rem(z, 2)}


def at_x(x):
    return {"x": lax.rem(x + 8, 4)}


def at_y(y):
    return {"y": lax.rem(y + 8, 4)}


def to(src, dst, sems, k, device):
    send, recv = sems
    return pltpu.make_async_remote_copy(
        src_ref=src,
        dst_ref=dst,
        send_sem=send.at[k],
        recv_sem=recv.at[k],
        device_id=device,
        device_id_type=MESH,
    )


def greet(devices):
    barrier = pltpu.get_barrier_semaphore()
    for device in devices:
        pl.semaphore_signal(barrier, inc=1, device_id=device, device_id_type=MESH)
    pl.semaphore_wait(barrier, len(devices))


def ds(start, size):
    return pl.ds(pl.multiple_of(start, size), size)


class Ring:
    def __init__(self, shard, whole, ring, pair):
        me = here()
        self.y, self.c = me["y"], me["c"]
        self.shard, self.whole, self.ring, self.pair = shard, whole, ring, pair
        self.nxt, self.prv = at_y(self.y + 1), at_y(self.y - 1)
        self.partner = {"c": 1 - self.c}

    def block(self, y, c, half=None):
        r = lax.rem(y + 8, 4) * 2 + c
        return self.whole.at[r] if half is None else self.whole.at[r, half]

    MOVES = (("n", 0, 0), ("p", 0, 1), ("n", 0, 1), ("p", 0, 0), ("n", 1, 0), ("p", 1, 1))

    def send(self, k):
        way, hops, half = self.MOVES[k]
        owner = self.y - hops if way == "n" else self.y + hops
        device = self.nxt if way == "n" else self.prv
        spot = self.block(owner, self.c, half)
        return to(spot, spot, self.ring, k, device)

    def landed(self, k):
        way, hops, half = self.MOVES[k]
        owner = self.y - 1 - hops if way == "n" else self.y + 1 + hops
        return owner, half

    def wait(self, k):
        owner, half = self.landed(k)
        spot = self.block(owner, self.c, half)
        to(spot, spot, self.ring, k, self.nxt).wait_recv()

    def give(self, k):
        if k == 6:
            spot = self.block(self.y, self.c)
            return to(spot, spot, self.pair, 6, self.partner)
        owner, half = self.landed(k)
        spot = self.block(owner, self.c, half)
        return to(spot, spot, self.pair, k, self.partner)

    def taken(self, k):
        if k == 6:
            spot = self.block(self.y, 1 - self.c)
        else:
            owner, half = self.landed(k)
            spot = self.block(owner, 1 - self.c, half)
        to(spot, spot, self.pair, k, self.partner).wait_recv()


class Chain:
    def __init__(self, whole, rows, out1, mate1, out2, mate2):
        me = here()
        self.zh, self.zl = me["zh"], me["zl"]
        z = self.zh * 2 + self.zl
        self.away = 2 * self.zl - 1
        self.out, self.mate = at_z(z + self.away), at_z(z - self.away)
        self.whole, self.sems = whole, (out1, mate1, out2, mate2)
        self.rows = rows

    def move(self, kind, slot, k, quarter, device):
        q = lax.rem(quarter + 8, 4)
        spot = self.whole.at[k, ds(q * self.rows, self.rows)]
        return to(spot, spot, self.sems[kind], slot, device)

    def out1(self, k):
        return self.move(0, k, k, self.zh, self.out)

    def mate1(self, k):
        return self.move(1, k, k, self.zh + self.away, self.mate)

    def out2(self, j):
        return self.move(2, j, 2 * j + 1 - self.zl, self.zh - self.away, self.out)

    def mate2(self, j):
        return self.move(3, j, 2 * j + self.zl, self.zh + 2 * self.away, self.mate)

    def got_out1(self, k):
        self.move(0, k, k, self.zh + self.away, self.out).wait_recv()

    def got_mate1(self, k):
        self.move(1, k, k, self.zh - self.away, self.out).wait_recv()

    def got_out2(self, j):
        self.move(2, j, 2 * j + self.zl, self.zh + 2 * self.away, self.out).wait_recv()

    def got_mate2(self, j):
        self.move(3, j, 2 * j + 1 - self.zl, self.zh - 2 * self.away, self.out).wait_recv()

    def pair(self, j):
        for k in (2 * j, 2 * j + 1):
            self.got_out1(k)
            self.mate1(k).start()

        @pl.when(j > 0)
        def _():
            self.back(j - 1)

    def back(self, j):
        self.got_mate1(2 * j)
        self.got_mate1(2 * j + 1)
        self.out2(j).start()

    def second(self, j):
        self.got_out2(j)
        self.mate2(j).start()

    def finish(self):
        @pl.loop(0, CHUNKS // 2)
        def _(j):
            for k in (2 * j, 2 * j + 1):
                self.out1(k).wait_send()
                self.mate1(k).wait_send()
            self.out2(j).wait_send()
            self.mate2(j).wait_send()


STATS = 7


def merge(first, second):
    out = []
    for peak, sums in ((0, (1, 2)), (3, (4,)), (5, (6,))):
        top = jnp.maximum(first[peak], second[peak])
        a, b = jnp.exp(first[peak] - top), jnp.exp(second[peak] - top)
        out.append(top)
        for k in sums:
            out.append(first[k] * a + second[k] * b)
    return out


def lines(block):
    return [block[k : k + 1, :] for k in range(STATS)]


def folded(ref, count):
    parts = [lines(ref[k]) for k in range(count)]
    while len(parts) > 1:
        parts = [merge(parts[k], parts[k + 1]) for k in range(0, len(parts), 2)]
    return parts[0]


class Exchange:
    def __init__(self, near, far, xs, zs):
        me = here()
        self.x, self.z = me["x"], me["zh"] * 2 + me["zl"]
        self.xs_of = [at_x(self.x + k) for k in range(1, 4)]
        self.zs_of = [at_z(self.z + k) for k in range(1, 8)]
        self.near, self.far, self.xs, self.zs = near, far, xs, zs

    def run(self, mine, out):
        x, z, near, far = self.x, self.z, self.near, self.far
        near[x] = mine[...]
        sends = [to(near.at[x], near.at[x], self.xs, k, device) for k, device in enumerate(self.xs_of)]
        for copy in sends:
            copy.start()
        for k in range(3):
            spot = near.at[lax.rem(x + 3 - k, 4)]
            to(spot, spot, self.xs, k, self.xs_of[0]).wait_recv()
        for k, line in enumerate(folded(near, 4)):
            far[z, k : k + 1, :] = line
        more = [to(far.at[z], far.at[z], self.zs, k, device) for k, device in enumerate(self.zs_of)]
        for copy in more:
            copy.start()
        for k in range(7):
            spot = far.at[lax.rem(z + 7 - k, 8)]
            to(spot, spot, self.zs, k, self.zs_of[0]).wait_recv()
        for k, line in enumerate(folded(far, 8)):
            out[k : k + 1, :] = line
        out[STATS:, :] = mine[STATS:, :]
        for copy in sends + more:
            copy.wait_send()


class Scatter4:
    def __init__(self, index, nxt, prv, own, bufs, temps, sems):
        self.i, self.nxt, self.prv, self.own = index, nxt, prv, own
        self.bufs, self.temps, self.sems = bufs, temps, sems

    def move(self, k, src, device):
        return to(src, self.bufs.at[k], self.sems, k, device)

    def send(self, k):
        i, nxt, prv = self.i, self.nxt, self.prv
        if k >= 4:
            return self.move(k, self.temps.at[k - 4], (nxt, prv)[k - 4])
        target, side, device = ((i + 2, 0, nxt), (i + 2, 1, prv), (i + 1, 1, nxt), (i - 1, 0, prv))[k]
        return self.move(k, self.own(target, side), device)

    def start(self):
        for k in range(4):
            self.send(k).start()

    def arrived(self, k):
        self.move(k, self.bufs.at[k], self.nxt).wait_recv()

    def middle(self):
        self.arrived(0)
        self.temps[0] = self.own(self.i + 1, 0)[...] + self.bufs[0]
        self.send(4).start()
        self.arrived(1)
        self.temps[1] = self.own(self.i - 1, 1)[...] + self.bufs[1]
        self.send(5).start()

    def last(self, put):
        for k in (2, 3, 4, 5):
            self.arrived(k)
        put(0, self.own(self.i, 0)[...] + self.bufs[3] + self.bufs[4])
        put(1, self.own(self.i, 1)[...] + self.bufs[2] + self.bufs[5])

    def finish(self):
        for k in range(6):
            self.send(k).wait_send()


class Scatter8:
    def __init__(self, index, nxt, prv, own, bufs, temps, up, down):
        self.i, self.nxt, self.prv, self.own = index, nxt, prv, own
        self.bufs, self.temps, self.up, self.down = bufs, temps, up, down
        self.n = bufs.shape[2]
        self.halves = (slice(0, self.n // 2), slice(self.n // 2, self.n))

    def up_move(self, s):
        if s == 0:
            src, dst = self.own(self.i + 4).at[self.halves[0]], self.bufs.at[0, 0, self.halves[0]]
        else:
            src, dst = self.temps.at[0, s - 1], self.bufs.at[0, s]
        return to(src, dst, self.up, s, self.nxt)

    def down_move(self, s):
        if s == 0:
            src, dst = self.own(self.i - 4).at[self.halves[1]], self.bufs.at[1, 0, self.halves[1]]
        else:
            src, dst = self.temps.at[1, s - 1], self.bufs.at[1, s]
        return to(src, dst, self.down, s, self.prv)

    def start(self):
        self.up_move(0).start()
        self.down_move(0).start()

    def step(self, s):
        a, b = self.halves
        self.up_move(s - 1).wait_recv()
        mine = self.own(self.i + 4 - s)
        if s == 1:
            self.temps[0, 0, a] = mine[a] + self.bufs[0, 0, a]
            self.temps[0, 0, b] = mine[b]
        else:
            self.temps[0, s - 1] = mine[...] + self.bufs[0, s - 1]
        self.up_move(s).start()
        self.down_move(s - 1).wait_recv()
        mine = self.own(self.i - 4 + s)
        if s == 1:
            self.temps[1, 0, a] = mine[a]
            self.temps[1, 0, b] = mine[b] + self.bufs[1, 0, b]
        else:
            self.temps[1, s - 1] = mine[...] + self.bufs[1, s - 1]
        self.down_move(s).start()

    def last(self):
        self.up_move(3).wait_recv()
        self.down_move(3).wait_recv()
        return self.own(self.i)[...] + self.bufs[0, 3] + self.bufs[1, 3]

    def finish(self):
        for s in range(4):
            self.up_move(s).wait_send()
            self.down_move(s).wait_send()


BOTH_MINOR = (((1,), (1,)), ((), ()))


def fused_kernel(
    tau, labels, ht, wt, hs, ws, whole_out, wg_out, hg_out,
    ht_all, wt_all, hs_all, ws_all, lt, ls, local_out, near, far, grad,
    hg, wg_give, pair_buf, y_buf, y_tmp, ux_buf, ux_tmp, uz_own, uz_buf, uz_tmp, vz_buf, vz_tmp, vx_own, vx_buf, vx_tmp,
    own_sem, o1s, o1r, m1s, m1r, o2s, o2r, m2s, m2r, ring_t_s, ring_t_r, ring_s_s, ring_s_r,
    pair_t_s, pair_t_r, pair_s_s, pair_s_r, xs, xr, zs, zr,
    pair_s, pair_r, y_s, y_r, ux_s, ux_r, vx_s, vx_r, uzu_s, uzu_r, uzd_s, uzd_r, vzu_s, vzu_r, vzd_s, vzd_r,
):
    me = here()
    y, c = me["y"], me["c"]
    chain = Chain(ht_all, ht.shape[0], (o1s, o1r), (m1s, m1r), (o2s, o2r), (m2s, m2r))
    teacher = Ring(wt, wt_all, (ring_t_s, ring_t_r), (pair_t_s, pair_t_r))
    student = Ring(ws, ws_all, (ring_s_s, ring_s_r), (pair_s_s, pair_s_r))
    exchange = Exchange(near, far, (xs, xr), (zs, zr))
    wide, tokens, padded = ht_all.shape[2], hs.shape[0], lt.shape[1]
    first = 4 * (y + 3)

    def mine(k):
        chunk = lax.rem(k + first, CHUNKS)
        spot = ht_all.at[k, ds(me["zh"] * ht.shape[0], ht.shape[0])]
        return pltpu.make_async_copy(ht.at[:, ds(chunk * wide, wide)], spot, own_sem.at[k])

    own = []
    for ring in (student, teacher):
        half = ring.shard.shape[1] // 2
        for side in (0, 1):
            src = ring.shard.at[:, side * half : (side + 1) * half]
            own.append(pltpu.make_async_copy(src, ring.block(y, c, side), own_sem.at[CHUNKS + len(own)]))
    states = pltpu.make_async_copy(hs, hs_all.at[pl.ds(0, tokens)], own_sem.at[CHUNKS + 4])

    @pl.loop(0, CHUNKS)
    def _(k):
        mine(k).start()

    for copy in own:
        copy.start()
    states.start()
    ht_all[:, pl.ds(tokens, padded - tokens)] = jnp.zeros((CHUNKS, padded - tokens, wide), jnp.bfloat16)
    hs_all[pl.ds(tokens, padded - tokens)] = jnp.zeros((padded - tokens, hs.shape[1]), jnp.bfloat16)
    greet([teacher.nxt, teacher.prv, teacher.partner] + exchange.xs_of + exchange.zs_of)
    for copy in own:
        copy.wait()
    for k in range(4):
        student.send(k).start()
    for k in range(2):
        teacher.send(k).start()

    @pl.loop(0, CHUNKS)
    def _(k):
        mine(k).wait()
        chain.out1(k).start()

    student.give(6).start()
    teacher.give(6).start()
    states.wait()

    def arrivals(ring):
        for k, onward in ((0, 4), (1, 5), (2, None), (3, None)):
            ring.wait(k)
            if onward is not None:
                ring.send(onward).start()
            ring.give(k).start()

    def block_of(i):
        return lax.rem(i + 2 * (y + 3), 8)

    def student_block(i):
        r = block_of(i)

        @pl.loop(0, padded // 256)
        def _(n):
            tile = ds(n * 256, 256)
            part = lax.dot_general(
                jnp.concatenate([ws_all[r, 0], ws_all[r, 1]], axis=1),
                hs_all[tile, ds(r * ws.shape[1], ws.shape[1])],
                BOTH_MINOR,
                preferred_element_type=jnp.float32,
            )

            @pl.when(i == 0)
            def _():
                ls[:, tile] = part

            @pl.when(i > 0)
            def _():
                ls[:, tile] += part

    def teacher_block(i):
        r = block_of(i)

        @pl.loop(0, padded // 256)
        def _(n):
            tile = ds(n * 256, 256)
            part = lax.dot_general(
                jnp.concatenate([wt_all[r, 0], wt_all[r, 1]], axis=1),
                jnp.concatenate([ht_all[2 * i, tile], ht_all[2 * i + 1, tile]], axis=1),
                BOTH_MINOR,
                preferred_element_type=jnp.float32,
            )

            @pl.when(i == 0)
            def _():
                lt[:, tile] = part

            @pl.when(i > 0)
            def _():
                lt[:, tile] += part

    @pl.loop(0, 3)
    def _(j):
        chain.pair(j)

    arrivals(student)
    for k in range(2, 4):
        teacher.send(k).start()
    for k in (6, 0, 1, 2, 3):
        student.taken(k)

    @pl.loop(3, 6)
    def _(j):
        chain.pair(j)
        student_block(2 * (j - 3))
        student_block(2 * (j - 3) + 1)

    for k in (4, 5):
        student.wait(k)
        student.give(k).start()

    @pl.loop(6, CHUNKS // 2)
    def _(j):
        chain.pair(j)

    chain.back(CHUNKS // 2 - 1)
    for k in (4, 5):
        student.taken(k)
    student_block(6)
    student_block(7)
    @pl.loop(0, padded // 128)
    def _(n):
        tile = ds(n * 128, 128)
        share = 1.0 / tau[:, tile]
        v = ls[:, tile]
        top = jnp.max(v, axis=0, keepdims=True)
        v = v - top
        local_out[3:4, tile] = top * share
        local_out[4:5, tile] = jnp.sum(jnp.exp(v * share), axis=0, keepdims=True)
        local_out[5:6, tile] = top
        local_out[6:7, tile] = jnp.sum(jnp.exp(v), axis=0, keepdims=True)
        local_out[7:8, tile] = tau[:, tile]

    arrivals(teacher)
    for k in (6, 0, 1, 2, 3):
        teacher.taken(k)

    @pl.loop(0, 6)
    def _(i):
        chain.second(i)

        @pl.when(i > 0)
        def _():
            chain.got_mate2(i - 1)
            teacher_block(i - 1)

    chain.second(6)
    chain.second(7)
    for k in (4, 5):
        teacher.wait(k)
        teacher.give(k).start()

    @pl.loop(5, 8)
    def _(i):
        chain.got_mate2(i)

        @pl.when(i == 6)
        def _():
            for k in (4, 5):
                teacher.taken(k)

        teacher_block(i)

    @pl.loop(0, padded // 128)
    def _(n):
        tile = ds(n * 128, 128)
        share = 1.0 / tau[:, tile]
        v = lt[:, tile] * share
        top = jnp.max(v, axis=0, keepdims=True)
        e = jnp.exp(v - top)
        local_out[0:1, tile] = top
        local_out[1:2, tile] = jnp.sum(e, axis=0, keepdims=True)
        local_out[2:3, tile] = jnp.sum(e * (v - ls[:, tile] * share), axis=0, keepdims=True)

    exchange.run(local_out, whole_out)

    vocab = wt.shape[0]
    z, x = exchange.z, exchange.x
    first_entry = (z * 4 + x) * vocab

    @pl.loop(0, padded // 128)
    def _(n):
        tile = ds(n * 128, 128)
        heat = tau[:, tile]
        share = 1.0 / heat
        lse_t, lse_s, lse_c = (
            whole_out[p : p + 1, tile] + jnp.log(whole_out[q : q + 1, tile]) for p, q in ((0, 1), (3, 4), (5, 6))
        )
        s = ls[:, tile]
        prob_t = jnp.exp(lt[:, tile] * share - lse_t)
        prob_s = jnp.exp(s * share - lse_s)
        prob_c = jnp.exp(s - lse_c)
        entries = first_entry + lax.broadcasted_iota(jnp.int32, s.shape, 0)
        hot = jnp.where(entries == labels[:, tile], 1.0, 0.0)
        grad[:, tile] = (heat * (prob_s - prob_t) + prob_c - hot).astype(jnp.bfloat16)

    partner, x_nxt, x_prv, z_nxt, z_prv = student.partner, at_x(x + 1), at_x(x - 1), at_z(z + 1), at_z(z - 1)
    feats = ws.shape[1]
    half = feats // 2

    ux = Scatter4(x, x_nxt, x_prv, lambda t, side: hg.at[:, lax.rem(t + 8, 4), 0, side], ux_buf, ux_tmp, (ux_s, ux_r))
    vz = Scatter8(z, z_nxt, z_prv, lambda t: hg.at[lax.rem(t + 16, 8), :, 1], vz_buf, vz_tmp, (vzu_s, vzu_r), (vzd_s, vzd_r))
    uz = Scatter8(z, z_nxt, z_prv, lambda t: uz_own.at[lax.rem(t + 16, 8)], uz_buf, uz_tmp, (uzu_s, uzu_r), (uzd_s, uzd_r))
    vx = Scatter4(x, x_nxt, x_prv, lambda t, side: vx_own.at[lax.rem(t + 8, 4), side], vx_buf, vx_tmp, (vx_s, vx_r))
    wy = Scatter4(
        y, student.nxt, student.prv,
        lambda t, side: pair_buf.at[lax.rem(t + 8, 4), :, side * half : (side + 1) * half], y_buf, y_tmp, (y_s, y_r),
    )

    def hidden_block(i):
        away = jnp.where(lax.rem(i, 2) == 1, 4 - (i + 1) // 2, i // 2 - 4)
        t = lax.rem(z + 16 + away, 8)
        value = lax.dot_general(
            jnp.concatenate([ws_all[t, 0], ws_all[t, 1]], axis=1),
            grad[:, :tokens],
            (((0,), (0,)), ((), ())),
            preferred_element_type=jnp.float32,
        )
        hg[t] = value.reshape(hg.shape[1:])

    def weight_block(r):
        return lax.dot_general(
            grad[...], hs_all[:, ds(r * feats, feats)], (((1,), (0,)), ((), ())), preferred_element_type=jnp.float32
        )

    def given(n):
        k = lax.rem(y + 2 + 3 * n, 4)
        return k, to(wg_give.at[n], pair_buf.at[k], (pair_s, pair_r), n, partner)

    def put_ux(side, value):
        uz_own[:, side] = value

    def put_vx(side, value):
        hg_out[1, side] = value

    def put_wy(side, value):
        wg_out[:, side * half : (side + 1) * half] = value

    hidden_block(jnp.int32(0))
    vz.start()

    @pl.loop(1, 8)
    def _(i):
        hidden_block(i)

    ux.start()

    @pl.loop(0, 4)
    def _(n):
        k, copy = given(n)
        wg_give[n] = weight_block(2 * k + 1 - c)
        copy.start()

    vz.step(1)

    @pl.loop(0, 4)
    def _(n):
        k, copy = given(n)
        value = weight_block(2 * k + c)
        copy.wait_recv()
        pair_buf[k] = pair_buf[k] + value
        for at, moves in ((0, (0, 1)), (1, (2,)), (3, (3,))):

            @pl.when(n == at)
            def _():
                for number in moves:
                    wy.send(number).start()

    ux.middle()
    vz.step(2)
    wy.middle()
    vz.step(3)
    ux.last(put_ux)
    uz.start()
    uz.step(1)
    vx_own[...] = vz.last()
    vx.start()
    uz.step(2)
    vx.middle()
    uz.step(3)
    wy.last(put_wy)
    vx.last(put_vx)
    hg_out[0] = uz.last()

    @pl.loop(0, 4)
    def _(n):
        given(n)[1].wait_send()

    for ring in (ux, vz, uz, vx, wy):
        ring.finish()
    for ring in (student, teacher):
        for k in range(6):
            ring.send(k).wait_send()
        for k in range(7):
            ring.give(k).wait_send()
    chain.finish()


def fused(tau, labels, ht, wt, hs, ws):
    dma, b16, f32 = pltpu.SemaphoreType.DMA, jnp.bfloat16, jnp.float32
    vocab, tokens, padded, feats = wt.shape[0], hs.shape[0], tau.shape[1], ws.shape[1]
    tile = (feats // 16, tokens)
    space, vmem = pl.BlockSpec(memory_space=pl.ANY), pl.BlockSpec(memory_space=pltpu.VMEM)
    pairs = lambda *shape: [dma(shape), dma(shape)]
    wide = lambda *shape: pltpu.VMEM(shape, f32)
    narrow = lambda *shape: pltpu.VMEM(shape, b16)
    return pl.pallas_call(
        fused_kernel,
        out_shape=[
            jax.ShapeDtypeStruct((8, padded), f32),
            jax.ShapeDtypeStruct((vocab, feats), f32),
            jax.ShapeDtypeStruct((2, 2, *tile), f32),
        ],
        in_specs=[vmem] * 2 + [space] * 4,
        out_specs=[vmem] * 3,
        scratch_shapes=[
            narrow(CHUNKS, padded, ht.shape[1] // CHUNKS),
            narrow(8, 2, vocab, wt.shape[1] // 2),
            narrow(padded, hs.shape[1]),
            narrow(8, 2, vocab, feats // 2),
            wide(vocab, padded), wide(vocab, padded), wide(8, padded), wide(4, 8, padded), wide(8, 8, padded),
            narrow(vocab, padded),
            wide(8, 4, 2, 2, *tile), wide(4, vocab, feats), wide(4, vocab, feats),
            wide(6, vocab, feats // 2), wide(2, vocab, feats // 2),
            wide(6, 8, *tile), wide(2, 8, *tile),
            wide(8, 2, *tile), wide(2, 4, 2, *tile), wide(2, 3, 2, *tile),
            wide(2, 4, 4, 2, *tile), wide(2, 3, 4, 2, *tile),
            wide(4, 2, *tile), wide(6, *tile), wide(2, *tile),
            dma((CHUNKS + 5,)),
        ]
        + pairs(CHUNKS) * 2
        + pairs(CHUNKS // 2) * 2
        + pairs(6) * 2
        + pairs(7) * 2
        + pairs(3)
        + pairs(7)
        + pairs(4)
        + pairs(6) * 3
        + pairs(4) * 4,
        compiler_params=pltpu.CompilerParams(collective_id=0, has_side_effects=True, vmem_limit_bytes=67043328),
        name="fused",
    )(tau, labels, ht, wt, hs, ws)


def heat_scalar(corruption_kinds, heat_per_kind):
    picked = (corruption_kinds[:, None] == jnp.arange(heat_per_kind.shape[0], dtype=jnp.int32)[None, :]).astype(jnp.float32)
    return jnp.sum(picked * heat_per_kind[None, :], axis=1)


def local(ht, wt, hs, ws, labels, kinds, heats):
    tokens = hs.shape[0]
    padded = -(-tokens // 256) * 256
    tau = jnp.pad(heat_scalar(kinds, heats), (0, padded - tokens), constant_values=1.0)[None, :]
    labels = jnp.pad(labels, (0, padded - tokens), constant_values=-1)[None, :]
    whole, wg, hg = fused(tau, labels, ht, wt.T, hs, ws.T)
    peak_t, sum_t, cross, peak_s, sum_s = (whole[k, :tokens] for k in range(5))
    divergence = cross / sum_t - peak_t - jnp.log(sum_t) + peak_s + jnp.log(sum_s)
    return divergence, hg.reshape(-1, tokens).T, wg.T


def solution(mesh):
    finer = Mesh(mesh.devices.reshape(mesh.shape["grp"], 2, 4, 4, 2), AXES)
    return jax.shard_map(
        local,
        mesh=finer,
        in_specs=(
            P((*ROWS, "zh"), None),
            P(ROWS, GRP_VOCAB),
            P(ROWS, None),
            P(ROWS, GRP_VOCAB),
            P(ROWS),
            P(ROWS),
            P(),
        ),
        out_specs=(P(ROWS), P(ROWS, GRP_VOCAB), P(ROWS, GRP_VOCAB)),
        check_vma=False,
    )
```

```python
import functools

import jax
import jax.numpy as jnp
from jax import lax
from jax.experimental import pallas as pl
from jax.experimental.pallas import tpu as pltpu
from jax.sharding import Mesh
from jax.sharding import PartitionSpec as P

AXES = ("zh", "zl", "x", "y", "c")
GRP_VOCAB = ("zh", "zl", "x")
ROWS = ("y", "c")
CHUNKS = 16
MESH = pl.DeviceIdType.MESH


def here():
    return {name: lax.axis_index(name) for name in AXES}


def at_z(z):
    z = lax.rem(z + 16, 8)
    return {"zh": z // 2, "zl": lax.rem(z, 2)}


def at_x(x):
    return {"x": lax.rem(x + 8, 4)}


def at_y(y):
    return {"y": lax.rem(y + 8, 4)}


def to(src, dst, sems, k, device):
    send, recv = sems
    return pltpu.make_async_remote_copy(
        src_ref=src,
        dst_ref=dst,
        send_sem=send.at[k],
        recv_sem=recv.at[k],
        device_id=device,
        device_id_type=MESH,
    )


def greet(devices):
    barrier = pltpu.get_barrier_semaphore()
    for device in devices:
        pl.semaphore_signal(barrier, inc=1, device_id=device, device_id_type=MESH)
    pl.semaphore_wait(barrier, len(devices))


def ds(start, size):
    return pl.ds(pl.multiple_of(start, size), size)


class Ring:
    def __init__(self, shard, whole, ring, pair):
        me = here()
        self.y, self.c = me["y"], me["c"]
        self.shard, self.whole, self.ring, self.pair = shard, whole, ring, pair
        self.nxt, self.prv = at_y(self.y + 1), at_y(self.y - 1)
        self.partner = {"c": 1 - self.c}

    def block(self, y, c, half=None):
        r = lax.rem(y + 8, 4) * 2 + c
        return self.whole.at[r] if half is None else self.whole.at[r, half]

    MOVES = (("n", 0, 0), ("p", 0, 1), ("n", 0, 1), ("p", 0, 0), ("n", 1, 0), ("p", 1, 1))

    def send(self, k):
        way, hops, half = self.MOVES[k]
        owner = self.y - hops if way == "n" else self.y + hops
        device = self.nxt if way == "n" else self.prv
        spot = self.block(owner, self.c, half)
        return to(spot, spot, self.ring, k, device)

    def landed(self, k):
        way, hops, half = self.MOVES[k]
        owner = self.y - 1 - hops if way == "n" else self.y + 1 + hops
        return owner, half

    def wait(self, k):
        owner, half = self.landed(k)
        spot = self.block(owner, self.c, half)
        to(spot, spot, self.ring, k, self.nxt).wait_recv()

    def give(self, k):
        if k == 6:
            spot = self.block(self.y, self.c)
            return to(spot, spot, self.pair, 6, self.partner)
        owner, half = self.landed(k)
        spot = self.block(owner, self.c, half)
        return to(spot, spot, self.pair, k, self.partner)

    def taken(self, k):
        if k == 6:
            spot = self.block(self.y, 1 - self.c)
        else:
            owner, half = self.landed(k)
            spot = self.block(owner, 1 - self.c, half)
        to(spot, spot, self.pair, k, self.partner).wait_recv()


class Chain:
    def __init__(self, whole, rows, out1, mate1, out2, mate2):
        me = here()
        self.zh, self.zl = me["zh"], me["zl"]
        z = self.zh * 2 + self.zl
        self.away = 2 * self.zl - 1
        self.out, self.mate = at_z(z + self.away), at_z(z - self.away)
        self.whole, self.sems = whole, (out1, mate1, out2, mate2)
        self.rows = rows

    def move(self, kind, slot, k, quarter, device):
        q = lax.rem(quarter + 8, 4)
        spot = self.whole.at[k, ds(q * self.rows, self.rows)]
        return to(spot, spot, self.sems[kind], slot, device)

    def out1(self, k):
        return self.move(0, k, k, self.zh, self.out)

    def mate1(self, k):
        return self.move(1, k, k, self.zh + self.away, self.mate)

    def out2(self, j):
        return self.move(2, j, 2 * j + 1 - self.zl, self.zh - self.away, self.out)

    def mate2(self, j):
        return self.move(3, j, 2 * j + self.zl, self.zh + 2 * self.away, self.mate)

    def got_out1(self, k):
        self.move(0, k, k, self.zh + self.away, self.out).wait_recv()

    def got_mate1(self, k):
        self.move(1, k, k, self.zh - self.away, self.out).wait_recv()

    def got_out2(self, j):
        self.move(2, j, 2 * j + self.zl, self.zh + 2 * self.away, self.out).wait_recv()

    def got_mate2(self, j):
        self.move(3, j, 2 * j + 1 - self.zl, self.zh - 2 * self.away, self.out).wait_recv()

    def pair(self, j):
        for k in (2 * j, 2 * j + 1):
            self.got_out1(k)
            self.mate1(k).start()

        @pl.when(j > 0)
        def _():
            self.back(j - 1)

    def back(self, j):
        self.got_mate1(2 * j)
        self.got_mate1(2 * j + 1)
        self.out2(j).start()

    def second(self, j):
        self.got_out2(j)
        self.mate2(j).start()

    def finish(self):
        @pl.loop(0, CHUNKS // 2)
        def _(j):
            for k in (2 * j, 2 * j + 1):
                self.out1(k).wait_send()
                self.mate1(k).wait_send()
            self.out2(j).wait_send()
            self.mate2(j).wait_send()


STATS = 7


def merge(first, second):
    out = []
    for peak, sums in ((0, (1, 2)), (3, (4,)), (5, (6,))):
        top = jnp.maximum(first[peak], second[peak])
        a, b = jnp.exp(first[peak] - top), jnp.exp(second[peak] - top)
        out.append(top)
        for k in sums:
            out.append(first[k] * a + second[k] * b)
    return out


def lines(block):
    return [block[k : k + 1, :] for k in range(STATS)]


def folded(ref, count):
    parts = [lines(ref[k]) for k in range(count)]
    while len(parts) > 1:
        parts = [merge(parts[k], parts[k + 1]) for k in range(0, len(parts), 2)]
    return parts[0]


class Exchange:
    def __init__(self, near, far, xs, zs):
        me = here()
        self.x, self.z = me["x"], me["zh"] * 2 + me["zl"]
        self.xs_of = [at_x(self.x + k) for k in range(1, 4)]
        self.zs_of = [at_z(self.z + k) for k in range(1, 8)]
        self.near, self.far, self.xs, self.zs = near, far, xs, zs

    def run(self, mine, out):
        x, z, near, far = self.x, self.z, self.near, self.far
        near[x] = mine[...]
        sends = [to(near.at[x], near.at[x], self.xs, k, device) for k, device in enumerate(self.xs_of)]
        for copy in sends:
            copy.start()
        for k in range(3):
            spot = near.at[lax.rem(x + 3 - k, 4)]
            to(spot, spot, self.xs, k, self.xs_of[0]).wait_recv()
        for k, line in enumerate(folded(near, 4)):
            far[z, k : k + 1, :] = line
        more = [to(far.at[z], far.at[z], self.zs, k, device) for k, device in enumerate(self.zs_of)]
        for copy in more:
            copy.start()
        for k in range(7):
            spot = far.at[lax.rem(z + 7 - k, 8)]
            to(spot, spot, self.zs, k, self.zs_of[0]).wait_recv()
        for k, line in enumerate(folded(far, 8)):
            out[k : k + 1, :] = line
        out[STATS:, :] = mine[STATS:, :]
        for copy in sends + more:
            copy.wait_send()


class Packets:
    def __init__(self, stage, bufs, stage_scale, scales, sems, scale_sems):
        self.stage, self.bufs, self.sems = stage, bufs, sems
        self.stage_scale, self.scales, self.scale_sems = stage_scale, scales, scale_sems

    def copies(self, k, device, part):
        pick = (k,) if part is None else (k, part)
        return (
            to(self.stage.at[pick], self.bufs.at[pick], self.sems, k, device),
            to(self.stage_scale.at[k], self.scales.at[k], self.scale_sems, k, device),
        )

    def send(self, k, value, device, part=None):
        top = jnp.max(jnp.abs(value), axis=tuple(range(value.ndim - 2)), keepdims=True)
        top = jnp.max(top.reshape(top.shape[-2:]), axis=0, keepdims=True)
        coded = jnp.round(value * (32767.0 / jnp.maximum(top, 1e-30))).astype(jnp.int16)
        self.stage[(k,) if part is None else (k, part)] = coded
        self.stage_scale[k] = top * (1.0 / 32767.0)
        for copy in self.copies(k, device, part):
            copy.start()

    def take(self, k, device, part=None):
        for copy in self.copies(k, device, part):
            copy.wait_recv()
        return self.bufs[(k,) if part is None else (k, part)].astype(jnp.float32) * self.scales[k]

    def sent(self, k, device, part=None):
        for copy in self.copies(k, device, part):
            copy.wait_send()


class Scatter4:
    def __init__(self, index, nxt, prv, own, *packets):
        self.i, self.nxt, self.prv, self.own = index, nxt, prv, own
        self.packets = Packets(*packets)

    def send(self, k):
        i, nxt, prv = self.i, self.nxt, self.prv
        target, side, device = ((i + 2, 0, nxt), (i + 2, 1, prv), (i + 1, 1, nxt), (i - 1, 0, prv))[k]
        self.packets.send(k, self.own(target, side)[...], device)

    def start(self):
        for k in range(4):
            self.send(k)

    def arrived(self, k):
        return self.packets.take(k, self.nxt)

    def middle(self):
        self.packets.send(4, self.own(self.i + 1, 0)[...] + self.arrived(0), self.nxt)
        self.packets.send(5, self.own(self.i - 1, 1)[...] + self.arrived(1), self.prv)

    def last(self, put):
        put(0, self.own(self.i, 0)[...] + self.arrived(3) + self.arrived(4))
        put(1, self.own(self.i, 1)[...] + self.arrived(2) + self.arrived(5))

    def finish(self):
        for k in range(6):
            self.packets.sent(k, self.nxt)


class Scatter8:
    def __init__(self, index, nxt, prv, own, *packets):
        self.i, self.nxt, self.prv, self.own = index, nxt, prv, own
        self.packets = Packets(*packets)
        n = self.packets.bufs.shape[1]
        self.halves = (pl.ds(0, n // 2), pl.ds(n // 2, n // 2))

    def start(self):
        a, b = self.halves
        self.packets.send(0, self.own(self.i + 4)[a], self.nxt, a)
        self.packets.send(4, self.own(self.i - 4)[b], self.prv, b)

    def step(self, s):
        a, b = self.halves
        up, down = self.own(self.i + 4 - s), self.own(self.i - 4 + s)
        if s == 1:
            value = jnp.concatenate([up[a] + self.packets.take(0, self.nxt, a), up[b]])
            self.packets.send(1, value, self.nxt)
            value = jnp.concatenate([down[a], down[b] + self.packets.take(4, self.prv, b)])
            self.packets.send(5, value, self.prv)
        else:
            self.packets.send(s, up[...] + self.packets.take(s - 1, self.nxt), self.nxt)
            self.packets.send(4 + s, down[...] + self.packets.take(3 + s, self.prv), self.prv)

    def last(self):
        return self.own(self.i)[...] + self.packets.take(3, self.nxt) + self.packets.take(7, self.prv)

    def finish(self):
        a, b = self.halves
        for k in range(8):
            self.packets.sent(k, self.nxt, {0: a, 4: b}.get(k))


BOTH_MINOR = (((1,), (1,)), ((), ()))


def fused_kernel(
    tau, labels, ht, wt, hs, ws, whole_out, wg_out, hg_out,
    ht_all, wt_all, hs_all, ws_all, lt, ls, local_out, near, far, grad,
    hg, wg_give, pair_buf, uz_own, vx_own,
    y_1, y_2, y_3, y_4, ux_1, ux_2, ux_3, ux_4, vx_1, vx_2, vx_3, vx_4, uz_1, uz_2, uz_3, uz_4, vz_1, vz_2, vz_3, vz_4,
    own_sem, o1s, o1r, m1s, m1r, o2s, o2r, m2s, m2r, ring_t_s, ring_t_r, ring_s_s, ring_s_r,
    pair_t_s, pair_t_r, pair_s_s, pair_s_r, xs, xr, zs, zr,
    pair_s, pair_r, y_s, y_r, ys_s, ys_r, ux_s, ux_r, uxs_s, uxs_r, vx_s, vx_r, vxs_s, vxs_r,
    uz_s, uz_r, uzs_s, uzs_r, vz_s, vz_r, vzs_s, vzs_r,
):
    me = here()
    y, c = me["y"], me["c"]
    chain = Chain(ht_all, ht.shape[0], (o1s, o1r), (m1s, m1r), (o2s, o2r), (m2s, m2r))
    teacher = Ring(wt, wt_all, (ring_t_s, ring_t_r), (pair_t_s, pair_t_r))
    student = Ring(ws, ws_all, (ring_s_s, ring_s_r), (pair_s_s, pair_s_r))
    exchange = Exchange(near, far, (xs, xr), (zs, zr))
    wide, tokens, padded = ht_all.shape[2], hs.shape[0], lt.shape[1]
    first = 4 * (y + 3)

    def mine(k):
        chunk = lax.rem(k + first, CHUNKS)
        spot = ht_all.at[k, ds(me["zh"] * ht.shape[0], ht.shape[0])]
        return pltpu.make_async_copy(ht.at[:, ds(chunk * wide, wide)], spot, own_sem.at[k])

    own = []
    for ring in (student, teacher):
        half = ring.shard.shape[1] // 2
        for side in (0, 1):
            src = ring.shard.at[:, side * half : (side + 1) * half]
            own.append(pltpu.make_async_copy(src, ring.block(y, c, side), own_sem.at[CHUNKS + len(own)]))
    states = pltpu.make_async_copy(hs, hs_all.at[pl.ds(0, tokens)], own_sem.at[CHUNKS + 4])

    @pl.loop(0, CHUNKS)
    def _(k):
        mine(k).start()

    for copy in own:
        copy.start()
    states.start()
    ht_all[:, pl.ds(tokens, padded - tokens)] = jnp.zeros((CHUNKS, padded - tokens, wide), jnp.bfloat16)
    hs_all[pl.ds(tokens, padded - tokens)] = jnp.zeros((padded - tokens, hs.shape[1]), jnp.bfloat16)
    greet([teacher.nxt, teacher.prv, teacher.partner] + exchange.xs_of + exchange.zs_of)
    for copy in own:
        copy.wait()
    for k in range(4):
        student.send(k).start()
    for k in range(2):
        teacher.send(k).start()

    @pl.loop(0, CHUNKS)
    def _(k):
        mine(k).wait()
        chain.out1(k).start()

    student.give(6).start()
    teacher.give(6).start()
    states.wait()

    def arrivals(ring):
        for k, onward in ((0, 4), (1, 5), (2, None), (3, None)):
            ring.wait(k)
            if onward is not None:
                ring.send(onward).start()
            ring.give(k).start()

    def block_of(i):
        return lax.rem(i + 2 * (y + 3), 8)

    def student_block(i):
        r = block_of(i)

        @pl.loop(0, padded // 256)
        def _(n):
            tile = ds(n * 256, 256)
            part = lax.dot_general(
                jnp.concatenate([ws_all[r, 0], ws_all[r, 1]], axis=1),
                hs_all[tile, ds(r * ws.shape[1], ws.shape[1])],
                BOTH_MINOR,
                preferred_element_type=jnp.float32,
            )

            @pl.when(i == 0)
            def _():
                ls[:, tile] = part

            @pl.when(i > 0)
            def _():
                ls[:, tile] += part

    def teacher_block(i):
        r = block_of(i)

        @pl.loop(0, padded // 256)
        def _(n):
            tile = ds(n * 256, 256)
            part = lax.dot_general(
                jnp.concatenate([wt_all[r, 0], wt_all[r, 1]], axis=1),
                jnp.concatenate([ht_all[2 * i, tile], ht_all[2 * i + 1, tile]], axis=1),
                BOTH_MINOR,
                preferred_element_type=jnp.float32,
            )

            @pl.when(i == 0)
            def _():
                lt[:, tile] = part

            @pl.when(i > 0)
            def _():
                lt[:, tile] += part

    @pl.loop(0, 3)
    def _(j):
        chain.pair(j)

    arrivals(student)
    for k in range(2, 4):
        teacher.send(k).start()
    for k in (6, 0, 1, 2, 3):
        student.taken(k)

    @pl.loop(3, 6)
    def _(j):
        chain.pair(j)
        student_block(2 * (j - 3))
        student_block(2 * (j - 3) + 1)

    for k in (4, 5):
        student.wait(k)
        student.give(k).start()

    @pl.loop(6, CHUNKS // 2)
    def _(j):
        chain.pair(j)

    chain.back(CHUNKS // 2 - 1)
    for k in (4, 5):
        student.taken(k)
    student_block(6)
    student_block(7)
    @pl.loop(0, padded // 128)
    def _(n):
        tile = ds(n * 128, 128)
        share = 1.0 / tau[:, tile]
        v = ls[:, tile]
        top = jnp.max(v, axis=0, keepdims=True)
        v = v - top
        local_out[3:4, tile] = top * share
        local_out[4:5, tile] = jnp.sum(jnp.exp(v * share), axis=0, keepdims=True)
        local_out[5:6, tile] = top
        local_out[6:7, tile] = jnp.sum(jnp.exp(v), axis=0, keepdims=True)
        local_out[7:8, tile] = tau[:, tile]

    arrivals(teacher)
    for k in (6, 0, 1, 2, 3):
        teacher.taken(k)

    @pl.loop(0, 6)
    def _(i):
        chain.second(i)

        @pl.when(i > 0)
        def _():
            chain.got_mate2(i - 1)
            teacher_block(i - 1)

    chain.second(6)
    chain.second(7)
    for k in (4, 5):
        teacher.wait(k)
        teacher.give(k).start()

    @pl.loop(5, 8)
    def _(i):
        chain.got_mate2(i)

        @pl.when(i == 6)
        def _():
            for k in (4, 5):
                teacher.taken(k)

        teacher_block(i)

    @pl.loop(0, padded // 128)
    def _(n):
        tile = ds(n * 128, 128)
        share = 1.0 / tau[:, tile]
        v = lt[:, tile] * share
        top = jnp.max(v, axis=0, keepdims=True)
        e = jnp.exp(v - top)
        local_out[0:1, tile] = top
        local_out[1:2, tile] = jnp.sum(e, axis=0, keepdims=True)
        local_out[2:3, tile] = jnp.sum(e * (v - ls[:, tile] * share), axis=0, keepdims=True)

    exchange.run(local_out, whole_out)

    vocab = wt.shape[0]
    z, x = exchange.z, exchange.x
    first_entry = (z * 4 + x) * vocab

    @pl.loop(0, padded // 128)
    def _(n):
        tile = ds(n * 128, 128)
        heat = tau[:, tile]
        share = 1.0 / heat
        lse_t, lse_s, lse_c = (
            whole_out[p : p + 1, tile] + jnp.log(whole_out[q : q + 1, tile]) for p, q in ((0, 1), (3, 4), (5, 6))
        )
        s = ls[:, tile]
        prob_t = jnp.exp(lt[:, tile] * share - lse_t)
        prob_s = jnp.exp(s * share - lse_s)
        prob_c = jnp.exp(s - lse_c)
        entries = first_entry + lax.broadcasted_iota(jnp.int32, s.shape, 0)
        hot = jnp.where(entries == labels[:, tile], 1.0, 0.0)
        grad[:, tile] = (heat * (prob_s - prob_t) + prob_c - hot).astype(jnp.bfloat16)

    partner, x_nxt, x_prv, z_nxt, z_prv = student.partner, at_x(x + 1), at_x(x - 1), at_z(z + 1), at_z(z - 1)
    feats = ws.shape[1]
    half = feats // 2

    ux = Scatter4(x, x_nxt, x_prv, lambda t, side: hg.at[:, lax.rem(t + 8, 4), 0, side], ux_1, ux_2, ux_3, ux_4, (ux_s, ux_r), (uxs_s, uxs_r))
    vz = Scatter8(z, z_nxt, z_prv, lambda t: hg.at[lax.rem(t + 16, 8), :, 1], vz_1, vz_2, vz_3, vz_4, (vz_s, vz_r), (vzs_s, vzs_r))
    uz = Scatter8(z, z_nxt, z_prv, lambda t: uz_own.at[lax.rem(t + 16, 8)], uz_1, uz_2, uz_3, uz_4, (uz_s, uz_r), (uzs_s, uzs_r))
    vx = Scatter4(x, x_nxt, x_prv, lambda t, side: vx_own.at[lax.rem(t + 8, 4), side], vx_1, vx_2, vx_3, vx_4, (vx_s, vx_r), (vxs_s, vxs_r))
    wy = Scatter4(
        y, student.nxt, student.prv,
        lambda t, side: pair_buf.at[lax.rem(t + 8, 4), :, side * half : (side + 1) * half], y_1, y_2, y_3, y_4, (y_s, y_r), (ys_s, ys_r),
    )

    def hidden_block(i):
        away = jnp.where(lax.rem(i, 2) == 1, 4 - (i + 1) // 2, i // 2 - 4)
        t = lax.rem(z + 16 + away, 8)
        value = lax.dot_general(
            jnp.concatenate([ws_all[t, 0], ws_all[t, 1]], axis=1),
            grad[:, :tokens],
            (((0,), (0,)), ((), ())),
            preferred_element_type=jnp.float32,
        )
        hg[t] = value.reshape(hg.shape[1:])

    def weight_block(r):
        return lax.dot_general(
            grad[...], hs_all[:, ds(r * feats, feats)], (((1,), (0,)), ((), ())), preferred_element_type=jnp.float32
        )

    def given(n):
        k = lax.rem(y + 2 + 3 * n, 4)
        return k, to(wg_give.at[n], pair_buf.at[k], (pair_s, pair_r), n, partner)

    def put_ux(side, value):
        uz_own[:, side] = value

    def put_vx(side, value):
        hg_out[1, side] = value

    def put_wy(side, value):
        wg_out[:, side * half : (side + 1) * half] = value

    hidden_block(jnp.int32(0))
    vz.start()

    @pl.loop(1, 8)
    def _(i):
        hidden_block(i)

    ux.start()

    @pl.loop(0, 4)
    def _(n):
        k, copy = given(n)
        wg_give[n] = weight_block(2 * k + 1 - c)
        copy.start()

    vz.step(1)

    @pl.loop(0, 4)
    def _(n):
        k, copy = given(n)
        value = weight_block(2 * k + c)
        copy.wait_recv()
        pair_buf[k] = pair_buf[k] + value
        for at, moves in ((0, (0, 1)), (1, (2,)), (3, (3,))):

            @pl.when(n == at)
            def _():
                for number in moves:
                    wy.send(number)

    ux.middle()
    vz.step(2)
    wy.middle()
    vz.step(3)
    ux.last(put_ux)
    uz.start()
    uz.step(1)
    vx_own[...] = vz.last()
    vx.start()
    uz.step(2)
    vx.middle()
    uz.step(3)
    wy.last(put_wy)
    vx.last(put_vx)
    hg_out[0] = uz.last()

    @pl.loop(0, 4)
    def _(n):
        given(n)[1].wait_send()

    for ring in (ux, vz, uz, vx, wy):
        ring.finish()
    for ring in (student, teacher):
        for k in range(6):
            ring.send(k).wait_send()
        for k in range(7):
            ring.give(k).wait_send()
    chain.finish()


def fused(tau, labels, ht, wt, hs, ws):
    dma, b16, f32 = pltpu.SemaphoreType.DMA, jnp.bfloat16, jnp.float32
    vocab, tokens, padded, feats = wt.shape[0], hs.shape[0], tau.shape[1], ws.shape[1]
    tile = (feats // 16, tokens)
    space, vmem = pl.BlockSpec(memory_space=pl.ANY), pl.BlockSpec(memory_space=pltpu.VMEM)
    pairs = lambda *shape: [dma(shape), dma(shape)]
    wide = lambda *shape: pltpu.VMEM(shape, f32)
    narrow = lambda *shape: pltpu.VMEM(shape, b16)

    def packets(count, *shape):
        coded, scale = pltpu.VMEM((count, *shape), jnp.int16), wide(count, 1, shape[-1])
        return coded, coded, scale, scale

    return pl.pallas_call(
        fused_kernel,
        out_shape=[
            jax.ShapeDtypeStruct((8, padded), f32),
            jax.ShapeDtypeStruct((vocab, feats), f32),
            jax.ShapeDtypeStruct((2, 2, *tile), f32),
        ],
        in_specs=[vmem] * 2 + [space] * 4,
        out_specs=[vmem] * 3,
        scratch_shapes=[
            narrow(CHUNKS, padded, ht.shape[1] // CHUNKS),
            narrow(8, 2, vocab, wt.shape[1] // 2),
            narrow(padded, hs.shape[1]),
            narrow(8, 2, vocab, feats // 2),
            wide(vocab, padded), wide(vocab, padded), wide(8, padded), wide(4, 8, padded), wide(8, 8, padded),
            narrow(vocab, padded),
            wide(8, 4, 2, 2, *tile), wide(4, vocab, feats), wide(4, vocab, feats),
            wide(8, 2, *tile), wide(4, 2, *tile),
            *packets(6, vocab, feats // 2), *packets(6, 8, *tile), *packets(6, *tile), *packets(8, 2, *tile), *packets(8, 4, 2, *tile),
            dma((CHUNKS + 5,)),
        ]
        + pairs(CHUNKS) * 2
        + pairs(CHUNKS // 2) * 2
        + pairs(6) * 2
        + pairs(7) * 2
        + pairs(3)
        + pairs(7)
        + pairs(4)
        + pairs(6) * 6
        + pairs(8) * 4,
        compiler_params=pltpu.CompilerParams(collective_id=0, has_side_effects=True, vmem_limit_bytes=67043328),
        name="fused",
    )(tau, labels, ht, wt, hs, ws)


def heat_scalar(corruption_kinds, heat_per_kind):
    picked = (corruption_kinds[:, None] == jnp.arange(heat_per_kind.shape[0], dtype=jnp.int32)[None, :]).astype(jnp.float32)
    return jnp.sum(picked * heat_per_kind[None, :], axis=1)


def local(ht, wt, hs, ws, labels, kinds, heats):
    tokens = hs.shape[0]
    padded = -(-tokens // 256) * 256
    tau = jnp.pad(heat_scalar(kinds, heats), (0, padded - tokens), constant_values=1.0)[None, :]
    labels = jnp.pad(labels, (0, padded - tokens), constant_values=-1)[None, :]
    whole, wg, hg = fused(tau, labels, ht, wt.T, hs, ws.T)
    peak_t, sum_t, cross, peak_s, sum_s = (whole[k, :tokens] for k in range(5))
    divergence = cross / sum_t - peak_t - jnp.log(sum_t) + peak_s + jnp.log(sum_s)
    return divergence, hg.reshape(-1, tokens).T, wg.T


def solution(mesh):
    finer = Mesh(mesh.devices.reshape(mesh.shape["grp"], 2, 4, 4, 2), AXES)
    return jax.shard_map(
        local,
        mesh=finer,
        in_specs=(
            P((*ROWS, "zh"), None),
            P(ROWS, GRP_VOCAB),
            P(ROWS, None),
            P(ROWS, GRP_VOCAB),
            P(ROWS),
            P(ROWS),
            P(),
        ),
        out_specs=(P(ROWS), P(ROWS, GRP_VOCAB), P(ROWS, GRP_VOCAB)),
        check_vma=False,
    )
```

```python
import functools

import jax
import jax.numpy as jnp
from jax import lax
from jax.experimental import pallas as pl
from jax.experimental.pallas import tpu as pltpu
from jax.sharding import Mesh
from jax.sharding import PartitionSpec as P

AXES = ("zh", "zl", "x", "y", "c")
GRP_VOCAB = ("zh", "zl", "x")
ROWS = ("y", "c")
CHUNKS = 16
MESH = pl.DeviceIdType.MESH


def here():
    return {name: lax.axis_index(name) for name in AXES}


def at_z(z):
    z = lax.rem(z + 16, 8)
    return {"zh": z // 2, "zl": lax.rem(z, 2)}


def at_x(x):
    return {"x": lax.rem(x + 8, 4)}


def at_y(y):
    return {"y": lax.rem(y + 8, 4)}


def to(src, dst, sems, k, device):
    send, recv = sems
    return pltpu.make_async_remote_copy(
        src_ref=src,
        dst_ref=dst,
        send_sem=send.at[k],
        recv_sem=recv.at[k],
        device_id=device,
        device_id_type=MESH,
    )


def greet(devices):
    barrier = pltpu.get_barrier_semaphore()
    for device in devices:
        pl.semaphore_signal(barrier, inc=1, device_id=device, device_id_type=MESH)
    pl.semaphore_wait(barrier, len(devices))


def ds(start, size):
    return pl.ds(pl.multiple_of(start, size), size)


class Ring:
    def __init__(self, shard, whole, ring, pair):
        me = here()
        self.y, self.c = me["y"], me["c"]
        self.shard, self.whole, self.ring, self.pair = shard, whole, ring, pair
        self.nxt, self.prv = at_y(self.y + 1), at_y(self.y - 1)
        self.partner = {"c": 1 - self.c}

    def block(self, y, c, half=None):
        r = lax.rem(y + 8, 4) * 2 + c
        return self.whole.at[r] if half is None else self.whole.at[r, half]

    MOVES = (("n", 0, 0), ("p", 0, 1), ("n", 0, 1), ("p", 0, 0), ("n", 1, 0), ("p", 1, 1))

    def send(self, k):
        way, hops, half = self.MOVES[k]
        owner = self.y - hops if way == "n" else self.y + hops
        device = self.nxt if way == "n" else self.prv
        spot = self.block(owner, self.c, half)
        return to(spot, spot, self.ring, k, device)

    def landed(self, k):
        way, hops, half = self.MOVES[k]
        owner = self.y - 1 - hops if way == "n" else self.y + 1 + hops
        return owner, half

    def wait(self, k):
        owner, half = self.landed(k)
        spot = self.block(owner, self.c, half)
        to(spot, spot, self.ring, k, self.nxt).wait_recv()

    def give(self, k):
        if k == 6:
            spot = self.block(self.y, self.c)
            return to(spot, spot, self.pair, 6, self.partner)
        owner, half = self.landed(k)
        spot = self.block(owner, self.c, half)
        return to(spot, spot, self.pair, k, self.partner)

    def taken(self, k):
        if k == 6:
            spot = self.block(self.y, 1 - self.c)
        else:
            owner, half = self.landed(k)
            spot = self.block(owner, 1 - self.c, half)
        to(spot, spot, self.pair, k, self.partner).wait_recv()


class Chain:
    def __init__(self, whole, rows, out1, mate1, out2, mate2):
        me = here()
        self.zh, self.zl = me["zh"], me["zl"]
        z = self.zh * 2 + self.zl
        self.away = 2 * self.zl - 1
        self.out, self.mate = at_z(z + self.away), at_z(z - self.away)
        self.whole, self.sems = whole, (out1, mate1, out2, mate2)
        self.rows = rows

    def move(self, kind, slot, k, quarter, device):
        q = lax.rem(quarter + 8, 4)
        spot = self.whole.at[k, ds(q * self.rows, self.rows)]
        return to(spot, spot, self.sems[kind], slot, device)

    def out1(self, k):
        return self.move(0, k, k, self.zh, self.out)

    def mate1(self, k):
        return self.move(1, k, k, self.zh + self.away, self.mate)

    def out2(self, j):
        return self.move(2, j, 2 * j + 1 - self.zl, self.zh - self.away, self.out)

    def mate2(self, j):
        return self.move(3, j, 2 * j + self.zl, self.zh + 2 * self.away, self.mate)

    def got_out1(self, k):
        self.move(0, k, k, self.zh + self.away, self.out).wait_recv()

    def got_mate1(self, k):
        self.move(1, k, k, self.zh - self.away, self.out).wait_recv()

    def got_out2(self, j):
        self.move(2, j, 2 * j + self.zl, self.zh + 2 * self.away, self.out).wait_recv()

    def got_mate2(self, j):
        self.move(3, j, 2 * j + 1 - self.zl, self.zh - 2 * self.away, self.out).wait_recv()

    def pair(self, j):
        for k in (2 * j, 2 * j + 1):
            self.got_out1(k)
            self.mate1(k).start()

        @pl.when(j > 0)
        def _():
            self.back(j - 1)

    def back(self, j):
        self.got_mate1(2 * j)
        self.got_mate1(2 * j + 1)
        self.out2(j).start()

    def second(self, j):
        self.got_out2(j)
        self.mate2(j).start()

    def finish(self):
        @pl.loop(0, CHUNKS // 2)
        def _(j):
            for k in (2 * j, 2 * j + 1):
                self.out1(k).wait_send()
                self.mate1(k).wait_send()
            self.out2(j).wait_send()
            self.mate2(j).wait_send()


def folded(ref, count, groups):
    for peak, sums in groups:
        tops = [ref[k, peak : peak + 1, :] for k in range(count)]
        top = functools.reduce(jnp.maximum, tops)
        shares = [jnp.exp(t - top) for t in tops]
        yield peak, top
        for row in sums:
            yield row, functools.reduce(jnp.add, [ref[k, row : row + 1, :] * shares[k] for k in range(count)])


class Exchange:
    def __init__(self, near, far, xs, zs, groups):
        me = here()
        self.x, self.z = me["x"], me["zh"] * 2 + me["zl"]
        self.xs_of = [at_x(self.x + k) for k in range(1, 4)]
        self.zs_of = [at_z(self.z + k) for k in range(1, 8)]
        self.near, self.far, self.xs, self.zs, self.groups = near, far, xs, zs, groups

    def near_copy(self, k):
        spot = self.near.at[self.x]
        return to(spot, spot, self.xs, k, self.xs_of[k])

    def far_copy(self, k):
        spot = self.far.at[self.z]
        return to(spot, spot, self.zs, k, self.zs_of[k])

    def start(self):
        for k in range(3):
            self.near_copy(k).start()

    def middle(self):
        for k in range(3):
            spot = self.near.at[lax.rem(self.x + 3 - k, 4)]
            to(spot, spot, self.xs, k, self.xs_of[0]).wait_recv()
        for row, line in folded(self.near, 4, self.groups):
            self.far[self.z, row : row + 1, :] = line
        for k in range(7):
            self.far_copy(k).start()

    def last(self, out):
        for k in range(7):
            spot = self.far.at[lax.rem(self.z + 7 - k, 8)]
            to(spot, spot, self.zs, k, self.zs_of[0]).wait_recv()
        for row, line in folded(self.far, 8, self.groups):
            out[row : row + 1, :] = line

    def finish(self):
        for k in range(3):
            self.near_copy(k).wait_send()
        for k in range(7):
            self.far_copy(k).wait_send()


class Packets:
    def __init__(self, stage, bufs, stage_scale, scales, sems, scale_sems):
        self.stage, self.bufs, self.sems = stage, bufs, sems
        self.stage_scale, self.scales, self.scale_sems = stage_scale, scales, scale_sems

    def copies(self, k, device, part):
        pick = (k,) if part is None else (k, part)
        return (
            to(self.stage.at[pick], self.bufs.at[pick], self.sems, k, device),
            to(self.stage_scale.at[k], self.scales.at[k], self.scale_sems, k, device),
        )

    def send(self, k, value, device, part=None):
        top = jnp.max(jnp.abs(value), axis=tuple(range(value.ndim - 2)), keepdims=True)
        top = jnp.max(top.reshape(top.shape[-2:]), axis=0, keepdims=True)
        coded = jnp.round(value * (32767.0 / jnp.maximum(top, 1e-30))).astype(jnp.int16)
        self.stage[(k,) if part is None else (k, part)] = coded
        self.stage_scale[k] = top * (1.0 / 32767.0)
        for copy in self.copies(k, device, part):
            copy.start()

    def take(self, k, device, part=None):
        for copy in self.copies(k, device, part):
            copy.wait_recv()
        return self.bufs[(k,) if part is None else (k, part)].astype(jnp.float32) * self.scales[k]

    def sent(self, k, device, part=None):
        for copy in self.copies(k, device, part):
            copy.wait_send()


class Scatter4:
    def __init__(self, index, nxt, prv, own, *packets):
        self.i, self.nxt, self.prv, self.own = index, nxt, prv, own
        self.packets = Packets(*packets)

    def send(self, k):
        i, nxt, prv = self.i, self.nxt, self.prv
        target, side, device = ((i + 2, 0, nxt), (i + 2, 1, prv), (i + 1, 1, nxt), (i - 1, 0, prv))[k]
        self.packets.send(k, self.own(target, side)[...], device)

    def start(self):
        for k in range(4):
            self.send(k)

    def arrived(self, k):
        return self.packets.take(k, self.nxt)

    def middle(self):
        self.packets.send(4, self.own(self.i + 1, 0)[...] + self.arrived(0), self.nxt)
        self.packets.send(5, self.own(self.i - 1, 1)[...] + self.arrived(1), self.prv)

    def last(self, put):
        put(0, self.own(self.i, 0)[...] + self.arrived(3) + self.arrived(4))
        put(1, self.own(self.i, 1)[...] + self.arrived(2) + self.arrived(5))

    def finish(self):
        for k in range(6):
            self.packets.sent(k, self.nxt)


class Scatter8:
    def __init__(self, index, nxt, prv, own, *packets):
        self.i, self.nxt, self.prv, self.own = index, nxt, prv, own
        self.packets = Packets(*packets)
        n = self.packets.bufs.shape[1]
        self.halves = (pl.ds(0, n // 2), pl.ds(n // 2, n // 2))

    def start(self):
        a, b = self.halves
        self.packets.send(0, self.own(self.i + 4)[a], self.nxt, a)
        self.packets.send(4, self.own(self.i - 4)[b], self.prv, b)

    def step(self, s):
        a, b = self.halves
        up, down = self.own(self.i + 4 - s), self.own(self.i - 4 + s)
        if s == 1:
            value = jnp.concatenate([up[a] + self.packets.take(0, self.nxt, a), up[b]])
            self.packets.send(1, value, self.nxt)
            value = jnp.concatenate([down[a], down[b] + self.packets.take(4, self.prv, b)])
            self.packets.send(5, value, self.prv)
        else:
            self.packets.send(s, up[...] + self.packets.take(s - 1, self.nxt), self.nxt)
            self.packets.send(4 + s, down[...] + self.packets.take(3 + s, self.prv), self.prv)

    def last(self):
        return self.own(self.i)[...] + self.packets.take(3, self.nxt) + self.packets.take(7, self.prv)

    def finish(self):
        a, b = self.halves
        for k in range(8):
            self.packets.sent(k, self.nxt, {0: a, 4: b}.get(k))


BOTH_MINOR = (((1,), (1,)), ((), ()))


def fused_kernel(
    kinds, heats, labels, ht, wt, hs, ws, div_out, wg_out, hg_out,
    ht_all, wt_all, hs_all, ws_all, lt, ls, tau, names, whole_t, whole_s, near_t, far_t, near_s, far_s, grad,
    hg, wg_give, pair_buf, uz_own, vx_own,
    y_1, y_2, y_3, y_4, ux_1, ux_2, ux_3, ux_4, vx_1, vx_2, vx_3, vx_4, uz_1, uz_2, uz_3, uz_4, vz_1, vz_2, vz_3, vz_4,
    own_sem, o1s, o1r, m1s, m1r, o2s, o2r, m2s, m2r, ring_t_s, ring_t_r, ring_s_s, ring_s_r,
    pair_t_s, pair_t_r, pair_s_s, pair_s_r, xt_s, xt_r, zt_s, zt_r, xs_s, xs_r, zs_s, zs_r,
    pair_s, pair_r, y_s, y_r, ys_s, ys_r, ux_s, ux_r, uxs_s, uxs_r, vx_s, vx_r, vxs_s, vxs_r,
    uz_s, uz_r, uzs_s, uzs_r, vz_s, vz_r, vzs_s, vzs_r,
):
    me = here()
    y, c = me["y"], me["c"]
    chain = Chain(ht_all, ht.shape[0], (o1s, o1r), (m1s, m1r), (o2s, o2r), (m2s, m2r))
    teacher = Ring(wt, wt_all, (ring_t_s, ring_t_r), (pair_t_s, pair_t_r))
    student = Ring(ws, ws_all, (ring_s_s, ring_s_r), (pair_s_s, pair_s_r))
    of_teacher = Exchange(near_t, far_t, (xt_s, xt_r), (zt_s, zt_r), ((0, (1, 2)),))
    of_student = Exchange(near_s, far_s, (xs_s, xs_r), (zs_s, zs_r), ((0, (1,)), (2, (3,))))
    wide, tokens, padded = ht_all.shape[2], hs.shape[0], lt.shape[1]
    z, x = of_teacher.z, of_teacher.x

    def block_of(i):
        q = i // 2
        return lax.rem(2 * (y + q + q // 2 * (5 - 2 * q)) + lax.rem(i, 2), 8)

    def mine(k):
        chunk = 2 * block_of(k // 2) + lax.rem(k, 2)
        spot = ht_all.at[k, ds(me["zh"] * ht.shape[0], ht.shape[0])]
        return pltpu.make_async_copy(ht.at[:, ds(chunk * wide, wide)], spot, own_sem.at[k])

    own = []
    for ring in (student, teacher):
        half = ring.shard.shape[1] // 2
        for side in (0, 1):
            src = ring.shard.at[:, side * half : (side + 1) * half]
            own.append(pltpu.make_async_copy(src, ring.block(y, c, side), own_sem.at[CHUNKS + len(own)]))
    states = pltpu.make_async_copy(hs, hs_all.at[pl.ds(0, tokens)], own_sem.at[CHUNKS + 4])

    @pl.loop(0, CHUNKS)
    def _(k):
        mine(k).start()

    for copy in own:
        copy.start()
    states.start()
    lt[...] = jnp.zeros(lt.shape, jnp.float32)
    ls[...] = jnp.zeros(ls.shape, jnp.float32)
    tau[...] = jnp.ones(tau.shape, jnp.float32)
    names[...] = jnp.full(names.shape, -1, jnp.int32)
    tau[:, pl.ds(0, tokens)] = functools.reduce(
        jnp.add, [jnp.where(kinds[...] == k, heats[k], 0.0) for k in range(heats.shape[0])]
    )
    names[:, pl.ds(0, tokens)] = labels[...]
    ht_all[:, pl.ds(tokens, padded - tokens)] = jnp.zeros((CHUNKS, padded - tokens, wide), jnp.bfloat16)
    hs_all[pl.ds(tokens, padded - tokens)] = jnp.zeros((padded - tokens, hs.shape[1]), jnp.bfloat16)
    greet([teacher.nxt, teacher.prv, teacher.partner] + of_teacher.xs_of + of_teacher.zs_of)
    for copy in own:
        copy.wait()
    for k in range(4):
        student.send(k).start()
    for k in range(2):
        teacher.send(k).start()

    @pl.loop(0, CHUNKS)
    def _(k):
        mine(k).wait()
        chain.out1(k).start()

    student.give(6).start()
    teacher.give(6).start()
    states.wait()

    def arrivals(ring, moves):
        for k in moves:
            ring.wait(k)
            if k < 2:
                ring.send(k + 4).start()
            ring.give(k).start()

    def rows_of(total):
        return [(a, min(256, total - a)) for a in range(0, total, 256)]

    def add_block(i, out, weights, states):
        for a, n in rows_of(out.shape[0]):
            part = lax.dot_general(
                jnp.concatenate([w[a : a + n] for w in weights], axis=1), states, BOTH_MINOR, preferred_element_type=jnp.float32
            )

            out[a : a + n] += part

    def student_block(i):
        r = [block_of(2 * i), block_of(2 * i + 1)]
        add_block(
            i, ls, [ws_all.at[t, side] for t in r for side in (0, 1)],
            jnp.concatenate([hs_all[:, ds(t * ws.shape[1], ws.shape[1])] for t in r], axis=1),
        )

    def teacher_block(i):
        r = block_of(i)
        add_block(
            i, lt, [wt_all.at[r, side] for side in (0, 1)], jnp.concatenate([ht_all[2 * i], ht_all[2 * i + 1]], axis=1)
        )

    def student_stats():
        @pl.loop(0, padded // 128)
        def _(n):
            tile = ds(n * 128, 128)
            share = 1.0 / tau[:, tile]
            v = ls[:, tile]
            top = jnp.max(v, axis=0, keepdims=True)
            v = v - top
            near_s[x, 0:1, tile] = top * share
            near_s[x, 1:2, tile] = jnp.sum(jnp.exp(v * share), axis=0, keepdims=True)
            near_s[x, 2:3, tile] = top
            near_s[x, 3:4, tile] = jnp.sum(jnp.exp(v), axis=0, keepdims=True)

        of_student.start()

    @pl.loop(0, 2)
    def _(j):
        chain.pair(j)

    arrivals(student, (0, 1))
    chain.pair(jnp.int32(2))
    arrivals(student, (2, 3))
    for k in range(2, 4):
        teacher.send(k).start()

    @pl.loop(3, CHUNKS // 2)
    def _(j):
        chain.pair(j)

        @pl.when(j == 4)
        def _():
            for k in (6, 0, 1, 2, 3):
                student.taken(k)

        @pl.when((j >= 4) & (j < 7))
        def _():
            student_block(j - 4)

        @pl.when(j == 6)
        def _():
            arrivals(teacher, (0, 1))

        @pl.when(j == 7)
        def _():
            arrivals(student, (4, 5))

    chain.back(CHUNKS // 2 - 1)
    for k in (4, 5):
        student.taken(k)

    @pl.loop(0, CHUNKS // 2)
    def _(j):
        chain.second(j)

        @pl.when(j == 0)
        def _():
            student_block(jnp.int32(3))

        @pl.when(j == 1)
        def _():
            student_stats()

        @pl.when(j == 3)
        def _():
            teacher.taken(6)

        @pl.when(j == 4)
        def _():
            of_student.middle()

        @pl.when(j == 5)
        def _():
            arrivals(teacher, (2, 3))
            for k in range(4):
                teacher.taken(k)

        @pl.when(j >= 3)
        def _():
            chain.got_mate2(j - 3)
            teacher_block(j - 3)

    arrivals(teacher, (4, 5))
    of_student.last(whole_s)

    @pl.loop(5, 8)
    def _(i):
        chain.got_mate2(i)

        @pl.when(i == 6)
        def _():
            for k in (4, 5):
                teacher.taken(k)

        teacher_block(i)

    @pl.loop(0, padded // 128)
    def _(n):
        tile = ds(n * 128, 128)
        share = 1.0 / tau[:, tile]
        v = lt[:, tile] * share
        top = jnp.max(v, axis=0, keepdims=True)
        e = jnp.exp(v - top)
        near_t[x, 0:1, tile] = top
        near_t[x, 1:2, tile] = jnp.sum(e, axis=0, keepdims=True)
        near_t[x, 2:3, tile] = jnp.sum(e * (v - ls[:, tile] * share), axis=0, keepdims=True)

    of_teacher.start()
    vocab = wt.shape[0]
    first_entry = (z * 4 + x) * vocab

    def student_share(first, last):
        @pl.loop(first, last)
        def _(n):
            tile = ds(n * 128, 128)
            heat = tau[:, tile]
            s = ls[:, tile]
            peak_s, sum_s, peak_c, sum_c = (whole_s[k : k + 1, tile] for k in range(4))
            prob_s = jnp.exp(s * (1.0 / heat) - (peak_s + jnp.log(sum_s)))
            prob_c = jnp.exp(s - (peak_c + jnp.log(sum_c)))
            entries = first_entry + lax.broadcasted_iota(jnp.int32, s.shape, 0)
            hot = jnp.where(entries == names[:, tile], 1.0, 0.0)
            ls[:, tile] = heat * prob_s + prob_c - hot

    student_share(0, 3)
    of_teacher.middle()
    student_share(3, padded // 128)
    of_teacher.last(whole_t)

    @pl.loop(0, padded // 128)
    def _(n):
        tile = ds(n * 128, 128)
        heat = tau[:, tile]
        peak_t, sum_t, cross = (whole_t[k : k + 1, tile] for k in range(3))
        peak_s, sum_s = (whole_s[k : k + 1, tile] for k in range(2))
        log_t = jnp.log(sum_t)
        div_out[:, tile] = cross / sum_t - peak_t - log_t + peak_s + jnp.log(sum_s)
        prob_t = jnp.exp(lt[:, tile] * (1.0 / heat) - (peak_t + log_t))
        grad[:, tile] = (ls[:, tile] - heat * prob_t).astype(jnp.bfloat16)

    partner, x_nxt, x_prv, z_nxt, z_prv = student.partner, at_x(x + 1), at_x(x - 1), at_z(z + 1), at_z(z - 1)
    feats = ws.shape[1]
    half = feats // 2

    ux = Scatter4(x, x_nxt, x_prv, lambda t, side: hg.at[:, lax.rem(t + 8, 4), 0, side], ux_1, ux_2, ux_3, ux_4, (ux_s, ux_r), (uxs_s, uxs_r))
    vz = Scatter8(z, z_nxt, z_prv, lambda t: hg.at[lax.rem(t + 16, 8), :, 1], vz_1, vz_2, vz_3, vz_4, (vz_s, vz_r), (vzs_s, vzs_r))
    uz = Scatter8(z, z_nxt, z_prv, lambda t: uz_own.at[lax.rem(t + 16, 8)], uz_1, uz_2, uz_3, uz_4, (uz_s, uz_r), (uzs_s, uzs_r))
    vx = Scatter4(x, x_nxt, x_prv, lambda t, side: vx_own.at[lax.rem(t + 8, 4), side], vx_1, vx_2, vx_3, vx_4, (vx_s, vx_r), (vxs_s, vxs_r))
    wy = Scatter4(
        y, student.nxt, student.prv,
        lambda t, side: pair_buf.at[lax.rem(t + 8, 4), :, side * half : (side + 1) * half], y_1, y_2, y_3, y_4, (y_s, y_r), (ys_s, ys_r),
    )

    def hidden_block(i):
        away = jnp.where(lax.rem(i, 2) == 1, 4 - (i + 1) // 2, i // 2 - 4)
        t = lax.rem(z + 16 + away, 8)
        value = lax.dot_general(
            jnp.concatenate([ws_all[t, 0], ws_all[t, 1]], axis=1),
            grad[:, :tokens],
            (((0,), (0,)), ((), ())),
            preferred_element_type=jnp.float32,
        )
        hg[t] = value.reshape(hg.shape[1:])

    def weight_block(r):
        return lax.dot_general(
            grad[...], hs_all[:, ds(r * feats, feats)], (((1,), (0,)), ((), ())), preferred_element_type=jnp.float32
        )

    def given(n):
        k = lax.rem(y + 2 + 3 * n, 4)
        return k, to(wg_give.at[n], pair_buf.at[k], (pair_s, pair_r), n, partner)

    def put_ux(side, value):
        uz_own[:, side] = value

    def put_vx(side, value):
        hg_out[1, side] = value

    def put_wy(side, value):
        wg_out[:, side * half : (side + 1) * half] = value

    hidden_block(jnp.int32(0))
    vz.start()

    @pl.loop(1, 8)
    def _(i):
        hidden_block(i)

    ux.start()
    vz.step(1)

    @pl.loop(0, 4)
    def _(n):
        k, copy = given(n)
        wg_give[n] = weight_block(2 * k + 1 - c)
        copy.start()

    vz.step(2)

    @pl.loop(0, 4)
    def _(n):
        k, copy = given(n)
        value = weight_block(2 * k + c)
        copy.wait_recv()
        pair_buf[k] = pair_buf[k] + value
        for at, moves in ((0, (0, 1)), (1, (2,)), (3, (3,))):

            @pl.when(n == at)
            def _():
                for number in moves:
                    wy.send(number)

    ux.middle()
    vz.step(3)
    wy.middle()
    ux.last(put_ux)
    uz.start()
    vx_own[...] = vz.last()
    vx.start()
    uz.step(1)
    vx.middle()
    uz.step(2)
    uz.step(3)
    vx.last(put_vx)
    wy.last(put_wy)
    hg_out[0] = uz.last()

    @pl.loop(0, 4)
    def _(n):
        given(n)[1].wait_send()

    for ring in (ux, vz, uz, vx, wy):
        ring.finish()
    for ring in (student, teacher):
        for k in range(6):
            ring.send(k).wait_send()
        for k in range(7):
            ring.give(k).wait_send()
    chain.finish()
    of_teacher.finish()
    of_student.finish()


def fused(kinds, heats, labels, ht, wt, hs, ws):
    dma, b16, f32 = pltpu.SemaphoreType.DMA, jnp.bfloat16, jnp.float32
    vocab, tokens, feats = wt.shape[0], hs.shape[0], ws.shape[1]
    padded = -(-tokens // 256) * 256
    tile = (feats // 16, tokens)
    space, vmem = pl.BlockSpec(memory_space=pl.ANY), pl.BlockSpec(memory_space=pltpu.VMEM)
    pairs = lambda *shape: [dma(shape), dma(shape)]
    wide = lambda *shape: pltpu.VMEM(shape, f32)
    narrow = lambda *shape: pltpu.VMEM(shape, b16)

    def packets(count, *shape):
        coded, scale = pltpu.VMEM((count, *shape), jnp.int16), wide(count, 1, shape[-1])
        return coded, coded, scale, scale

    return pl.pallas_call(
        fused_kernel,
        out_shape=[
            jax.ShapeDtypeStruct((1, padded), f32),
            jax.ShapeDtypeStruct((vocab, feats), f32),
            jax.ShapeDtypeStruct((2, 2, *tile), f32),
        ],
        in_specs=[vmem, pl.BlockSpec(memory_space=pltpu.SMEM), vmem] + [space] * 4,
        out_specs=[vmem] * 3,
        scratch_shapes=[
            narrow(CHUNKS, padded, ht.shape[1] // CHUNKS),
            narrow(8, 2, vocab, wt.shape[1] // 2),
            narrow(padded, hs.shape[1]),
            narrow(8, 2, vocab, feats // 2),
            wide(vocab, padded), wide(vocab, padded), wide(1, padded), pltpu.VMEM((1, padded), jnp.int32),
            wide(4, padded), wide(4, padded), wide(4, 4, padded), wide(8, 4, padded), wide(4, 4, padded), wide(8, 4, padded),
            narrow(vocab, padded),
            wide(8, 4, 2, 2, *tile), wide(4, vocab, feats), wide(4, vocab, feats),
            wide(8, 2, *tile), wide(4, 2, *tile),
            *packets(6, vocab, feats // 2), *packets(6, 8, *tile), *packets(6, *tile), *packets(8, 2, *tile), *packets(8, 4, 2, *tile),
            dma((CHUNKS + 5,)),
        ]
        + pairs(CHUNKS) * 2
        + pairs(CHUNKS // 2) * 2
        + pairs(6) * 2
        + pairs(7) * 2
        + (pairs(3) + pairs(7)) * 2
        + pairs(4)
        + pairs(6) * 6
        + pairs(8) * 4,
        compiler_params=pltpu.CompilerParams(collective_id=0, has_side_effects=True, vmem_limit_bytes=67043328),
        name="fused",
    )(kinds, heats, labels, ht, wt, hs, ws)


def finish_kernel(div, wg, hg, div_out, wg_out, hg_out):
    tokens = div_out.shape[0]
    div_out[...] = div[:, :tokens].reshape(tokens)
    wg_out[...] = wg[...]
    hg_out[...] = hg[...].reshape(hg_out.shape)


def finish(div, wg, hg):
    vmem, f32 = pl.BlockSpec(memory_space=pltpu.VMEM), jnp.float32
    tokens = hg.shape[-1]
    return pl.pallas_call(
        finish_kernel,
        out_shape=[
            jax.ShapeDtypeStruct((tokens,), f32),
            jax.ShapeDtypeStruct(wg.shape, f32),
            jax.ShapeDtypeStruct((hg.size // tokens, tokens), f32),
        ],
        in_specs=[vmem] * 3,
        out_specs=[vmem] * 3,
        name="finish",
    )(div, wg, hg)


def local(ht, wt, hs, ws, labels, kinds, heats):
    divergence, wg, hg = finish(*fused(kinds[None, :], heats, labels[None, :], ht, wt.T, hs, ws.T))
    return divergence, hg.T, wg.T


def solution(mesh):
    finer = Mesh(mesh.devices.reshape(mesh.shape["grp"], 2, 4, 4, 2), AXES)
    return jax.shard_map(
        local,
        mesh=finer,
        in_specs=(
            P((*ROWS, "zh"), None),
            P(ROWS, GRP_VOCAB),
            P(ROWS, None),
            P(ROWS, GRP_VOCAB),
            P(ROWS),
            P(ROWS),
            P(),
        ),
        out_specs=(P(ROWS), P(ROWS, GRP_VOCAB), P(ROWS, GRP_VOCAB)),
        check_vma=False,
    )
```

```python
import functools

import jax
import jax.numpy as jnp
from jax import lax
from jax.experimental import pallas as pl
from jax.experimental.pallas import tpu as pltpu
from jax.sharding import Mesh
from jax.sharding import PartitionSpec as P

AXES = ("zh", "zl", "x", "y", "c")
GRP_VOCAB = ("zh", "zl", "x")
ROWS = ("y", "c")
CHUNKS = 16
ROWS_X_FIRST = 24
MESH = pl.DeviceIdType.MESH


def here():
    return {name: lax.axis_index(name) for name in AXES}


def at_z(z):
    z = lax.rem(z + 16, 8)
    return {"zh": z // 2, "zl": lax.rem(z, 2)}


def at_x(x):
    return {"x": lax.rem(x + 8, 4)}


def at_y(y):
    return {"y": lax.rem(y + 8, 4)}


def to(src, dst, sems, k, device):
    send, recv = sems
    return pltpu.make_async_remote_copy(
        src_ref=src,
        dst_ref=dst,
        send_sem=send.at[k],
        recv_sem=recv.at[k],
        device_id=device,
        device_id_type=MESH,
    )


def greet(devices):
    barrier = pltpu.get_barrier_semaphore()
    for device in devices:
        pl.semaphore_signal(barrier, inc=1, device_id=device, device_id_type=MESH)


def greeted(devices):
    pl.semaphore_wait(pltpu.get_barrier_semaphore(), len(devices))


def ds(start, size):
    return pl.ds(pl.multiple_of(start, size), size)


class Ring:
    def __init__(self, shard, whole, ring, pair):
        me = here()
        self.y, self.c = me["y"], me["c"]
        self.shard, self.whole, self.ring, self.pair = shard, whole, ring, pair
        self.nxt, self.prv = at_y(self.y + 1), at_y(self.y - 1)
        self.partner = {"c": 1 - self.c}

    def block(self, y, c, half=None):
        r = lax.rem(y + 8, 4) * 2 + c
        return self.whole.at[r] if half is None else self.whole.at[r, half]

    MOVES = (("n", 0, 0), ("p", 0, 1), ("n", 0, 1), ("p", 0, 0), ("n", 1, 0), ("p", 1, 1))

    def send(self, k):
        way, hops, half = self.MOVES[k]
        owner = self.y - hops if way == "n" else self.y + hops
        device = self.nxt if way == "n" else self.prv
        spot = self.block(owner, self.c, half)
        return to(spot, spot, self.ring, k, device)

    def landed(self, k):
        way, hops, half = self.MOVES[k]
        owner = self.y - 1 - hops if way == "n" else self.y + 1 + hops
        return owner, half

    def wait(self, k):
        owner, half = self.landed(k)
        spot = self.block(owner, self.c, half)
        to(spot, spot, self.ring, k, self.nxt).wait_recv()

    def give(self, k):
        if k == 6:
            spot = self.block(self.y, self.c)
            return to(spot, spot, self.pair, 6, self.partner)
        owner, half = self.landed(k)
        spot = self.block(owner, self.c, half)
        return to(spot, spot, self.pair, k, self.partner)

    def taken(self, k):
        if k == 6:
            spot = self.block(self.y, 1 - self.c)
        else:
            owner, half = self.landed(k)
            spot = self.block(owner, 1 - self.c, half)
        to(spot, spot, self.pair, k, self.partner).wait_recv()


class Chain:
    def __init__(self, whole, rows, out1, mate1, out2, mate2):
        me = here()
        self.zh, self.zl = me["zh"], me["zl"]
        z = self.zh * 2 + self.zl
        self.away = 2 * self.zl - 1
        self.out, self.mate = at_z(z + self.away), at_z(z - self.away)
        self.whole, self.sems = whole, (out1, mate1, out2, mate2)
        self.rows = rows

    def move(self, kind, slot, k, quarter, device):
        q = lax.rem(quarter + 8, 4)
        spot = self.whole.at[k, ds(q * self.rows, self.rows)]
        return to(spot, spot, self.sems[kind], slot, device)

    def out1(self, k):
        return self.move(0, k, k, self.zh, self.out)

    def mate1(self, k):
        return self.move(1, k, k, self.zh + self.away, self.mate)

    def out2(self, j):
        return self.move(2, j, 2 * j + 1 - self.zl, self.zh - self.away, self.out)

    def mate2(self, j):
        return self.move(3, j, 2 * j + self.zl, self.zh + 2 * self.away, self.mate)

    def got_out1(self, k):
        self.move(0, k, k, self.zh + self.away, self.out).wait_recv()

    def got_mate1(self, k):
        self.move(1, k, k, self.zh - self.away, self.out).wait_recv()

    def got_out2(self, j):
        self.move(2, j, 2 * j + self.zl, self.zh + 2 * self.away, self.out).wait_recv()

    def got_mate2(self, j):
        self.move(3, j, 2 * j + 1 - self.zl, self.zh - 2 * self.away, self.out).wait_recv()

    def pair(self, j):
        for k in (2 * j, 2 * j + 1):
            self.got_out1(k)
            self.mate1(k).start()

        @pl.when(j > 0)
        def _():
            self.back(j - 1)

    def back(self, j):
        self.got_mate1(2 * j)
        self.got_mate1(2 * j + 1)
        self.out2(j).start()

    def second(self, j):
        self.got_out2(j)
        self.mate2(j).start()

    def finish(self):
        @pl.loop(0, CHUNKS // 2)
        def _(j):
            for k in (2 * j, 2 * j + 1):
                self.out1(k).wait_send()
                self.mate1(k).wait_send()
            self.out2(j).wait_send()
            self.mate2(j).wait_send()


def folded(ref, count, groups):
    for peak, sums in groups:
        tops = [ref[k, peak : peak + 1, :] for k in range(count)]
        top = functools.reduce(jnp.maximum, tops)
        shares = [jnp.exp(t - top) for t in tops]
        yield peak, top
        for row in sums:
            yield row, functools.reduce(jnp.add, [ref[k, row : row + 1, :] * shares[k] for k in range(count)])


class Exchange:
    def __init__(self, near, far, xs, zs, groups):
        me = here()
        self.x, self.z = me["x"], me["zh"] * 2 + me["zl"]
        self.xs_of = [at_x(self.x + k) for k in range(1, 4)]
        self.zs_of = [at_z(self.z + k) for k in range(1, 8)]
        self.near, self.far, self.xs, self.zs, self.groups = near, far, xs, zs, groups

    def near_copy(self, k):
        spot = self.near.at[self.x]
        return to(spot, spot, self.xs, k, self.xs_of[k])

    def far_copy(self, k):
        spot = self.far.at[self.z]
        return to(spot, spot, self.zs, k, self.zs_of[k])

    def start(self):
        for k in (1, 0, 2):
            self.near_copy(k).start()

    def middle(self):
        for k in range(3):
            spot = self.near.at[lax.rem(self.x + 3 - k, 4)]
            to(spot, spot, self.xs, k, self.xs_of[0]).wait_recv()
        for row, line in folded(self.near, 4, self.groups):
            self.far[self.z, row : row + 1, :] = line
        for k in (3, 2, 4, 1, 5, 0, 6):
            self.far_copy(k).start()

    def last(self, out):
        for k in range(7):
            spot = self.far.at[lax.rem(self.z + 7 - k, 8)]
            to(spot, spot, self.zs, k, self.zs_of[0]).wait_recv()
        for row, line in folded(self.far, 8, self.groups):
            out[row : row + 1, :] = line

    def finish(self):
        for k in range(3):
            self.near_copy(k).wait_send()
        for k in range(7):
            self.far_copy(k).wait_send()


class Packets:
    def __init__(self, stage, bufs, stage_scale, scales, sems, scale_sems):
        self.stage, self.bufs, self.sems = stage, bufs, sems
        self.stage_scale, self.scales, self.scale_sems = stage_scale, scales, scale_sems

    def copies(self, k, device, part):
        pick = (k,) if part is None else (k, part)
        return (
            to(self.stage.at[pick], self.bufs.at[pick], self.sems, k, device),
            to(self.stage_scale.at[k], self.scales.at[k], self.scale_sems, k, device),
        )

    def send(self, k, value, device, part=None):
        top = jnp.max(jnp.abs(value), axis=tuple(range(value.ndim - 2)), keepdims=True)
        top = jnp.max(top.reshape(top.shape[-2:]), axis=0, keepdims=True)
        coded = jnp.round(value * (32767.0 / jnp.maximum(top, 1e-30))).astype(jnp.int16)
        self.stage[(k,) if part is None else (k, part)] = coded
        self.stage_scale[k] = top * (1.0 / 32767.0)
        for copy in self.copies(k, device, part):
            copy.start()

    def take(self, k, device, part=None):
        for copy in self.copies(k, device, part):
            copy.wait_recv()
        return self.bufs[(k,) if part is None else (k, part)].astype(jnp.float32) * self.scales[k]

    def sent(self, k, device, part=None):
        for copy in self.copies(k, device, part):
            copy.wait_send()


class Scatter4:
    SIDE = (0, 1, 1, 0, 0, 1)

    def __init__(self, index, nxt, prv, own, parts, *packets):
        self.i, self.nxt, self.prv, self.own, self.parts = index, nxt, prv, own, parts
        self.packets = Packets(*packets)

    def pack(self, k, value, device):
        self.packets.send(k, value, device, self.parts[self.SIDE[k]])

    def send(self, k):
        i, nxt, prv = self.i, self.nxt, self.prv
        target, device = ((i + 2, nxt), (i + 2, prv), (i + 1, nxt), (i - 1, prv))[k]
        self.pack(k, self.own(target, self.SIDE[k])[...], device)

    def start(self):
        for k in range(4):
            self.send(k)

    def arrived(self, k):
        return self.packets.take(k, self.nxt, self.parts[self.SIDE[k]])

    def middle(self):
        self.pack(4, self.own(self.i + 1, 0)[...] + self.arrived(0), self.nxt)
        self.pack(5, self.own(self.i - 1, 1)[...] + self.arrived(1), self.prv)

    def last(self, put):
        put(0, self.own(self.i, 0)[...] + self.arrived(3) + self.arrived(4))
        put(1, self.own(self.i, 1)[...] + self.arrived(2) + self.arrived(5))

    def finish(self):
        for k in range(6):
            self.packets.sent(k, self.nxt, self.parts[self.SIDE[k]])


class Scatter8:
    def __init__(self, index, nxt, prv, own, *packets):
        self.i, self.nxt, self.prv, self.own = index, nxt, prv, own
        self.packets = Packets(*packets)
        n = self.packets.bufs.shape[1]
        self.halves = (pl.ds(0, n // 2), pl.ds(n // 2, n - n // 2))

    def start(self):
        a, b = self.halves
        self.packets.send(0, self.own(self.i + 4)[a], self.nxt, a)
        self.packets.send(4, self.own(self.i - 4)[b], self.prv, b)

    def step(self, s):
        a, b = self.halves
        up, down = self.own(self.i + 4 - s), self.own(self.i - 4 + s)
        if s == 1:
            value = jnp.concatenate([up[a] + self.packets.take(0, self.nxt, a), up[b]])
            self.packets.send(1, value, self.nxt)
            value = jnp.concatenate([down[a], down[b] + self.packets.take(4, self.prv, b)])
            self.packets.send(5, value, self.prv)
        else:
            self.packets.send(s, up[...] + self.packets.take(s - 1, self.nxt), self.nxt)
            self.packets.send(4 + s, down[...] + self.packets.take(3 + s, self.prv), self.prv)

    def last(self):
        return self.own(self.i)[...] + self.packets.take(3, self.nxt) + self.packets.take(7, self.prv)

    def finish(self):
        a, b = self.halves
        for k in range(8):
            self.packets.sent(k, self.nxt, {0: a, 4: b}.get(k))


BOTH_MINOR = (((1,), (1,)), ((), ()))


def fused_kernel(
    kinds, heats, labels, ht, wt, hs, ws, div_out, wg_out, hg_out,
    ht_all, wt_all, hs_all, ws_all, lt, ls, tau, names, whole_t, whole_s, near_t, far_t, near_s, far_s, grad,
    hg_u, hg_v, wg_give, pair_buf, uz_own, vx_own,
    y_1, y_2, y_3, y_4, ux_1, ux_2, ux_3, ux_4, vx_1, vx_2, vx_3, vx_4, uz_1, uz_2, uz_3, uz_4, vz_1, vz_2, vz_3, vz_4,
    own_sem, o1s, o1r, m1s, m1r, o2s, o2r, m2s, m2r, ring_t_s, ring_t_r, ring_s_s, ring_s_r,
    pair_t_s, pair_t_r, pair_s_s, pair_s_r, xt_s, xt_r, zt_s, zt_r, xs_s, xs_r, zs_s, zs_r,
    pair_s, pair_r, y_s, y_r, ys_s, ys_r, ux_s, ux_r, uxs_s, uxs_r, vx_s, vx_r, vxs_s, vxs_r,
    uz_s, uz_r, uzs_s, uzs_r, vz_s, vz_r, vzs_s, vzs_r,
):
    me = here()
    y, c = me["y"], me["c"]
    chain = Chain(ht_all, ht.shape[0], (o1s, o1r), (m1s, m1r), (o2s, o2r), (m2s, m2r))
    teacher = Ring(wt, wt_all, (ring_t_s, ring_t_r), (pair_t_s, pair_t_r))
    student = Ring(ws, ws_all, (ring_s_s, ring_s_r), (pair_s_s, pair_s_r))
    of_teacher = Exchange(near_t, far_t, (xt_s, xt_r), (zt_s, zt_r), ((0, (1, 2)),))
    of_student = Exchange(near_s, far_s, (xs_s, xs_r), (zs_s, zs_r), ((0, (1,)), (2, (3,))))
    wide, tokens, padded = ht_all.shape[2], hs.shape[0], lt.shape[1]
    z, x = of_teacher.z, of_teacher.x

    def block_of(i):
        q = i // 2
        return lax.rem(2 * (y + q + q // 2 * (5 - 2 * q)) + lax.rem(i, 2), 8)

    def mine(k):
        chunk = 2 * block_of(k // 2) + lax.rem(k, 2)
        spot = ht_all.at[k, ds(me["zh"] * ht.shape[0], ht.shape[0])]
        return pltpu.make_async_copy(ht.at[:, ds(chunk * wide, wide)], spot, own_sem.at[k])

    peers = [teacher.nxt, teacher.prv, teacher.partner] + of_teacher.xs_of + of_teacher.zs_of
    greet(peers)
    own = []
    for ring in (student, teacher):
        half = ring.shard.shape[1] // 2
        for side in (0, 1):
            src = ring.shard.at[:, side * half : (side + 1) * half]
            own.append(pltpu.make_async_copy(src, ring.block(y, c, side), own_sem.at[CHUNKS + len(own)]))
    states = pltpu.make_async_copy(hs, hs_all.at[pl.ds(0, tokens)], own_sem.at[CHUNKS + 4])

    @pl.loop(0, CHUNKS)
    def _(k):
        mine(k).start()

    for copy in own:
        copy.start()
    states.start()
    lt[...] = jnp.zeros(lt.shape, jnp.float32)
    ls[...] = jnp.zeros(ls.shape, jnp.float32)
    tau[...] = jnp.ones(tau.shape, jnp.float32)
    names[...] = jnp.full(names.shape, -1, jnp.int32)
    tau[:, pl.ds(0, tokens)] = functools.reduce(
        jnp.add, [jnp.where(kinds[...].reshape(1, tokens) == k, heats[k], 0.0) for k in range(heats.shape[0])]
    )
    names[:, pl.ds(0, tokens)] = labels[...].reshape(1, tokens)
    ht_all[:, pl.ds(tokens, padded - tokens)] = jnp.zeros((CHUNKS, padded - tokens, wide), jnp.bfloat16)
    hs_all[pl.ds(tokens, padded - tokens)] = jnp.zeros((padded - tokens, hs.shape[1]), jnp.bfloat16)
    greeted(peers)
    for copy in own:
        copy.wait()
    for k in range(4):
        student.send(k).start()
    for k in range(2):
        teacher.send(k).start()

    @pl.loop(0, CHUNKS)
    def _(k):
        mine(k).wait()
        chain.out1(k).start()

    student.give(6).start()
    teacher.give(6).start()
    states.wait()

    def arrivals(ring, moves):
        for k in moves:
            ring.wait(k)
            if k < 2:
                ring.send(k + 4).start()
            ring.give(k).start()

    def rows_of(total):
        return [(a, min(256, total - a)) for a in range(0, total, 256)]

    def add_block(i, out, weights, states):
        for a, n in rows_of(out.shape[0]):
            part = lax.dot_general(
                jnp.concatenate([w[a : a + n] for w in weights], axis=1), states, BOTH_MINOR, preferred_element_type=jnp.float32
            )

            out[a : a + n] += part

    def student_block(i):
        r = [block_of(2 * i), block_of(2 * i + 1)]
        add_block(
            i, ls, [ws_all.at[t, side] for t in r for side in (0, 1)],
            jnp.concatenate([hs_all[:, ds(t * ws.shape[1], ws.shape[1])] for t in r], axis=1),
        )

    def teacher_block(i):
        r = block_of(i)
        add_block(
            i, lt, [wt_all.at[r, side] for side in (0, 1)], jnp.concatenate([ht_all[2 * i], ht_all[2 * i + 1]], axis=1)
        )

    def student_stats():
        @pl.loop(0, padded // 128)
        def _(n):
            tile = ds(n * 128, 128)
            share = 1.0 / tau[:, tile]
            v = ls[:, tile]
            top = jnp.max(v, axis=0, keepdims=True)
            v = v - top
            near_s[x, 0:1, tile] = top * share
            near_s[x, 1:2, tile] = jnp.sum(jnp.exp(v * share), axis=0, keepdims=True)
            near_s[x, 2:3, tile] = top
            near_s[x, 3:4, tile] = jnp.sum(jnp.exp(v), axis=0, keepdims=True)

        of_student.start()

    @pl.loop(0, 2)
    def _(j):
        chain.pair(j)

    arrivals(student, (0, 1))
    chain.pair(jnp.int32(2))
    arrivals(student, (2, 3))
    for k in range(2, 4):
        teacher.send(k).start()

    @pl.loop(3, CHUNKS // 2)
    def _(j):
        chain.pair(j)

        @pl.when(j == 4)
        def _():
            for k in (6, 0, 1, 2, 3):
                student.taken(k)

        @pl.when((j >= 4) & (j < 7))
        def _():
            student_block(j - 4)

        @pl.when(j == 6)
        def _():
            arrivals(teacher, (0, 1))

        @pl.when(j == 7)
        def _():
            arrivals(student, (4, 5))

    chain.back(CHUNKS // 2 - 1)
    for k in (4, 5):
        student.taken(k)

    @pl.loop(0, CHUNKS // 2)
    def _(j):
        chain.second(j)

        @pl.when(j == 0)
        def _():
            student_block(jnp.int32(3))

        @pl.when(j == 1)
        def _():
            student_stats()

        @pl.when(j == 3)
        def _():
            teacher.taken(6)

        @pl.when(j == 4)
        def _():
            of_student.middle()

        @pl.when(j == 5)
        def _():
            arrivals(teacher, (2, 3))
            for k in range(4):
                teacher.taken(k)

        @pl.when(j >= 3)
        def _():
            chain.got_mate2(j - 3)
            teacher_block(j - 3)

    arrivals(teacher, (4, 5))
    of_student.last(whole_s)

    @pl.loop(5, 8)
    def _(i):
        chain.got_mate2(i)

        @pl.when(i == 6)
        def _():
            for k in (4, 5):
                teacher.taken(k)

        teacher_block(i)

    @pl.loop(0, padded // 128)
    def _(n):
        tile = ds(n * 128, 128)
        share = 1.0 / tau[:, tile]
        v = lt[:, tile] * share
        top = jnp.max(v, axis=0, keepdims=True)
        e = jnp.exp(v - top)
        near_t[x, 0:1, tile] = top
        near_t[x, 1:2, tile] = jnp.sum(e, axis=0, keepdims=True)
        near_t[x, 2:3, tile] = jnp.sum(e * (v - ls[:, tile] * share), axis=0, keepdims=True)

    of_teacher.start()
    vocab = wt.shape[0]
    first_entry = (z * 4 + x) * vocab

    def student_share(first, last):
        @pl.loop(first, last)
        def _(n):
            tile = ds(n * 128, 128)
            heat = tau[:, tile]
            s = ls[:, tile]
            peak_s, sum_s, peak_c, sum_c = (whole_s[k : k + 1, tile] for k in range(4))
            prob_s = jnp.exp(s * (1.0 / heat) - (peak_s + jnp.log(sum_s)))
            prob_c = jnp.exp(s - (peak_c + jnp.log(sum_c)))
            entries = first_entry + lax.broadcasted_iota(jnp.int32, s.shape, 0)
            hot = jnp.where(entries == names[:, tile], 1.0, 0.0)
            ls[:, tile] = heat * prob_s + prob_c - hot

    student_share(0, padded // 256)
    of_teacher.middle()
    student_share(padded // 256, padded // 128)
    of_teacher.last(whole_t)

    @pl.loop(0, padded // 128)
    def _(n):
        tile = ds(n * 128, 128)
        heat = tau[:, tile]
        peak_t, sum_t, cross = (whole_t[k : k + 1, tile] for k in range(3))
        peak_s, sum_s = (whole_s[k : k + 1, tile] for k in range(2))
        log_t = jnp.log(sum_t)
        div_out[:, tile] = cross / sum_t - peak_t - log_t + peak_s + jnp.log(sum_s)
        prob_t = jnp.exp(lt[:, tile] * (1.0 / heat) - (peak_t + log_t))
        grad[:, tile] = (ls[:, tile] - heat * prob_t).astype(jnp.bfloat16)

    partner, x_nxt, x_prv, z_nxt, z_prv = student.partner, at_x(x + 1), at_x(x - 1), at_z(z + 1), at_z(z - 1)
    feats = ws.shape[1]
    half = feats // 2

    groups_u, groups_v = hg_u.shape[2], hg_v.shape[2]
    cut = groups_v // 2
    sides = (pl.ds(0, cut), pl.ds(cut, groups_v - cut))
    ux = Scatter4(
        x, x_nxt, x_prv, lambda t, side: hg_u.at[pl.ds(side * 4, 4), lax.rem(t + 8, 4)], (None, None),
        ux_1, ux_2, ux_3, ux_4, (ux_s, ux_r), (uxs_s, uxs_r),
    )
    vz = Scatter8(z, z_nxt, z_prv, lambda t: hg_v.at[lax.rem(t + 16, 8)], vz_1, vz_2, vz_3, vz_4, (vz_s, vz_r), (vzs_s, vzs_r))
    uz = Scatter8(z, z_nxt, z_prv, lambda t: uz_own.at[lax.rem(t + 16, 8)], uz_1, uz_2, uz_3, uz_4, (uz_s, uz_r), (uzs_s, uzs_r))
    vx = Scatter4(
        x, x_nxt, x_prv, lambda t, side: vx_own.at[lax.rem(t + 8, 4), sides[side]], (pl.ds(0, cut), pl.ds(0, groups_v - cut)),
        vx_1, vx_2, vx_3, vx_4, (vx_s, vx_r), (vxs_s, vxs_r),
    )
    wy = Scatter4(
        y, student.nxt, student.prv,
        lambda t, side: pair_buf.at[lax.rem(t + 8, 4), :, side * half : (side + 1) * half], (None, None), y_1, y_2, y_3, y_4, (y_s, y_r), (ys_s, ys_r),
    )

    def hidden_block(i):
        away = jnp.where(lax.rem(i, 2) == 1, 4 - (i + 1) // 2, i // 2 - 4)
        t = lax.rem(z + 16 + away, 8)
        value = lax.dot_general(
            jnp.concatenate([ws_all[t, 0], ws_all[t, 1]], axis=1),
            grad[...],
            (((0,), (0,)), ((), ())),
            preferred_element_type=jnp.float32,
        )
        value = value.reshape(4, groups_u + groups_v, 8, padded)
        hg_u[t] = value[:, :groups_u]
        hg_v[t] = value[:, groups_u:]

    def weight_block(r):
        return lax.dot_general(
            grad[...], hs_all[:, ds(r * feats, feats)], (((1,), (0,)), ((), ())), preferred_element_type=jnp.float32
        )

    def given(n):
        k = lax.rem(y + 2 + 3 * n, 4)
        return k, to(wg_give.at[n], pair_buf.at[k], (pair_s, pair_r), n, partner)

    def put_ux(side, value):
        uz_own[pl.ds(side * 4, 4)] = value

    def put_vx(side, value):
        hg_out[pl.ds(8 * (groups_u + side * cut), value.shape[0] * 8)] = value.reshape(-1, padded)

    def put_wy(side, value):
        wg_out[:, side * half : (side + 1) * half] = value

    def give_block(n):
        k, copy = given(n)
        wg_give[n] = weight_block(2 * k + 1 - c)
        copy.start()

    def own_block(n):
        k, copy = given(n)
        value = weight_block(2 * k + c)
        copy.wait_recv()
        pair_buf[k] = pair_buf[k] + value

    hidden_block(jnp.int32(0))
    vz.start()

    @pl.loop(1, 4)
    def _(i):
        hidden_block(i)

    give_block(jnp.int32(0))
    vz.step(1)

    @pl.loop(4, 8)
    def _(i):
        hidden_block(i)

    ux.start()
    own_block(jnp.int32(0))
    wy.send(0)
    wy.send(1)

    @pl.loop(1, 4)
    def _(n):
        give_block(n)

    vz.step(2)

    @pl.loop(1, 4)
    def _(n):
        own_block(n)
        for at, number in ((1, 2), (3, 3)):

            @pl.when(n == at)
            def _():
                wy.send(number)

    ux.middle()
    wy.middle()
    vz.step(3)
    ux.last(put_ux)
    uz.start()
    uz.step(1)
    vx_own[...] = vz.last()
    vx.start()
    uz.step(2)
    vx.middle()
    uz.step(3)
    wy.last(put_wy)
    vx.last(put_vx)
    hg_out[pl.ds(0, 8 * groups_u)] = uz.last().reshape(8 * groups_u, padded)

    @pl.loop(0, 4)
    def _(n):
        given(n)[1].wait_send()

    for ring in (ux, vz, uz, vx, wy):
        ring.finish()
    for ring in (student, teacher):
        for k in range(6):
            ring.send(k).wait_send()
        for k in range(7):
            ring.give(k).wait_send()
    chain.finish()
    of_teacher.finish()
    of_student.finish()


def fused(kinds, heats, labels, ht, wt, hs, ws):
    dma, b16, f32 = pltpu.SemaphoreType.DMA, jnp.bfloat16, jnp.float32
    vocab, tokens, feats = wt.shape[0], hs.shape[0], ws.shape[1]
    padded = -(-tokens // 256) * 256
    tile = (8, padded)
    groups_u = ROWS_X_FIRST // 8
    groups_v = feats // 32 - groups_u
    space, vmem = pl.BlockSpec(memory_space=pl.ANY), pl.BlockSpec(memory_space=pltpu.VMEM)
    pairs = lambda *shape: [dma(shape), dma(shape)]
    wide = lambda *shape: pltpu.VMEM(shape, f32)
    narrow = lambda *shape: pltpu.VMEM(shape, b16)

    def packets(count, *shape):
        coded, scale = pltpu.VMEM((count, *shape), jnp.int16), wide(count, 1, shape[-1])
        return coded, coded, scale, scale

    return pl.pallas_call(
        fused_kernel,
        out_shape=[
            jax.ShapeDtypeStruct((1, padded), f32),
            jax.ShapeDtypeStruct((vocab, feats), f32),
            jax.ShapeDtypeStruct((feats // 4, padded), f32),
        ],
        in_specs=[vmem, pl.BlockSpec(memory_space=pltpu.SMEM), vmem] + [space] * 4,
        out_specs=[vmem] * 3,
        scratch_shapes=[
            narrow(CHUNKS, padded, ht.shape[1] // CHUNKS),
            narrow(8, 2, vocab, wt.shape[1] // 2),
            narrow(padded, hs.shape[1]),
            narrow(8, 2, vocab, feats // 2),
            wide(vocab, padded), wide(vocab, padded), wide(1, padded), pltpu.VMEM((1, padded), jnp.int32),
            wide(4, padded), wide(4, padded), wide(4, 4, padded), wide(8, 4, padded), wide(4, 4, padded), wide(8, 4, padded),
            narrow(vocab, padded),
            wide(8, 4, groups_u, *tile), wide(8, 4, groups_v, *tile), wide(4, vocab, feats), wide(4, vocab, feats),
            wide(8, groups_u, *tile), wide(4, groups_v, *tile),
            *packets(6, vocab, feats // 2), *packets(6, 4, groups_u, *tile), *packets(6, groups_v - groups_v // 2, *tile),
            *packets(8, groups_u, *tile), *packets(8, 4, groups_v, *tile),
            dma((CHUNKS + 5,)),
        ]
        + pairs(CHUNKS) * 2
        + pairs(CHUNKS // 2) * 2
        + pairs(6) * 2
        + pairs(7) * 2
        + (pairs(3) + pairs(7)) * 2
        + pairs(4)
        + pairs(6) * 6
        + pairs(8) * 4,
        compiler_params=pltpu.CompilerParams(collective_id=0, has_side_effects=True, vmem_limit_bytes=67043328),
        name="fused",
    )(kinds, heats, labels, ht, wt, hs, ws)


def finish_kernel(div, wg, hg, div_out, wg_out, hg_out):
    tokens = div_out.shape[0]
    div_out[...] = div[:, :tokens].reshape(tokens)
    wg_out[...] = wg[...]
    hg_out[...] = hg[:, :tokens]


def finish(tokens, div, wg, hg):
    vmem, f32 = pl.BlockSpec(memory_space=pltpu.VMEM), jnp.float32
    return pl.pallas_call(
        finish_kernel,
        out_shape=[
            jax.ShapeDtypeStruct((tokens,), f32),
            jax.ShapeDtypeStruct(wg.shape, f32),
            jax.ShapeDtypeStruct((hg.shape[0], tokens), f32),
        ],
        in_specs=[vmem] * 3,
        out_specs=[vmem] * 3,
        name="finish",
    )(div, wg, hg)


def local(ht, wt, hs, ws, labels, kinds, heats):
    divergence, wg, hg = finish(hs.shape[0], *fused(kinds, heats, labels, ht, wt.T, hs, ws.T))
    return divergence, hg.T, wg.T


def solution(mesh):
    finer = Mesh(mesh.devices.reshape(mesh.shape["grp"], 2, 4, 4, 2), AXES)
    return jax.shard_map(
        local,
        mesh=finer,
        in_specs=(
            P((*ROWS, "zh"), None),
            P(ROWS, GRP_VOCAB),
            P(ROWS, None),
            P(ROWS, GRP_VOCAB),
            P(ROWS),
            P(ROWS),
            P(),
        ),
        out_specs=(P(ROWS), P(ROWS, GRP_VOCAB), P(ROWS, GRP_VOCAB)),
        check_vma=False,
    )
```

```python
import functools

import jax
import jax.numpy as jnp
from jax import lax
from jax.experimental import pallas as pl
from jax.experimental.pallas import tpu as pltpu
from jax.sharding import Mesh
from jax.sharding import PartitionSpec as P

AXES = ("zh", "zl", "x", "y", "c")
GRP_VOCAB = ("zh", "zl", "x")
ROWS = ("y", "c")
CHUNKS = 16
ROWS_X_FIRST = 24
MESH = pl.DeviceIdType.MESH


def here():
    return {name: lax.axis_index(name) for name in AXES}


def at_z(z):
    z = lax.rem(z + 16, 8)
    return {"zh": z // 2, "zl": lax.rem(z, 2)}


def at_x(x):
    return {"x": lax.rem(x + 8, 4)}


def at_y(y):
    return {"y": lax.rem(y + 8, 4)}


def to(src, dst, sems, k, device):
    send, recv = sems
    return pltpu.make_async_remote_copy(
        src_ref=src,
        dst_ref=dst,
        send_sem=send.at[k],
        recv_sem=recv.at[k],
        device_id=device,
        device_id_type=MESH,
    )


def greet(devices):
    barrier = pltpu.get_barrier_semaphore()
    for device in devices:
        pl.semaphore_signal(barrier, inc=1, device_id=device, device_id_type=MESH)


def greeted(devices):
    pl.semaphore_wait(pltpu.get_barrier_semaphore(), len(devices))


def ds(start, size):
    return pl.ds(pl.multiple_of(start, size), size)


class Ring:
    def __init__(self, shard, whole, ring, pair):
        me = here()
        self.y, self.c = me["y"], me["c"]
        self.shard, self.whole, self.ring, self.pair = shard, whole, ring, pair
        self.nxt, self.prv = at_y(self.y + 1), at_y(self.y - 1)
        self.partner = {"c": 1 - self.c}

    def block(self, y, c, half=None):
        r = lax.rem(y + 8, 4) * 2 + c
        return self.whole.at[r] if half is None else self.whole.at[r, half]

    MOVES = (("n", 0, 0), ("p", 0, 1), ("n", 0, 1), ("p", 0, 0), ("n", 1, 0), ("p", 1, 1))

    def send(self, k):
        way, hops, half = self.MOVES[k]
        owner = self.y - hops if way == "n" else self.y + hops
        device = self.nxt if way == "n" else self.prv
        spot = self.block(owner, self.c, half)
        return to(spot, spot, self.ring, k, device)

    def landed(self, k):
        way, hops, half = self.MOVES[k]
        owner = self.y - 1 - hops if way == "n" else self.y + 1 + hops
        return owner, half

    def wait(self, k):
        owner, half = self.landed(k)
        spot = self.block(owner, self.c, half)
        to(spot, spot, self.ring, k, self.nxt).wait_recv()

    def give(self, k):
        if k == 6:
            spot = self.block(self.y, self.c)
            return to(spot, spot, self.pair, 6, self.partner)
        owner, half = self.landed(k)
        spot = self.block(owner, self.c, half)
        return to(spot, spot, self.pair, k, self.partner)

    def taken(self, k):
        if k == 6:
            spot = self.block(self.y, 1 - self.c)
        else:
            owner, half = self.landed(k)
            spot = self.block(owner, 1 - self.c, half)
        to(spot, spot, self.pair, k, self.partner).wait_recv()


class Chain:
    def __init__(self, whole, rows, out1, mate1, out2, mate2):
        me = here()
        self.zh, self.zl = me["zh"], me["zl"]
        z = self.zh * 2 + self.zl
        self.away = 2 * self.zl - 1
        self.out, self.mate = at_z(z + self.away), at_z(z - self.away)
        self.whole, self.sems = whole, (out1, mate1, out2, mate2)
        self.rows = rows

    def move(self, kind, slot, k, quarter, device):
        q = lax.rem(quarter + 8, 4)
        spot = self.whole.at[k, ds(q * self.rows, self.rows)]
        return to(spot, spot, self.sems[kind], slot, device)

    def out1(self, k):
        return self.move(0, k, k, self.zh, self.out)

    def mate1(self, k):
        return self.move(1, k, k, self.zh + self.away, self.mate)

    def out2(self, j):
        return self.move(2, j, 2 * j + 1 - self.zl, self.zh - self.away, self.out)

    def mate2(self, j):
        return self.move(3, j, 2 * j + self.zl, self.zh + 2 * self.away, self.mate)

    def got_out1(self, k):
        self.move(0, k, k, self.zh + self.away, self.out).wait_recv()

    def got_mate1(self, k):
        self.move(1, k, k, self.zh - self.away, self.out).wait_recv()

    def got_out2(self, j):
        self.move(2, j, 2 * j + self.zl, self.zh + 2 * self.away, self.out).wait_recv()

    def got_mate2(self, j):
        self.move(3, j, 2 * j + 1 - self.zl, self.zh - 2 * self.away, self.out).wait_recv()

    def pair(self, j):
        for k in (2 * j, 2 * j + 1):
            self.got_out1(k)
            self.mate1(k).start()

        @pl.when(j > 0)
        def _():
            self.back(j - 1)

    def back(self, j):
        self.got_mate1(2 * j)
        self.got_mate1(2 * j + 1)
        self.out2(j).start()

    def second(self, j):
        self.got_out2(j)
        self.mate2(j).start()

    def finish(self):
        @pl.loop(0, CHUNKS // 2)
        def _(j):
            for k in (2 * j, 2 * j + 1):
                self.out1(k).wait_send()
                self.mate1(k).wait_send()
            self.out2(j).wait_send()
            self.mate2(j).wait_send()


def folded(ref, count, groups):
    for peak, sums in groups:
        tops = [ref[k, peak : peak + 1, :] for k in range(count)]
        top = functools.reduce(jnp.maximum, tops)
        shares = [jnp.exp(t - top) for t in tops]
        yield peak, top
        for row in sums:
            yield row, functools.reduce(jnp.add, [ref[k, row : row + 1, :] * shares[k] for k in range(count)])


class Exchange:
    def __init__(self, near, far, xs, zs, groups):
        me = here()
        self.x, self.z = me["x"], me["zh"] * 2 + me["zl"]
        self.xs_of = [at_x(self.x + k) for k in range(1, 4)]
        self.zs_of = [at_z(self.z + k) for k in range(1, 8)]
        self.near, self.far, self.xs, self.zs, self.groups = near, far, xs, zs, groups

    def near_copy(self, k):
        spot = self.near.at[self.x]
        return to(spot, spot, self.xs, k, self.xs_of[k])

    def far_copy(self, k):
        spot = self.far.at[self.z]
        return to(spot, spot, self.zs, k, self.zs_of[k])

    def start(self):
        for k in (1, 0, 2):
            self.near_copy(k).start()

    def middle(self):
        for k in range(3):
            spot = self.near.at[lax.rem(self.x + 3 - k, 4)]
            to(spot, spot, self.xs, k, self.xs_of[0]).wait_recv()
        for row, line in folded(self.near, 4, self.groups):
            self.far[self.z, row : row + 1, :] = line
        for k in (3, 2, 4, 1, 5, 0, 6):
            self.far_copy(k).start()

    def last(self, out):
        for k in range(7):
            spot = self.far.at[lax.rem(self.z + 7 - k, 8)]
            to(spot, spot, self.zs, k, self.zs_of[0]).wait_recv()
        for row, line in folded(self.far, 8, self.groups):
            out[row : row + 1, :] = line

    def finish(self):
        for k in range(3):
            self.near_copy(k).wait_send()
        for k in range(7):
            self.far_copy(k).wait_send()


class Packets:
    def __init__(self, stage, bufs, stage_scale, scales, sems, scale_sems):
        self.stage, self.bufs, self.sems = stage, bufs, sems
        self.stage_scale, self.scales, self.scale_sems = stage_scale, scales, scale_sems

    def copies(self, k, device, part):
        pick = (k,) if part is None else (k, part)
        return (
            to(self.stage.at[pick], self.bufs.at[pick], self.sems, k, device),
            to(self.stage_scale.at[k], self.scales.at[k], self.scale_sems, k, device),
        )

    def send(self, k, value, device, part=None):
        top = jnp.max(jnp.abs(value), axis=tuple(range(value.ndim - 2)), keepdims=True)
        top = jnp.max(top.reshape(top.shape[-2:]), axis=0, keepdims=True)
        coded = jnp.round(value * (32767.0 / jnp.maximum(top, 1e-30))).astype(jnp.int16)
        self.stage[(k,) if part is None else (k, part)] = coded
        self.stage_scale[k] = top * (1.0 / 32767.0)
        for copy in self.copies(k, device, part):
            copy.start()

    def take(self, k, device, part=None):
        for copy in self.copies(k, device, part):
            copy.wait_recv()
        return self.bufs[(k,) if part is None else (k, part)].astype(jnp.float32) * self.scales[k]

    def sent(self, k, device, part=None):
        for copy in self.copies(k, device, part):
            copy.wait_send()


class Scatter4:
    SIDE = (0, 1, 1, 0, 0, 1)

    def __init__(self, index, nxt, prv, own, parts, *packets):
        self.i, self.nxt, self.prv, self.own, self.parts = index, nxt, prv, own, parts
        self.packets = Packets(*packets)

    def pack(self, k, value, device):
        self.packets.send(k, value, device, self.parts[self.SIDE[k]])

    def send(self, k):
        i, nxt, prv = self.i, self.nxt, self.prv
        target, device = ((i + 2, nxt), (i + 2, prv), (i + 1, nxt), (i - 1, prv))[k]
        self.pack(k, self.own(target, self.SIDE[k])[...], device)

    def start(self):
        for k in range(4):
            self.send(k)

    def arrived(self, k):
        return self.packets.take(k, self.nxt, self.parts[self.SIDE[k]])

    def middle(self):
        self.pack(4, self.own(self.i + 1, 0)[...] + self.arrived(0), self.nxt)
        self.pack(5, self.own(self.i - 1, 1)[...] + self.arrived(1), self.prv)

    def last(self, put):
        put(0, self.own(self.i, 0)[...] + self.arrived(3) + self.arrived(4))
        put(1, self.own(self.i, 1)[...] + self.arrived(2) + self.arrived(5))

    def finish(self):
        for k in range(6):
            self.packets.sent(k, self.nxt, self.parts[self.SIDE[k]])


class Scatter8:
    def __init__(self, index, nxt, prv, own, *packets):
        self.i, self.nxt, self.prv, self.own = index, nxt, prv, own
        self.packets = Packets(*packets)
        n = self.packets.bufs.shape[1]
        self.halves = (pl.ds(0, n // 2), pl.ds(n // 2, n - n // 2))

    def start(self):
        a, b = self.halves
        self.packets.send(0, self.own(self.i + 4)[a], self.nxt, a)
        self.packets.send(4, self.own(self.i - 4)[b], self.prv, b)

    def step(self, s):
        a, b = self.halves
        up, down = self.own(self.i + 4 - s), self.own(self.i - 4 + s)
        if s == 1:
            value = jnp.concatenate([up[a] + self.packets.take(0, self.nxt, a), up[b]])
            self.packets.send(1, value, self.nxt)
            value = jnp.concatenate([down[a], down[b] + self.packets.take(4, self.prv, b)])
            self.packets.send(5, value, self.prv)
        else:
            self.packets.send(s, up[...] + self.packets.take(s - 1, self.nxt), self.nxt)
            self.packets.send(4 + s, down[...] + self.packets.take(3 + s, self.prv), self.prv)

    def last(self):
        return self.own(self.i)[...] + self.packets.take(3, self.nxt) + self.packets.take(7, self.prv)

    def finish(self):
        a, b = self.halves
        for k in range(8):
            self.packets.sent(k, self.nxt, {0: a, 4: b}.get(k))


BOTH_MINOR = (((1,), (1,)), ((), ()))


def fused_kernel(
    kinds, heats, labels, ht, wt, hs, ws, div_out, wg_out, hg_out,
    ht_all, wt_all, hs_all, ws_all, lt, ls, tau, names, whole_t, whole_s, near_t, far_t, near_s, far_s, grad,
    hg_u, hg_v, wg_give, pair_buf, uz_own, vx_own,
    y_1, y_2, y_3, y_4, ux_1, ux_2, ux_3, ux_4, vx_1, vx_2, vx_3, vx_4, uz_1, uz_2, uz_3, uz_4, va_1, va_2, va_3, va_4,
    vb_1, vb_2, vb_3, vb_4,
    own_sem, o1s, o1r, m1s, m1r, o2s, o2r, m2s, m2r, ring_t_s, ring_t_r, ring_s_s, ring_s_r,
    pair_t_s, pair_t_r, pair_s_s, pair_s_r, xt_s, xt_r, zt_s, zt_r, xs_s, xs_r, zs_s, zs_r,
    pair_s, pair_r, y_s, y_r, ys_s, ys_r, ux_s, ux_r, uxs_s, uxs_r, vx_s, vx_r, vxs_s, vxs_r,
    uz_s, uz_r, uzs_s, uzs_r, va_s, va_r, vas_s, vas_r, vb_s, vb_r, vbs_s, vbs_r,
):
    me = here()
    y, c = me["y"], me["c"]
    chain = Chain(ht_all, ht.shape[0], (o1s, o1r), (m1s, m1r), (o2s, o2r), (m2s, m2r))
    teacher = Ring(wt, wt_all, (ring_t_s, ring_t_r), (pair_t_s, pair_t_r))
    student = Ring(ws, ws_all, (ring_s_s, ring_s_r), (pair_s_s, pair_s_r))
    of_teacher = Exchange(near_t, far_t, (xt_s, xt_r), (zt_s, zt_r), ((0, (1, 2)),))
    of_student = Exchange(near_s, far_s, (xs_s, xs_r), (zs_s, zs_r), ((0, (1,)), (2, (3,))))
    wide, tokens, padded = ht_all.shape[2], hs.shape[0], lt.shape[1]
    z, x = of_teacher.z, of_teacher.x

    def block_of(i):
        q = i // 2
        return lax.rem(2 * (y + q + q // 2 * (5 - 2 * q)) + lax.rem(i, 2), 8)

    def mine(k):
        chunk = 2 * block_of(k // 2) + lax.rem(k, 2)
        spot = ht_all.at[k, ds(me["zh"] * ht.shape[0], ht.shape[0])]
        return pltpu.make_async_copy(ht.at[:, ds(chunk * wide, wide)], spot, own_sem.at[k])

    peers = [teacher.nxt, teacher.prv, teacher.partner] + of_teacher.xs_of + of_teacher.zs_of
    greet(peers)
    own = []
    for ring in (student, teacher):
        half = ring.shard.shape[1] // 2
        for side in (0, 1):
            src = ring.shard.at[:, side * half : (side + 1) * half]
            own.append(pltpu.make_async_copy(src, ring.block(y, c, side), own_sem.at[CHUNKS + len(own)]))
    states = pltpu.make_async_copy(hs, hs_all.at[pl.ds(0, tokens)], own_sem.at[CHUNKS + 4])

    @pl.loop(0, CHUNKS)
    def _(k):
        mine(k).start()

    for copy in own:
        copy.start()
    states.start()
    lt[...] = jnp.zeros(lt.shape, jnp.float32)
    ls[...] = jnp.zeros(ls.shape, jnp.float32)
    tau[...] = jnp.ones(tau.shape, jnp.float32)
    names[...] = jnp.full(names.shape, -1, jnp.int32)
    tau[:, pl.ds(0, tokens)] = functools.reduce(
        jnp.add, [jnp.where(kinds[...].reshape(1, tokens) == k, heats[k], 0.0) for k in range(heats.shape[0])]
    )
    names[:, pl.ds(0, tokens)] = labels[...].reshape(1, tokens)
    ht_all[:, pl.ds(tokens, padded - tokens)] = jnp.zeros((CHUNKS, padded - tokens, wide), jnp.bfloat16)
    hs_all[pl.ds(tokens, padded - tokens)] = jnp.zeros((padded - tokens, hs.shape[1]), jnp.bfloat16)
    greeted(peers)
    for copy in own:
        copy.wait()
    for k in range(4):
        student.send(k).start()
    for k in range(2):
        teacher.send(k).start()

    @pl.loop(0, CHUNKS)
    def _(k):
        mine(k).wait()
        chain.out1(k).start()

    student.give(6).start()
    teacher.give(6).start()
    states.wait()

    def arrivals(ring, moves):
        for k in moves:
            ring.wait(k)
            if k < 2:
                ring.send(k + 4).start()
            ring.give(k).start()

    def rows_of(total):
        return [(a, min(256, total - a)) for a in range(0, total, 256)]

    def add_block(i, out, weights, states):
        for a, n in rows_of(out.shape[0]):
            part = lax.dot_general(
                jnp.concatenate([w[a : a + n] for w in weights], axis=1), states, BOTH_MINOR, preferred_element_type=jnp.float32
            )

            out[a : a + n] += part

    def student_block(i):
        r = [block_of(2 * i), block_of(2 * i + 1)]
        add_block(
            i, ls, [ws_all.at[t, side] for t in r for side in (0, 1)],
            jnp.concatenate([hs_all[:, ds(t * ws.shape[1], ws.shape[1])] for t in r], axis=1),
        )

    def teacher_block(i):
        r = block_of(i)
        add_block(
            i, lt, [wt_all.at[r, side] for side in (0, 1)], jnp.concatenate([ht_all[2 * i], ht_all[2 * i + 1]], axis=1)
        )

    def student_stats():
        @pl.loop(0, padded // 128)
        def _(n):
            tile = ds(n * 128, 128)
            share = 1.0 / tau[:, tile]
            v = ls[:, tile]
            top = jnp.max(v, axis=0, keepdims=True)
            v = v - top
            near_s[x, 0:1, tile] = top * share
            near_s[x, 1:2, tile] = jnp.sum(jnp.exp(v * share), axis=0, keepdims=True)
            near_s[x, 2:3, tile] = top
            near_s[x, 3:4, tile] = jnp.sum(jnp.exp(v), axis=0, keepdims=True)

        of_student.start()

    @pl.loop(0, 2)
    def _(j):
        chain.pair(j)

    arrivals(student, (0, 1))
    chain.pair(jnp.int32(2))
    arrivals(student, (2, 3))
    for k in range(2, 4):
        teacher.send(k).start()

    @pl.loop(3, CHUNKS // 2)
    def _(j):
        chain.pair(j)

        @pl.when(j == 4)
        def _():
            for k in (6, 0, 1, 2, 3):
                student.taken(k)

        @pl.when((j >= 4) & (j < 7))
        def _():
            student_block(j - 4)

        @pl.when(j == 6)
        def _():
            arrivals(teacher, (0, 1))

        @pl.when(j == 7)
        def _():
            arrivals(student, (4, 5))

    chain.back(CHUNKS // 2 - 1)
    for k in (4, 5):
        student.taken(k)

    @pl.loop(0, CHUNKS // 2)
    def _(j):
        chain.second(j)

        @pl.when(j == 0)
        def _():
            student_block(jnp.int32(3))

        @pl.when(j == 1)
        def _():
            student_stats()

        @pl.when(j == 3)
        def _():
            teacher.taken(6)

        @pl.when(j == 4)
        def _():
            of_student.middle()

        @pl.when(j == 5)
        def _():
            arrivals(teacher, (2, 3))
            for k in range(4):
                teacher.taken(k)

        @pl.when(j >= 3)
        def _():
            chain.got_mate2(j - 3)
            teacher_block(j - 3)

    arrivals(teacher, (4, 5))
    of_student.last(whole_s)

    @pl.loop(5, 8)
    def _(i):
        chain.got_mate2(i)

        @pl.when(i == 6)
        def _():
            for k in (4, 5):
                teacher.taken(k)

        teacher_block(i)

    @pl.loop(0, padded // 128)
    def _(n):
        tile = ds(n * 128, 128)
        share = 1.0 / tau[:, tile]
        v = lt[:, tile] * share
        top = jnp.max(v, axis=0, keepdims=True)
        e = jnp.exp(v - top)
        near_t[x, 0:1, tile] = top
        near_t[x, 1:2, tile] = jnp.sum(e, axis=0, keepdims=True)
        near_t[x, 2:3, tile] = jnp.sum(e * (v - ls[:, tile] * share), axis=0, keepdims=True)

    of_teacher.start()
    vocab = wt.shape[0]
    first_entry = (z * 4 + x) * vocab

    def student_share(first, last):
        @pl.loop(first, last)
        def _(n):
            tile = ds(n * 128, 128)
            heat = tau[:, tile]
            s = ls[:, tile]
            peak_s, sum_s, peak_c, sum_c = (whole_s[k : k + 1, tile] for k in range(4))
            prob_s = jnp.exp(s * (1.0 / heat) - (peak_s + jnp.log(sum_s)))
            prob_c = jnp.exp(s - (peak_c + jnp.log(sum_c)))
            entries = first_entry + lax.broadcasted_iota(jnp.int32, s.shape, 0)
            hot = jnp.where(entries == names[:, tile], 1.0, 0.0)
            ls[:, tile] = heat * prob_s + prob_c - hot

    student_share(0, padded // 256)
    of_teacher.middle()
    student_share(padded // 256, padded // 128)
    of_teacher.last(whole_t)

    @pl.loop(0, padded // 128)
    def _(n):
        tile = ds(n * 128, 128)
        heat = tau[:, tile]
        peak_t, sum_t, cross = (whole_t[k : k + 1, tile] for k in range(3))
        peak_s, sum_s = (whole_s[k : k + 1, tile] for k in range(2))
        log_t = jnp.log(sum_t)
        div_out[:, tile] = cross / sum_t - peak_t - log_t + peak_s + jnp.log(sum_s)
        prob_t = jnp.exp(lt[:, tile] * (1.0 / heat) - (peak_t + log_t))
        grad[:, tile] = (ls[:, tile] - heat * prob_t).astype(jnp.bfloat16)

    partner, x_nxt, x_prv, z_nxt, z_prv = student.partner, at_x(x + 1), at_x(x - 1), at_z(z + 1), at_z(z - 1)
    feats = ws.shape[1]
    half = feats // 2

    groups_u, groups_v = hg_u.shape[2], hg_v.shape[2]
    cut = groups_v // 2
    sides = (pl.ds(0, cut), pl.ds(cut, groups_v - cut))
    ux = Scatter4(
        x, x_nxt, x_prv, lambda t, side: hg_u.at[pl.ds(side * 4, 4), lax.rem(t + 8, 4)], (None, None),
        ux_1, ux_2, ux_3, ux_4, (ux_s, ux_r), (uxs_s, uxs_r),
    )
    va = Scatter8(
        z, z_nxt, z_prv, lambda t: hg_v.at[lax.rem(t + 16, 8), :, sides[0]], va_1, va_2, va_3, va_4, (va_s, va_r), (vas_s, vas_r)
    )
    vb = Scatter8(
        z, z_nxt, z_prv, lambda t: hg_v.at[lax.rem(t + 16, 8), :, sides[1]], vb_1, vb_2, vb_3, vb_4, (vb_s, vb_r), (vbs_s, vbs_r)
    )
    uz = Scatter8(z, z_nxt, z_prv, lambda t: uz_own.at[lax.rem(t + 16, 8)], uz_1, uz_2, uz_3, uz_4, (uz_s, uz_r), (uzs_s, uzs_r))
    vx = Scatter4(
        x, x_nxt, x_prv, lambda t, side: vx_own.at[lax.rem(t + 8, 4), sides[side]], (pl.ds(0, cut), pl.ds(0, groups_v - cut)),
        vx_1, vx_2, vx_3, vx_4, (vx_s, vx_r), (vxs_s, vxs_r),
    )
    wy = Scatter4(
        y, student.nxt, student.prv,
        lambda t, side: pair_buf.at[lax.rem(t + 8, 4), :, side * half : (side + 1) * half], (None, None), y_1, y_2, y_3, y_4, (y_s, y_r), (ys_s, ys_r),
    )

    def hidden_block(i):
        away = jnp.where(lax.rem(i, 2) == 1, 4 - (i + 1) // 2, i // 2 - 4)
        t = lax.rem(z + 16 + away, 8)
        value = lax.dot_general(
            jnp.concatenate([ws_all[t, 0], ws_all[t, 1]], axis=1),
            grad[...],
            (((0,), (0,)), ((), ())),
            preferred_element_type=jnp.float32,
        )
        value = value.reshape(4, groups_u + groups_v, 8, padded)
        hg_u[t] = value[:, :groups_u]
        hg_v[t] = value[:, groups_u:]

    def weight_block(r):
        return lax.dot_general(
            grad[...], hs_all[:, ds(r * feats, feats)], (((1,), (0,)), ((), ())), preferred_element_type=jnp.float32
        )

    def given(n):
        k = lax.rem(y + 2 + 3 * n, 4)
        return k, to(wg_give.at[n], pair_buf.at[k], (pair_s, pair_r), n, partner)

    def put_ux(side, value):
        uz_own[pl.ds(side * 4, 4)] = value

    def put_vx(side, value):
        hg_out[pl.ds(8 * (groups_u + side * cut), value.shape[0] * 8)] = value.reshape(-1, padded)

    def put_wy(side, value):
        wg_out[:, side * half : (side + 1) * half] = value

    def give_block(n):
        k, copy = given(n)
        wg_give[n] = weight_block(2 * k + 1 - c)
        copy.start()

    def own_block(n):
        k, copy = given(n)
        value = weight_block(2 * k + c)
        copy.wait_recv()
        pair_buf[k] = pair_buf[k] + value

    hidden_block(jnp.int32(0))
    va.start()
    vb.start()

    @pl.loop(1, 4)
    def _(i):
        hidden_block(i)

    give_block(jnp.int32(0))
    va.step(1)
    vb.step(1)

    @pl.loop(4, 8)
    def _(i):
        hidden_block(i)

    ux.start()
    own_block(jnp.int32(0))
    wy.send(0)
    wy.send(1)

    @pl.loop(1, 4)
    def _(n):
        give_block(n)

    va.step(2)
    vb.step(2)

    @pl.loop(1, 4)
    def _(n):
        own_block(n)
        for at, number in ((1, 2), (3, 3)):

            @pl.when(n == at)
            def _():
                wy.send(number)

    ux.middle()
    wy.middle()
    va.step(3)
    vb.step(3)
    ux.last(put_ux)
    uz.start()
    uz.step(1)
    vx_own[:, sides[0]] = va.last()
    vx_own[:, sides[1]] = vb.last()
    vx.start()
    uz.step(2)
    vx.middle()
    uz.step(3)
    wy.last(put_wy)
    vx.last(put_vx)
    hg_out[pl.ds(0, 8 * groups_u)] = uz.last().reshape(8 * groups_u, padded)

    @pl.loop(0, 4)
    def _(n):
        given(n)[1].wait_send()

    for ring in (ux, va, vb, uz, vx, wy):
        ring.finish()
    for ring in (student, teacher):
        for k in range(6):
            ring.send(k).wait_send()
        for k in range(7):
            ring.give(k).wait_send()
    chain.finish()
    of_teacher.finish()
    of_student.finish()


def fused(kinds, heats, labels, ht, wt, hs, ws):
    dma, b16, f32 = pltpu.SemaphoreType.DMA, jnp.bfloat16, jnp.float32
    vocab, tokens, feats = wt.shape[0], hs.shape[0], ws.shape[1]
    padded = -(-tokens // 256) * 256
    tile = (8, padded)
    groups_u = ROWS_X_FIRST // 8
    groups_v = feats // 32 - groups_u
    space, vmem = pl.BlockSpec(memory_space=pl.ANY), pl.BlockSpec(memory_space=pltpu.VMEM)
    pairs = lambda *shape: [dma(shape), dma(shape)]
    wide = lambda *shape: pltpu.VMEM(shape, f32)
    narrow = lambda *shape: pltpu.VMEM(shape, b16)

    def packets(count, *shape):
        coded, scale = pltpu.VMEM((count, *shape), jnp.int16), wide(count, 1, shape[-1])
        return coded, coded, scale, scale

    return pl.pallas_call(
        fused_kernel,
        out_shape=[
            jax.ShapeDtypeStruct((1, padded), f32),
            jax.ShapeDtypeStruct((vocab, feats), f32),
            jax.ShapeDtypeStruct((feats // 4, padded), f32),
        ],
        in_specs=[vmem, pl.BlockSpec(memory_space=pltpu.SMEM), vmem] + [space] * 4,
        out_specs=[vmem] * 3,
        scratch_shapes=[
            narrow(CHUNKS, padded, ht.shape[1] // CHUNKS),
            narrow(8, 2, vocab, wt.shape[1] // 2),
            narrow(padded, hs.shape[1]),
            narrow(8, 2, vocab, feats // 2),
            wide(vocab, padded), wide(vocab, padded), wide(1, padded), pltpu.VMEM((1, padded), jnp.int32),
            wide(4, padded), wide(4, padded), wide(4, 4, padded), wide(8, 4, padded), wide(4, 4, padded), wide(8, 4, padded),
            narrow(vocab, padded),
            wide(8, 4, groups_u, *tile), wide(8, 4, groups_v, *tile), wide(4, vocab, feats), wide(4, vocab, feats),
            wide(8, groups_u, *tile), wide(4, groups_v, *tile),
            *packets(6, vocab, feats // 2), *packets(6, 4, groups_u, *tile), *packets(6, groups_v - groups_v // 2, *tile),
            *packets(8, groups_u, *tile), *packets(8, 4, groups_v // 2, *tile), *packets(8, 4, groups_v - groups_v // 2, *tile),
            dma((CHUNKS + 5,)),
        ]
        + pairs(CHUNKS) * 2
        + pairs(CHUNKS // 2) * 2
        + pairs(6) * 2
        + pairs(7) * 2
        + (pairs(3) + pairs(7)) * 2
        + pairs(4)
        + pairs(6) * 6
        + pairs(8) * 6,
        compiler_params=pltpu.CompilerParams(collective_id=0, has_side_effects=True, vmem_limit_bytes=67043328),
        name="fused",
    )(kinds, heats, labels, ht, wt, hs, ws)


def finish_kernel(div, wg, hg, div_out, wg_out, hg_out):
    tokens = div_out.shape[0]
    div_out[...] = div[:, :tokens].reshape(tokens)
    wg_out[...] = wg[...]
    hg_out[...] = hg[:, :tokens]


def finish(tokens, div, wg, hg):
    vmem, f32 = pl.BlockSpec(memory_space=pltpu.VMEM), jnp.float32
    return pl.pallas_call(
        finish_kernel,
        out_shape=[
            jax.ShapeDtypeStruct((tokens,), f32),
            jax.ShapeDtypeStruct(wg.shape, f32),
            jax.ShapeDtypeStruct((hg.shape[0], tokens), f32),
        ],
        in_specs=[vmem] * 3,
        out_specs=[vmem] * 3,
        name="finish",
    )(div, wg, hg)


def local(ht, wt, hs, ws, labels, kinds, heats):
    divergence, wg, hg = finish(hs.shape[0], *fused(kinds, heats, labels, ht, wt.T, hs, ws.T))
    return divergence, hg.T, wg.T


def solution(mesh):
    finer = Mesh(mesh.devices.reshape(mesh.shape["grp"], 2, 4, 4, 2), AXES)
    return jax.shard_map(
        local,
        mesh=finer,
        in_specs=(
            P((*ROWS, "zh"), None),
            P(ROWS, GRP_VOCAB),
            P(ROWS, None),
            P(ROWS, GRP_VOCAB),
            P(ROWS),
            P(ROWS),
            P(),
        ),
        out_specs=(P(ROWS), P(ROWS, GRP_VOCAB), P(ROWS, GRP_VOCAB)),
        check_vma=False,
    )
```
